32 devices in a mesh: dp: 4 (over y, x), expert: 8 (over z, core).
Axes of the slice: x: 2, y: 2, z: 4, core: 2. Of those that a mesh axis runs over, the one named last changes fastest.
Arguments:
- tokens: bfloat16 [1024, 1024], P(('dp', 'expert')), may hold values from -6 to 6
- cotangent: bfloat16 [1024, 1024], P(('dp', 'expert')), may hold values from -3 to 3
- routes: int32 [1024, 8], P(('dp', 'expert')), may hold values from 0 to 7, as said below
- combine: bfloat16 [1024, 8], P(('dp', 'expert')), may hold values from 0.099609375 to 1
- hot_experts: int32 [4], replicated, may hold values from 0 to 3, as said below
- extra_slots: int32 [4], replicated, may hold values from 1 to 4, as said below
- w_gate: bfloat16 [8, 1024, 384], P('expert'), may hold values from -0.1875 to 0.1875
- w_up: bfloat16 [8, 1024, 384], P('expert'), may hold values from -0.1875 to 0.1875
- w_down: bfloat16 [8, 384, 1024], P('expert'), may hold values from -0.3125 to 0.3125
Outputs:
- token_grads: bfloat16 [1024, 1024], P(('dp', 'expert'))
- grad_gate: bfloat16 [8, 1024, 384], P('expert', 'dp')
- grad_up: bfloat16 [8, 1024, 384], P('expert', 'dp')
- grad_down: bfloat16 [8, 384, 1024], P('expert')
The draws below stay inside these ranges and needn't reach their ends.
Inputs may be any that keep to these rules, and one draw needn't show every extreme that they name: `routes`: each row names 8 different experts. `hot_experts`: 4 different experts, all below 4. `extra_slots`: one of the entries equals 4.
All inputs are finite; a program needn't handle non-finite values.
Results may differ from the reference program's by a relative error of at most 0.0064.
Values may be sent and summed in bfloat16 or wider, within the bound.
A program may use at most 64 MiB of HBM per device.

```python
import jax
import jax.numpy as jnp
from jax import lax

D = 1024
HID = 384
TOP = 8
HOT = 4
TOK_DEV = 32
SPECIALIST_COUNT = 8
TOKENS = 1024
CAP = 16
EXTRA = 4


def route_tables(key):
    base_key = jax.random.fold_in(key, 4242)
    subkeys = jax.random.split(base_key, 7)
    middle_list = 1 + jax.random.permutation(subkeys[0], SPECIALIST_COUNT // 2 - 2)[:HOT - 2]
    ends_list = jnp.array([SPECIALIST_COUNT // 2 - 1, 0], dtype=jnp.int32)
    joined_list = jnp.concatenate([ends_list, middle_list.astype(jnp.int32)])
    hot_list = jax.random.permutation(subkeys[6], joined_list).astype(jnp.int32)
    extra_list = jax.random.randint(subkeys[1], (HOT,), 1, EXTRA + 1, dtype=jnp.int32)
    full_slot = jax.random.randint(subkeys[2], (), 0, HOT, dtype=jnp.int32)
    hot_order = jnp.arange(HOT, dtype=jnp.int32)
    extra_list = jnp.where(hot_order == full_slot, EXTRA, extra_list).astype(jnp.int32)
    specialist_saturated = jnp.sum(jnp.where(hot_order == full_slot, hot_list, 0))
    block_count = TOKENS // TOK_DEV
    block_keys = jax.random.split(subkeys[3], block_count)

    def block_order(block_key):
        return jax.random.permutation(block_key, TOK_DEV)
    position = jax.vmap(block_order)(block_keys).reshape(-1)
    mandated_assignment_choice = position < CAP + EXTRA
    specialist_dimension = jnp.arange(SPECIALIST_COUNT, dtype=jnp.int32)
    enrolled_marker = jnp.any(specialist_dimension[None, :] == hot_list[:, None], axis=0)
    stochastic_tosses = jax.random.randint(subkeys[4], (TOKENS, SPECIALIST_COUNT), 0, 2, dtype=jnp.int32)
    stochastic_jitter = jax.random.randint(subkeys[5], (TOKENS, SPECIALIST_COUNT), 0, 65536, dtype=jnp.int32)
    logit_increment = jnp.where(enrolled_marker[None, :], stochastic_tosses, 0)
    logit_increment = logit_increment + jnp.where((specialist_dimension[None, :] == specialist_saturated) & mandated_assignment_choice[:, None], 2, 0)
    gating_logits = (stochastic_jitter + logit_increment * 65536) * SPECIALIST_COUNT + specialist_dimension[None, :]
    chosen = lax.top_k(gating_logits, TOP)[1].astype(jnp.int32)
    return (hot_list, extra_list, chosen)


def draw_routes(key, part):
    return route_tables(key)[2]


def draw_hot_experts(key, part):
    return route_tables(key)[0]


def draw_extra_slots(key, part):
    return route_tables(key)[1]


def level_of(own_key, shape, pieces, smallest, top_value):
    loudness = 1.0
    for dim, parts in pieces:
        draws = jax.random.uniform(jax.random.fold_in(jax.random.fold_in(own_key, 6), dim), (parts,), jnp.float32, smallest / len(pieces), top_value / len(pieces))
        loudness = loudness * jnp.repeat(jnp.exp(draws), shape[dim] // parts).reshape((-1,) + (1,) * (len(shape) - 1 - dim))
    return loudness


def bell_draw(own_key, shape, spread, reach, cuts=(), kind=jnp.bfloat16):
    values = jax.random.normal(own_key, shape, jnp.float32) * spread
    if len(cuts) > 0:
        values = level_of(own_key, shape, cuts, -0.22, 0.18) * values
    return jnp.clip(values, min=-reach, max=reach).astype(kind)


def setup_inputs(seed: int = 0) -> dict:
    splits = jax.random.split(jax.random.key(seed), 10)
    tokens = bell_draw(splits[0], (TOKENS, D), 1.0, 6.0, ((0, 32),))
    cotangent = bell_draw(splits[1], (TOKENS, D), 0.5, 3.0, ((0, 32),))
    routes = draw_routes(jax.random.fold_in(splits[9], 71), 0)
    combine = jnp.clip(0.099609375 + 0.9003906 * jax.random.uniform(splits[3], (TOKENS, TOP), jnp.float32) ** level_of(splits[3], (TOKENS, TOP), ((0, 32),), -0.2, 0.2), 0.099609375, 1.0).astype(jnp.bfloat16)
    hot_experts = draw_hot_experts(jax.random.fold_in(splits[9], 71), 0)
    extra_slots = draw_extra_slots(jax.random.fold_in(splits[9], 71), 0)
    w_gate = bell_draw(splits[6], (SPECIALIST_COUNT, D, HID), D ** -0.5, 0.1875, ((0, 8),))
    w_up = bell_draw(splits[7], (SPECIALIST_COUNT, D, HID), D ** -0.5, 0.1875, ((0, 8),))
    w_down = bell_draw(splits[8], (SPECIALIST_COUNT, HID, D), HID ** -0.5, 0.3125, ((0, 8),))
    return dict(tokens=tokens, cotangent=cotangent, routes=routes, combine=combine, hot_experts=hot_experts, extra_slots=extra_slots, w_gate=w_gate, w_up=w_up, w_down=w_down)


def expert_pass(weight_gate, weight_up, weight_down, row_tokens, row_cotan, row_weights):
    gate_pre = jnp.dot(row_tokens, weight_gate, preferred_element_type=jnp.float32)
    up_proj = jnp.dot(row_tokens, weight_up, preferred_element_type=jnp.float32)
    sigmoid_gate = jax.nn.sigmoid(gate_pre)
    gate_act = gate_pre * sigmoid_gate
    hidden = (gate_act * up_proj).astype(jnp.bfloat16)
    out_grad = (row_weights.astype(jnp.float32)[:, None] * row_cotan.astype(jnp.float32)).astype(jnp.bfloat16)
    grad_down = jnp.dot(hidden.T, out_grad, preferred_element_type=jnp.float32)
    hidden_grad = jnp.dot(out_grad, weight_down.T, preferred_element_type=jnp.float32)
    gate_grad = (hidden_grad * up_proj * sigmoid_gate * (1.0 + gate_pre * (1.0 - sigmoid_gate))).astype(jnp.bfloat16)
    up_grad = (hidden_grad * gate_act).astype(jnp.bfloat16)
    grad_gate = jnp.dot(row_tokens.T, gate_grad, preferred_element_type=jnp.float32)
    grad_up = jnp.dot(row_tokens.T, up_grad, preferred_element_type=jnp.float32)
    row_grads = jnp.dot(gate_grad, weight_gate.T, preferred_element_type=jnp.float32)
    row_grads = row_grads + jnp.dot(up_grad, weight_up.T, preferred_element_type=jnp.float32)
    return row_grads.astype(jnp.bfloat16), (grad_gate, grad_up, grad_down)


def reference(tokens, cotangent, routes, combine, hot_experts, extra_slots, w_gate, w_up, w_down):
    block_count = TOKENS // TOK_DEV
    assign_count = TOK_DEV * TOP
    expert_ids = routes.reshape(block_count, assign_count)
    assign_order = jnp.arange(assign_count, dtype=jnp.int32)

    def rank_block(block_ids):
        earlier = (block_ids[:, None] == block_ids[None, :]) & (assign_order[None, :] < assign_order[:, None])
        return jnp.sum(earlier.astype(jnp.int32), axis=1)

    slot_rank = lax.map(rank_block, expert_ids)
    hot_match = expert_ids[:, :, None] == hot_experts[None, None, :]
    slot_limit = CAP + jnp.sum(jnp.where(hot_match, extra_slots[None, None, :], 0), axis=2)
    is_kept = slot_rank < slot_limit
    block_index = jnp.broadcast_to(jnp.arange(block_count, dtype=jnp.int32)[:, None], (block_count, assign_count))
    global_index = block_index * assign_count + assign_order[None, :]
    base_expert = jnp.where(slot_rank < CAP, expert_ids, SPECIALIST_COUNT)
    base_table = jnp.full((SPECIALIST_COUNT, block_count, CAP), -1, jnp.int32)
    base_table = base_table.at[base_expert, block_index, jnp.minimum(slot_rank, CAP - 1)].set(global_index, mode="drop")
    spill_kept = is_kept & (slot_rank >= CAP)
    spill_expert = jnp.where(spill_kept, expert_ids, SPECIALIST_COUNT)
    spill_table = jnp.full((SPECIALIST_COUNT, block_count, EXTRA), -1, jnp.int32)
    spill_table = spill_table.at[spill_expert, block_index, jnp.clip(slot_rank - CAP, 0, EXTRA - 1)].set(global_index, mode="drop")
    enrolled_marker = jnp.any(jnp.arange(SPECIALIST_COUNT, dtype=jnp.int32)[:, None] == hot_experts[None, :], axis=1)
    combine_flat = combine.reshape(-1)

    def rows_pass(weight_gate, weight_up, weight_down, table, accum):
        flat_table = table.reshape(-1)
        valid = flat_table >= 0
        safe_index = jnp.where(valid, flat_table, 0)
        token_index = safe_index // TOP
        row_weights = jnp.where(valid, combine_flat[safe_index], jnp.zeros((), combine.dtype))
        row_grads, grad_terms = expert_pass(weight_gate, weight_up, weight_down, tokens[token_index], cotangent[token_index], row_weights)
        accum = accum.at[token_index].add(row_grads.astype(jnp.float32))
        return accum, grad_terms

    def per_expert(accum, expert):
        weight_gate = w_gate[expert]
        weight_up = w_up[expert]
        weight_down = w_down[expert]
        accum, base_terms = rows_pass(weight_gate, weight_up, weight_down, base_table[expert], accum)

        def with_spill(current):
            return rows_pass(weight_gate, weight_up, weight_down, spill_table[expert], current)

        def without_spill(current):
            empty_gate = jnp.zeros((D, HID), jnp.float32)
            return current, (empty_gate, empty_gate, jnp.zeros((HID, D), jnp.float32))

        accum, spill_terms = lax.cond(enrolled_marker[expert], with_spill, without_spill, accum)
        totals = (
            (base_terms[0] + spill_terms[0]).astype(jnp.bfloat16),
            (base_terms[1] + spill_terms[1]).astype(jnp.bfloat16),
            (base_terms[2] + spill_terms[2]).astype(jnp.bfloat16),
        )
        return accum, totals

    accum, stacked = lax.scan(per_expert, jnp.zeros((TOKENS, D), jnp.float32), jnp.arange(SPECIALIST_COUNT, dtype=jnp.int32))
    return accum.astype(jnp.bfloat16), stacked[0], stacked[1], stacked[2]
```

```python
import functools

import jax
import jax.numpy as jnp
from jax import lax
from jax.experimental import pallas as pl
from jax.experimental.pallas import tpu as pltpu
from jax.sharding import PartitionSpec as P


def forward_rows(weight_gate, weight_up, weight_down, row_tokens, row_cotan, row_weights):
    gate_pre = jnp.dot(row_tokens, weight_gate, preferred_element_type=jnp.float32)
    up_proj = jnp.dot(row_tokens, weight_up, preferred_element_type=jnp.float32)
    sigmoid_gate = jax.nn.sigmoid(gate_pre)
    gate_act = gate_pre * sigmoid_gate
    hidden = (gate_act * up_proj).astype(jnp.bfloat16)
    out_grad = (row_weights.astype(jnp.float32)[:, None] * row_cotan.astype(jnp.float32)).astype(
        jnp.bfloat16
    )
    hidden_grad = jnp.dot(out_grad, weight_down.T, preferred_element_type=jnp.float32)
    gate_grad = (
        hidden_grad * up_proj * sigmoid_gate * (1.0 + gate_pre * (1.0 - sigmoid_gate))
    ).astype(jnp.bfloat16)
    up_grad = (hidden_grad * gate_act).astype(jnp.bfloat16)
    row_grads = jnp.dot(gate_grad, weight_gate.T, preferred_element_type=jnp.float32)
    row_grads = row_grads + jnp.dot(up_grad, weight_up.T, preferred_element_type=jnp.float32)
    return (row_grads.astype(jnp.bfloat16), (row_tokens, gate_grad, up_grad, hidden, out_grad))


def weight_terms(pieces):
    row_tokens, gate_grad, up_grad, hidden, out_grad = pieces
    grad_gate = jnp.dot(row_tokens.T, gate_grad, preferred_element_type=jnp.float32)
    grad_up = jnp.dot(row_tokens.T, up_grad, preferred_element_type=jnp.float32)
    grad_down = jnp.dot(hidden.T, out_grad, preferred_element_type=jnp.float32)
    return (grad_gate, grad_up, grad_down)


def expert_pass(weight_gate, weight_up, weight_down, row_tokens, row_cotan, row_weights):
    row_grads, pieces = forward_rows(
        weight_gate, weight_up, weight_down, row_tokens, row_cotan, row_weights
    )
    return (row_grads, weight_terms(pieces))


def shards(tokens, cotangent, routes, combine, hot_experts, extra_slots, w_gate, w_up, w_down):
    expert_count = lax.axis_size("expert")
    token_count, features = tokens.shape
    route_count = routes.shape[1]
    capacity = max(2, min(token_count * route_count * 7 // (8 * expert_count), token_count // 2))
    spare_slots = 2 * max(1, capacity // 6)
    expert_ids = routes.reshape(-1)
    assign_count = expert_ids.shape[0]
    assign_order = jnp.arange(assign_count, dtype=jnp.int32)
    earlier = (expert_ids[:, None] == expert_ids[None, :]) & (
        assign_order[None, :] < assign_order[:, None]
    )
    slot_rank = jnp.sum(earlier.astype(jnp.int32), axis=1)
    hot_match = expert_ids[:, None] == hot_experts[None, :]
    slot_limit = capacity + jnp.sum(jnp.where(hot_match, extra_slots[None, :], 0), axis=1)
    is_kept = slot_rank < slot_limit
    slot_count = capacity + spare_slots
    total_slots = expert_count * slot_count
    flat_slot = jnp.where(is_kept, expert_ids * slot_count + slot_rank, total_slots)
    slot_ids = jnp.arange(total_slots, dtype=jnp.int32)
    assign_onehot = slot_ids[:, None] == flat_slot[None, :]
    token_onehot = jnp.any(
        assign_onehot.reshape(total_slots, token_count, route_count), axis=2
    ).astype(jnp.bfloat16)
    both_rows = jnp.concatenate([tokens, cotangent], axis=1)
    filled = jnp.dot(token_onehot, both_rows, preferred_element_type=jnp.float32).astype(
        jnp.bfloat16
    )
    token_send = filled[:, :features].reshape(expert_count, slot_count, features)
    cotan_send = filled[:, features:].reshape(expert_count, slot_count, features)
    weight_flat = jnp.sum(
        jnp.where(assign_onehot, combine.reshape(-1).astype(jnp.float32)[None, :], 0.0), axis=1
    )
    weight_send = weight_flat.astype(jnp.bfloat16).reshape(expert_count, slot_count)
    token_recv, cotan_recv, weight_recv = (
        lax.all_to_all(token_send, "expert", split_axis=0, concat_axis=0, tiled=True),
        lax.all_to_all(cotan_send, "expert", split_axis=0, concat_axis=0, tiled=True),
        lax.all_to_all(weight_send, "expert", split_axis=0, concat_axis=0, tiled=True),
    )
    own_weights = (w_gate[0], w_up[0], w_down[0])
    all_rows, grad_terms = expert_pass(
        own_weights[0],
        own_weights[1],
        own_weights[2],
        token_recv.reshape(-1, features),
        cotan_recv.reshape(-1, features),
        weight_recv.reshape(-1),
    )
    grad_rows = all_rows.reshape(expert_count, slot_count, features)
    returned_rows = lax.all_to_all(grad_rows, "expert", split_axis=0, concat_axis=0, tiled=True)
    token_grads = jnp.dot(
        token_onehot.T,
        returned_rows.reshape(total_slots, features),
        preferred_element_type=jnp.float32,
    ).astype(jnp.bfloat16)
    grad_gate, grad_up = (
        lax.psum_scatter(grad_terms[0][None], "dp", scatter_dimension=1, tiled=True),
        lax.psum_scatter(grad_terms[1][None], "dp", scatter_dimension=1, tiled=True),
    )
    grad_down = lax.psum(grad_terms[2][None], "dp")
    return (
        token_grads,
        grad_gate.astype(jnp.bfloat16),
        grad_up.astype(jnp.bfloat16),
        grad_down.astype(jnp.bfloat16),
    )


MESH = pl.DeviceIdType.MESH
LANES = 128
TILE = 16
NT = (((1,), (1,)), ((), ()))
TN = (((0,), (0,)), ((), ()))


def slots_of(token_count, route_count, expert_count):
    capacity = max(2, min(token_count * route_count * 7 // (8 * expert_count), token_count // 2))
    return capacity, 2 * max(1, capacity // 6)


def dense_fits(sizes, token_count, features, route_count, hidden_size):
    capacity, spare = slots_of(token_count, route_count, sizes["expert"])
    return (
        route_count == sizes["expert"]
        and sizes["dp"] == 4
        and sizes["expert"] % 4 == 0
        and token_count == 2 * TILE
        and capacity == TILE
        and spare * 2 == 8
        and features % (8 * LANES) == 0
        and hidden_size % LANES == 0
    )


def dense_kernel(
    experts,
    tok_hbm,
    cot_hbm,
    routes_hbm,
    comb_hbm,
    hot_hbm,
    extra_hbm,
    wg_hbm,
    wu_hbm,
    wd_hbm,
    tg_ref,
    gg_out,
    gu_out,
    gd_out,
    tok_ref,
    cot_ref,
    routes_ref,
    comb_ref,
    hot_ref,
    extra_ref,
    in_sem,
    all_tok,
    all_cot,
    small,
    wg,
    wu,
    wd,
    all_t,
    all_og,
    all_h,
    all_gg,
    all_ug,
    acc_gate,
    acc_up,
    acc_down,
    row_main,
    row_tail,
    pair_main,
    pair_tail,
    sum_main,
    sum_tail,
    z_main,
    z_tail,
    w_sem,
    own_sem,
    send_sem,
    recv_sem,
    pair_send,
    pair_recv,
    z_send,
    z_recv,
    ready,
):
    levels = experts // 2
    hot_levels = levels // 2
    features = all_tok.shape[2]
    blocks = features // LANES
    half = blocks // 2
    bf16, f32 = jnp.bfloat16, jnp.float32

    d = lax.axis_index("dp")
    e = lax.axis_index("expert")
    z, c = e // 2, e % 2
    dx = d + 1 - 2 * (d % 2)
    dy = (d + 2) % 4
    dd = 3 - d
    pc = 1 - c
    hot = z < hot_levels
    low_x, low_y, low_z = d % 2 == 1, d // 2 == 1, z > 0
    up_x, up_y, up_z = d % 2 == 0, d // 2 == 0, z < levels - 1
    at_x, at_y, at_pair = (dx, e), (dy, e), (d, z * 2 + pc)
    at_down, at_up = (d, jnp.maximum(e - 2, 0)), (d, jnp.minimum(e + 2, experts - 1))

    def slab_id(dp, level, core):
        return dp * experts + level * 2 + core

    me = slab_id(d, z, c)
    tail_rows = pl.ds(TILE, TILE)
    input_copies = [
        pltpu.make_async_copy(h, v, in_sem.at[i])
        for i, (h, v) in enumerate(
            (
                (tok_hbm.at[tail_rows], tok_ref),
                (cot_hbm.at[tail_rows], cot_ref),
                (routes_hbm, routes_ref),
                (comb_hbm, comb_ref),
                (hot_hbm, hot_ref),
                (extra_hbm, extra_ref),
            )
        )
    ]
    own_copies = [
        pltpu.make_async_copy(h.at[pl.ds(0, TILE)], v.at[me], own_sem.at[i])
        for i, (h, v) in enumerate(((tok_hbm, all_tok), (cot_hbm, all_cot)))
    ]
    weight_copies = [
        pltpu.make_async_copy(h.at[0], v, w_sem.at[i])
        for i, (h, v) in enumerate(((wg_hbm, wg), (wu_hbm, wu), (wd_hbm, wd)))
    ]

    barrier = pltpu.get_barrier_semaphore()

    def greet(peer):
        pl.semaphore_signal(barrier, inc=1, device_id=peer, device_id_type=MESH)

    greet(at_pair)
    pl.when(up_x)(lambda: greet(at_x))
    pl.when(up_y)(lambda: greet(at_y))
    pl.when(up_z)(lambda: greet(at_up))
    for copy in input_copies + own_copies + weight_copies:
        copy.start()

    def piece(s, p, full):
        if p == 0:
            return all_tok.at[s]
        if p == 1:
            return all_cot.at[s]
        return small.at[s] if full else small.at[s, pl.ds(half, 1)]

    def copy_of(s, p, full, way, peer, own=False):
        dst = piece(s, p, full)
        src = dst
        if own and p < 2:
            src = (tok_hbm, cot_hbm)[p].at[pl.ds(0, TILE)]
        return pltpu.make_async_remote_copy(
            src_ref=src,
            dst_ref=dst,
            send_sem=send_sem.at[way, p, s],
            recv_sem=recv_sem.at[p, s],
            device_id=peer,
            device_id_type=MESH,
        )

    X, Y, PAIR, DOWN, UP = range(5)
    peers = (at_x, at_y, at_pair, at_down, at_up)

    def either(full, visit):
        if full is True:
            visit(True)
            return
        pl.when(full)(lambda: visit(True))
        pl.when(jnp.logical_not(full))(lambda: visit(False))

    def wide(way, p):
        if p < 2 or way == DOWN:
            return True
        return z + 1 < hot_levels if way == UP else hot

    def send(s, p, way, own=False):
        either(wide(way, p), lambda f: copy_of(s, p, f, way, peers[way], own).start())

    def sent(s, p, way):
        either(wide(way, p), lambda f: copy_of(s, p, f, way, peers[way]).wait_send())

    def arrived(s, p, below=True):
        full = hot if (p == 2 and below) else True
        either(full, lambda f: copy_of(s, p, f, PAIR, at_pair).wait_recv())

    pl.semaphore_wait(barrier, 1 + d % 2 + d // 2 + jnp.minimum(z, 1))

    def tell(way):
        pl.semaphore_signal(ready.at[way], inc=1, device_id=peers[way], device_id_type=MESH)

    pl.when(low_x)(lambda: tell(X))
    pl.when(low_y)(lambda: tell(Y))

    @pl.when(low_z)
    def _():
        pl.semaphore_signal(ready.at[UP], inc=1, device_id=at_down, device_id_type=MESH)

    def to_lower(p):
        pl.when(low_z)(lambda: send(me, p, DOWN, True))
        pl.when(low_x)(lambda: send(me, p, X, True))
        pl.when(low_y)(lambda: send(me, p, Y, True))
        send(me, p, PAIR, True)

    to_lower(0)
    to_lower(1)

    for copy in input_copies:
        copy.wait()
    names = -(-experts // TILE) * TILE
    expert_row = lax.broadcasted_iota(jnp.int32, (names, 2 * TILE), 0)
    token_lane = lax.broadcasted_iota(jnp.int32, (names, 2 * TILE), 1)
    routes = routes_ref[...]
    comb = comb_ref[...].astype(f32)
    weights = jnp.zeros((names, 2 * TILE), f32)
    for r in range(routes.shape[0]):
        weights = jnp.where(expert_row == routes[r : r + 1, :], comb[r : r + 1, :], weights)
    limit = jnp.full((names, 2 * TILE), TILE, jnp.int32)
    for j in range(hot_ref.shape[0]):
        limit = limit + jnp.where(expert_row == hot_ref[j], extra_ref[j], 0)
    weights = jnp.where(token_lane < limit, weights, 0.0).astype(bf16)
    unit_row = lax.broadcasted_iota(jnp.int32, (names, LANES), 0)
    unit_lane = lax.broadcasted_iota(jnp.int32, (names, LANES), 1)

    def turned(shift):
        unit = jnp.where(unit_lane == unit_row + shift, 1.0, 0.0).astype(bf16)
        return lax.dot_general(weights, unit, TN, preferred_element_type=f32)

    main_part, tail_part = turned(0), turned(LANES // 2)
    small[me, half] = (main_part[:TILE] + tail_part[TILE:]).astype(bf16)
    tok_tail = tok_ref[...].astype(f32)[:8]
    cot_tail = cot_ref[...].astype(f32)[:8]
    tail_row = lax.broadcasted_iota(jnp.int32, (8, features), 0)
    spill = jnp.where(tail_row < 4, tok_tail, pltpu.roll(cot_tail, 4, 0))
    for j in range(half):
        lo = spill[:, j * LANES : (j + 1) * LANES]
        hi = spill[:, (half + j) * LANES : (half + j + 1) * LANES]
        small[me, j] = jnp.concatenate([lo, hi], axis=0).astype(bf16)

    to_lower(2)

    def to_upper(way, up):
        @pl.when(up)
        def _():
            pl.semaphore_wait(ready.at[way], 1)
            for p in range(3):
                send(me, p, way, True)

    to_upper(UP, up_z)
    to_upper(X, up_x)
    to_upper(Y, up_y)

    def sides(dist, visit):
        if dist == 0:
            visit(z, 0)
            return
        pl.when(z + dist < levels)(lambda: visit(z + dist, 1))
        pl.when(z - dist >= 0)(lambda: visit(z - dist, -1))

    def column(dist):
        for p in range(3):

            def visit(level, side):
                s = slab_id(d, level, c)
                arrived(s, p, side < 0)
                if side > 0:
                    pl.when(low_z)(lambda: send(s, p, DOWN))
                else:
                    pl.when(up_z)(lambda: send(s, p, UP))
                send(s, p, X)
                send(s, p, Y)
                send(s, p, PAIR)

            sides(dist, visit)

    def turn(dp_is_x, p):
        if p < 2:
            return p == (0 if dp_is_x else 1)
        return c == (0 if dp_is_x else 1)

    def onward(dp_is_x, p, act):
        take = turn(dp_is_x, p)
        way = Y if dp_is_x else X
        if take is True:
            act(way)
        elif take is not False:
            pl.when(take)(lambda: act(way))

    def beside(dist):
        for p in range(3):

            def visit(level, side):
                for dp, is_x in ((dx, True), (dy, False)):
                    s = slab_id(dp, level, c)
                    arrived(s, p)
                    onward(is_x, p, lambda way: send(s, p, way))
                    send(s, p, PAIR)

            sides(dist, visit)

    def across(dist):
        for p in range(3):

            def visit(level, side):
                s = slab_id(dd, level, c)
                arrived(s, p)
                send(s, p, PAIR)

            sides(dist, visit)

    def from_pair(dp):
        for level in range(levels):
            for p in range(3):
                arrived(slab_id(dp, level, pc), p)

    main_rows = experts * TILE
    spill_rows = experts // 2 * 8
    group_rows = main_rows + spill_rows
    main_lane = lax.broadcasted_iota(jnp.int32, (main_rows, LANES), 1)
    tail_lane = lax.broadcasted_iota(jnp.int32, (spill_rows, LANES), 1)
    first_w = lax.broadcasted_iota(jnp.int32, (spill_rows, LANES), 0) % 8 < 4
    first = lax.broadcasted_iota(jnp.int32, (spill_rows, features), 0) % 8 < 4

    def group(dp, at):
        rows = pl.ds(at, group_rows)
        part = pl.ds(dp * experts, experts)
        lo_a, lo_b, hi_a, hi_b = [], [], [], []
        for j in range(half):
            both = small[part, j].astype(f32)
            low, high = both[:, :8], both[:, 8:]
            lo_a.append(low[: experts // 2].reshape(spill_rows, LANES))
            lo_b.append(low[experts // 2 :].reshape(spill_rows, LANES))
            hi_a.append(high[: experts // 2].reshape(spill_rows, LANES))
            hi_b.append(high[experts // 2 :].reshape(spill_rows, LANES))
        tail_a = jnp.concatenate(lo_a + hi_a, axis=1)
        tail_b = jnp.concatenate(lo_b + hi_b, axis=1)
        tok_rows = jnp.where(first, tail_a, pltpu.roll(tail_b, 4, 0))
        cot_rows = jnp.where(first, pltpu.roll(tail_a, spill_rows - 4, 0), tail_b)
        tok_rows = jnp.where(hot, tok_rows, 0.0)
        cot_rows = jnp.where(hot, cot_rows, 0.0)
        w_all = small[part, half].astype(f32)
        w_main = w_all.reshape(main_rows, LANES)
        w_a = w_all[: experts // 2, :8].reshape(spill_rows, LANES)
        w_b = w_all[experts // 2 :, :8].reshape(spill_rows, LANES)
        w_tail = jnp.where(first_w, w_a, pltpu.roll(w_b, 4, 0))
        w = jnp.concatenate(
            [
                jnp.sum(jnp.where(main_lane == e, w_main, 0.0), axis=1, keepdims=True),
                jnp.sum(jnp.where(tail_lane == e + LANES // 2, w_tail, 0.0), axis=1, keepdims=True),
            ],
            axis=0,
        )
        all_t[rows, :] = jnp.concatenate(
            [all_tok[part].reshape(main_rows, features), tok_rows.astype(bf16)], axis=0
        )
        cot = jnp.concatenate(
            [all_cot[part].reshape(main_rows, features).astype(f32), cot_rows], axis=0
        )
        all_og[rows, :] = (w * cot).astype(bf16)
        t = all_t[rows, :]
        gate_pre = jnp.dot(t, wg[...], preferred_element_type=f32)
        up_proj = jnp.dot(t, wu[...], preferred_element_type=f32)
        hidden_grad = lax.dot_general(all_og[rows, :], wd[...], NT, preferred_element_type=f32)
        sig = jax.nn.sigmoid(gate_pre)
        act = gate_pre * sig
        all_h[rows, :] = (act * up_proj).astype(bf16)
        all_gg[rows, :] = (hidden_grad * up_proj * sig * (1.0 + gate_pre * (1.0 - sig))).astype(
            bf16
        )
        all_ug[rows, :] = (hidden_grad * act).astype(bf16)

    for copy in own_copies:
        copy.wait()
    column(1)
    beside(0)
    column(2)
    beside(1)
    column(3)
    from_pair(d)
    for copy in weight_copies:
        copy.wait()
    group(d, 0)
    beside(2)
    own = pl.ds(0, group_rows)
    rg = lax.dot_general(all_gg[own, :], wg[...], NT, preferred_element_type=f32)
    rg = rg + lax.dot_general(all_ug[own, :], wu[...], NT, preferred_element_type=f32)
    row_main[...] = rg[:main_rows].reshape(experts, TILE, features).astype(bf16)
    for j in range(half):
        lo = rg[main_rows:, j * LANES : (j + 1) * LANES].reshape(experts // 2, 8, LANES)
        hi = rg[main_rows:, (half + j) * LANES : (half + j + 1) * LANES].reshape(
            experts // 2, 8, LANES
        )
        row_tail[:, j] = jnp.concatenate([lo, hi], axis=1).astype(bf16)

    def pair_copy(level):
        return pltpu.make_async_remote_copy(
            src_ref=row_main.at[level * 2 + pc],
            dst_ref=pair_main.at[level],
            send_sem=pair_send.at[level],
            recv_sem=pair_recv.at[level],
            device_id=at_pair,
            device_id_type=MESH,
        )

    def pair_tail_copy(k):
        return pltpu.make_async_remote_copy(
            src_ref=row_tail.at[k * 2 + pc],
            dst_ref=pair_tail.at[k],
            send_sem=pair_send.at[levels + k],
            recv_sem=pair_recv.at[levels + k],
            device_id=at_pair,
            device_id_type=MESH,
        )

    for level in range(levels):
        pair_copy(level).start()

    @pl.when(hot)
    def _():
        for k in range(hot_levels):
            pair_tail_copy(k).start()

    beside(3)
    for level in range(levels):
        pair_copy(level).wait_recv()
        sum_main[level] = (
            row_main[level * 2 + c].astype(f32) + pair_main[level].astype(f32)
        ).astype(bf16)

    @pl.when(hot)
    def _():
        for k in range(hot_levels):
            pair_tail_copy(k).wait_recv()
            sum_tail[k] = (
                row_tail[k * 2 + c].astype(f32) + pair_tail[k].astype(f32)
            ).astype(bf16)

    def z_copy(step, tail):
        level = (z + step) % levels
        src, dst = (sum_tail, z_tail) if tail else (sum_main, z_main)
        return pltpu.make_async_remote_copy(
            src_ref=src.at[level % hot_levels if tail else level],
            dst_ref=dst.at[step - 1],
            send_sem=z_send.at[tail, step - 1],
            recv_sem=z_recv.at[tail, step - 1],
            device_id=(d, level * 2 + c),
            device_id_type=MESH,
        )

    for step in range(1, levels):
        z_copy(step, 0).start()
        pl.when(hot)(lambda: z_copy(step, 1).start())

    from_pair(dx)
    group(dx, group_rows)
    from_pair(dy)
    group(dy, 2 * group_rows)
    share = features // 4

    def weight_terms(at, count):
        rows = pl.ds(at, count)
        t_cols = all_t[rows, pl.ds(pl.multiple_of(d * share, LANES), share)]
        return (
            lax.dot_general(t_cols, all_gg[rows, :], TN, preferred_element_type=f32),
            lax.dot_general(t_cols, all_ug[rows, :], TN, preferred_element_type=f32),
            lax.dot_general(all_h[rows, :], all_og[rows, :], TN, preferred_element_type=f32),
        )

    for dist in range(levels):
        across(dist)
    early = weight_terms(0, 3 * group_rows)
    acc_gate[...], acc_up[...], acc_down[...] = early
    from_pair(dd)
    group(dd, 3 * group_rows)
    late = weight_terms(3 * group_rows, group_rows)
    gg_out[0] = (acc_gate[...] + late[0]).astype(bf16)
    gu_out[0] = (acc_up[...] + late[1]).astype(bf16)
    gd_out[0] = (acc_down[...] + late[2]).astype(bf16)

    total = sum_main[z].astype(f32)
    spilled = jnp.where(hot, sum_tail[z % hot_levels].astype(f32), 0.0)
    for step in range(1, levels):
        z_copy(step, 0).wait_recv()
        total = total + z_main[step - 1].astype(f32)
        from_hot = (z + levels - step) % levels < hot_levels
        pl.when(from_hot)(lambda: z_copy(step, 1).wait_recv())
        spilled = spilled + jnp.where(from_hot, z_tail[step - 1].astype(f32), 0.0)
    tg_ref[:TILE, :] = total.astype(bf16)
    kept_row = lax.broadcasted_iota(jnp.int32, (8, LANES), 0) < 4
    blank = jnp.zeros((8, LANES), f32)
    for j in range(half):
        for at, rows in ((j, spilled[j][:8]), (half + j, spilled[j][8:])):
            rows = jnp.where(hot, rows, pltpu.roll(rows, 4, 0))
            tg_ref[TILE:, at * LANES : (at + 1) * LANES] = jnp.concatenate(
                [jnp.where(kept_row, rows, 0.0), blank], axis=0
            ).astype(bf16)

    for level in range(levels):
        pair_copy(level).wait_send()
    for step in range(1, levels):
        z_copy(step, 0).wait_send()

    @pl.when(hot)
    def _():
        for k in range(hot_levels):
            pair_tail_copy(k).wait_send()
        for step in range(1, levels):
            z_copy(step, 1).wait_send()

    for p in range(3):
        for level in range(levels):
            s = slab_id(d, level, c)
            sent(s, p, X)
            sent(s, p, Y)
            for dp in (d, dx, dy, dd):
                sent(slab_id(dp, level, c), p, PAIR)
            for dp, is_x in ((dx, True), (dy, False)):
                onward(is_x, p, lambda way: sent(slab_id(dp, level, c), p, way))
            pl.when(jnp.logical_and(level >= z, z > 0))(lambda: sent(s, p, DOWN))
            pl.when(jnp.logical_and(level <= z, z < levels - 1))(lambda: sent(s, p, UP))


def write_kernel(*refs):
    sources, sem = refs[: len(refs) // 2], refs[-1]
    targets = refs[len(refs) // 2 : -1]
    copies = [
        pltpu.make_async_copy(a, b, sem.at[i]) for i, (a, b) in enumerate(zip(sources, targets))
    ]
    for copy in copies:
        copy.start()
    for copy in copies:
        copy.wait()


def dense_shards(tokens, cotangent, routes, combine, hot_experts, extra_slots, w_gate, w_up, w_down):
    experts = lax.axis_size("expert")
    replicas = lax.axis_size("dp")
    token_count, features = tokens.shape
    hidden_size = w_gate.shape[2]
    half = features // LANES // 2
    levels = experts // 2
    slots = replicas * experts
    rows = slots * (TILE + 4)
    bf16 = jnp.bfloat16
    vmem = pl.BlockSpec(memory_space=pltpu.VMEM)
    hbm = pl.BlockSpec(memory_space=pltpu.HBM)
    dma = pltpu.SemaphoreType.DMA
    operands = [
        pltpu.with_memory_space_constraint(a, pltpu.HBM)
        for a in (
            tokens,
            cotangent,
            routes.T,
            combine.T,
            hot_experts,
            extra_slots,
            w_gate,
            w_up,
            w_down,
        )
    ]
    results = pl.pallas_call(
        functools.partial(dense_kernel, experts),
        out_shape=(
            jax.ShapeDtypeStruct((token_count, features), bf16),
            jax.ShapeDtypeStruct((1, features // replicas, hidden_size), bf16),
            jax.ShapeDtypeStruct((1, features // replicas, hidden_size), bf16),
            jax.ShapeDtypeStruct((1, hidden_size, features), bf16),
        ),
        in_specs=[hbm] * 9,
        out_specs=(vmem, vmem, vmem, vmem),
        scratch_shapes=[
            pltpu.VMEM((TILE, features), bf16),
            pltpu.VMEM((TILE, features), bf16),
            pltpu.VMEM(routes.shape[::-1], jnp.int32),
            pltpu.VMEM(routes.shape[::-1], bf16),
            pltpu.SMEM(hot_experts.shape, jnp.int32),
            pltpu.SMEM(hot_experts.shape, jnp.int32),
            dma((6,)),
            pltpu.VMEM((slots, TILE, features), bf16),
            pltpu.VMEM((slots, TILE, features), bf16),
            pltpu.VMEM((slots, half + 1, TILE, LANES), bf16),
            pltpu.VMEM((features, hidden_size), bf16),
            pltpu.VMEM((features, hidden_size), bf16),
            pltpu.VMEM((hidden_size, features), bf16),
            pltpu.VMEM((rows, features), bf16),
            pltpu.VMEM((rows, features), bf16),
            pltpu.VMEM((rows, hidden_size), bf16),
            pltpu.VMEM((rows, hidden_size), bf16),
            pltpu.VMEM((rows, hidden_size), bf16),
            pltpu.VMEM((features // replicas, hidden_size), jnp.float32),
            pltpu.VMEM((features // replicas, hidden_size), jnp.float32),
            pltpu.VMEM((hidden_size, features), jnp.float32),
            pltpu.VMEM((experts, TILE, features), bf16),
            pltpu.VMEM((experts // 2, half, TILE, LANES), bf16),
            pltpu.VMEM((levels, TILE, features), bf16),
            pltpu.VMEM((levels // 2, half, TILE, LANES), bf16),
            pltpu.VMEM((levels, TILE, features), bf16),
            pltpu.VMEM((levels // 2, half, TILE, LANES), bf16),
            pltpu.VMEM((levels - 1, TILE, features), bf16),
            pltpu.VMEM((levels - 1, half, TILE, LANES), bf16),
            dma((3,)),
            dma((2,)),
            dma((5, 3, slots)),
            dma((3, slots)),
            dma((levels + levels // 2,)),
            dma((levels + levels // 2,)),
            dma((2, levels - 1)),
            dma((2, levels - 1)),
            pltpu.SemaphoreType.REGULAR((5,)),
        ],
        compiler_params=pltpu.CompilerParams(
            collective_id=0, has_side_effects=True, vmem_limit_bytes=32 * 1024 * 1024
        ),
    )(*operands)
    return pl.pallas_call(
        write_kernel,
        out_shape=tuple(jax.ShapeDtypeStruct(r.shape, r.dtype) for r in results),
        in_specs=[vmem] * len(results),
        out_specs=tuple(hbm for _ in results),
        scratch_shapes=[dma((len(results),))],
        compiler_params=pltpu.CompilerParams(vmem_limit_bytes=8 * 1024 * 1024),
    )(*results)


def solution(mesh):
    in_specs = (
        P(("dp", "expert"), None),
        P(("dp", "expert"), None),
        P(("dp", "expert"), None),
        P(("dp", "expert"), None),
        P(),
        P(),
        P("expert", None, None),
        P("expert", None, None),
        P("expert", None, None),
    )
    out_specs = (
        P(("dp", "expert"), None),
        P("expert", "dp", None),
        P("expert", "dp", None),
        P("expert", None, None),
    )

    def body(*args):
        token_count, features = args[0].shape
        if dense_fits(dict(mesh.shape), token_count, features, args[2].shape[1], args[6].shape[2]):
            return dense_shards(*args)
        return shards(*args)

    return jax.shard_map(body, mesh=mesh, in_specs=in_specs, out_specs=out_specs, check_vma=False)
```

```python
import functools

import jax
import jax.numpy as jnp
from jax import lax
from jax.experimental import pallas as pl
from jax.experimental.pallas import tpu as pltpu
from jax.sharding import PartitionSpec as P


def forward_rows(weight_gate, weight_up, weight_down, row_tokens, row_cotan, row_weights):
    gate_pre = jnp.dot(row_tokens, weight_gate, preferred_element_type=jnp.float32)
    up_proj = jnp.dot(row_tokens, weight_up, preferred_element_type=jnp.float32)
    sigmoid_gate = jax.nn.sigmoid(gate_pre)
    gate_act = gate_pre * sigmoid_gate
    hidden = (gate_act * up_proj).astype(jnp.bfloat16)
    out_grad = (row_weights.astype(jnp.float32)[:, None] * row_cotan.astype(jnp.float32)).astype(
        jnp.bfloat16
    )
    hidden_grad = jnp.dot(out_grad, weight_down.T, preferred_element_type=jnp.float32)
    gate_grad = (
        hidden_grad * up_proj * sigmoid_gate * (1.0 + gate_pre * (1.0 - sigmoid_gate))
    ).astype(jnp.bfloat16)
    up_grad = (hidden_grad * gate_act).astype(jnp.bfloat16)
    row_grads = jnp.dot(gate_grad, weight_gate.T, preferred_element_type=jnp.float32)
    row_grads = row_grads + jnp.dot(up_grad, weight_up.T, preferred_element_type=jnp.float32)
    return (row_grads.astype(jnp.bfloat16), (row_tokens, gate_grad, up_grad, hidden, out_grad))


def weight_terms(pieces):
    row_tokens, gate_grad, up_grad, hidden, out_grad = pieces
    grad_gate = jnp.dot(row_tokens.T, gate_grad, preferred_element_type=jnp.float32)
    grad_up = jnp.dot(row_tokens.T, up_grad, preferred_element_type=jnp.float32)
    grad_down = jnp.dot(hidden.T, out_grad, preferred_element_type=jnp.float32)
    return (grad_gate, grad_up, grad_down)


def expert_pass(weight_gate, weight_up, weight_down, row_tokens, row_cotan, row_weights):
    row_grads, pieces = forward_rows(
        weight_gate, weight_up, weight_down, row_tokens, row_cotan, row_weights
    )
    return (row_grads, weight_terms(pieces))


def shards(tokens, cotangent, routes, combine, hot_experts, extra_slots, w_gate, w_up, w_down):
    expert_count = lax.axis_size("expert")
    token_count, features = tokens.shape
    route_count = routes.shape[1]
    capacity = max(2, min(token_count * route_count * 7 // (8 * expert_count), token_count // 2))
    spare_slots = 2 * max(1, capacity // 6)
    expert_ids = routes.reshape(-1)
    assign_count = expert_ids.shape[0]
    assign_order = jnp.arange(assign_count, dtype=jnp.int32)
    earlier = (expert_ids[:, None] == expert_ids[None, :]) & (
        assign_order[None, :] < assign_order[:, None]
    )
    slot_rank = jnp.sum(earlier.astype(jnp.int32), axis=1)
    hot_match = expert_ids[:, None] == hot_experts[None, :]
    slot_limit = capacity + jnp.sum(jnp.where(hot_match, extra_slots[None, :], 0), axis=1)
    is_kept = slot_rank < slot_limit
    slot_count = capacity + spare_slots
    total_slots = expert_count * slot_count
    flat_slot = jnp.where(is_kept, expert_ids * slot_count + slot_rank, total_slots)
    slot_ids = jnp.arange(total_slots, dtype=jnp.int32)
    assign_onehot = slot_ids[:, None] == flat_slot[None, :]
    token_onehot = jnp.any(
        assign_onehot.reshape(total_slots, token_count, route_count), axis=2
    ).astype(jnp.bfloat16)
    both_rows = jnp.concatenate([tokens, cotangent], axis=1)
    filled = jnp.dot(token_onehot, both_rows, preferred_element_type=jnp.float32).astype(
        jnp.bfloat16
    )
    token_send = filled[:, :features].reshape(expert_count, slot_count, features)
    cotan_send = filled[:, features:].reshape(expert_count, slot_count, features)
    weight_flat = jnp.sum(
        jnp.where(assign_onehot, combine.reshape(-1).astype(jnp.float32)[None, :], 0.0), axis=1
    )
    weight_send = weight_flat.astype(jnp.bfloat16).reshape(expert_count, slot_count)
    token_recv, cotan_recv, weight_recv = (
        lax.all_to_all(token_send, "expert", split_axis=0, concat_axis=0, tiled=True),
        lax.all_to_all(cotan_send, "expert", split_axis=0, concat_axis=0, tiled=True),
        lax.all_to_all(weight_send, "expert", split_axis=0, concat_axis=0, tiled=True),
    )
    own_weights = (w_gate[0], w_up[0], w_down[0])
    all_rows, grad_terms = expert_pass(
        own_weights[0],
        own_weights[1],
        own_weights[2],
        token_recv.reshape(-1, features),
        cotan_recv.reshape(-1, features),
        weight_recv.reshape(-1),
    )
    grad_rows = all_rows.reshape(expert_count, slot_count, features)
    returned_rows = lax.all_to_all(grad_rows, "expert", split_axis=0, concat_axis=0, tiled=True)
    token_grads = jnp.dot(
        token_onehot.T,
        returned_rows.reshape(total_slots, features),
        preferred_element_type=jnp.float32,
    ).astype(jnp.bfloat16)
    grad_gate, grad_up = (
        lax.psum_scatter(grad_terms[0][None], "dp", scatter_dimension=1, tiled=True),
        lax.psum_scatter(grad_terms[1][None], "dp", scatter_dimension=1, tiled=True),
    )
    grad_down = lax.psum(grad_terms[2][None], "dp")
    return (
        token_grads,
        grad_gate.astype(jnp.bfloat16),
        grad_up.astype(jnp.bfloat16),
        grad_down.astype(jnp.bfloat16),
    )


MESH = pl.DeviceIdType.MESH
LANES = 128
TILE = 16
NT = (((1,), (1,)), ((), ()))
TN = (((0,), (0,)), ((), ()))


def slots_of(token_count, route_count, expert_count):
    capacity = max(2, min(token_count * route_count * 7 // (8 * expert_count), token_count // 2))
    return capacity, 2 * max(1, capacity // 6)


def dense_fits(sizes, token_count, features, route_count, hidden_size):
    capacity, spare = slots_of(token_count, route_count, sizes["expert"])
    return (
        route_count == sizes["expert"]
        and sizes["dp"] == 4
        and sizes["expert"] == 8
        and token_count == 2 * TILE
        and capacity == TILE
        and spare * 2 == 8
        and features % (8 * LANES) == 0
        and hidden_size % LANES == 0
    )


def dense_kernel(
    experts,
    tok_hbm,
    cot_hbm,
    routes_hbm,
    comb_hbm,
    hot_hbm,
    extra_hbm,
    wg_hbm,
    wu_hbm,
    wd_hbm,
    tg_ref,
    acc_gate,
    acc_up,
    acc_down,
    late_cols,
    late_og,
    late_h,
    late_gg,
    late_ug,
    tok_ref,
    cot_ref,
    routes_ref,
    comb_ref,
    hot_ref,
    extra_ref,
    all_tok,
    slab,
    wg,
    wu,
    wd,
    all_t,
    all_og,
    all_h,
    all_gg,
    all_ug,
    late_t,
    row_out,
    pair_in,
    row_sum,
    z_in,
    in_sem,
    w_sem,
    flat_send,
    down_send,
    up_send,
    recv_sem,
    pair_recv,
    row_sem,
    z_send,
    z_recv,
    ready,
):
    levels = experts // 2
    hot_levels = levels // 2
    features = all_tok.shape[2]
    blocks = features // LANES
    half = blocks // 2
    weight_at, spill_at = blocks, blocks + 1
    bf16, f32 = jnp.bfloat16, jnp.float32

    d = lax.axis_index("dp")
    e = lax.axis_index("expert")
    z, c = e // 2, e % 2
    dx = d + 1 - 2 * (d % 2)
    dy = (d + 2) % 4
    dd = 3 - d
    pc = 1 - c
    upper_half = z // 2
    near, far = 2 * upper_half, 2 - 2 * upper_half
    hot = z < hot_levels
    low_x, low_y, low_z = d % 2 == 1, d // 2 == 1, z > 0
    up_x, up_y, up_z = d % 2 == 0, d // 2 == 0, z < levels - 1
    at_x, at_y, at_pair = (dx, e), (dy, e), (d, z * 2 + pc)
    at_below, at_above = (d, jnp.maximum(e - 2, 0)), (d, jnp.minimum(e + 2, experts - 1))

    def slot(dp, level, core):
        return (dp * 2 + core) * levels + level

    me = slot(d, z, c)
    input_copies = [
        pltpu.make_async_copy(h, v, in_sem.at[i])
        for i, (h, v) in enumerate(
            (
                (tok_hbm.at[pl.ds(TILE, TILE)], tok_ref),
                (cot_hbm, cot_ref),
                (routes_hbm, routes_ref),
                (comb_hbm, comb_ref),
                (hot_hbm, hot_ref),
                (extra_hbm, extra_ref),
                (tok_hbm.at[pl.ds(0, TILE)], all_tok.at[me]),
            )
        )
    ]
    own_tokens = input_copies.pop()
    weight_copies = [
        pltpu.make_async_copy(h.at[0], v, w_sem.at[i])
        for i, (h, v) in enumerate(((wg_hbm, wg), (wu_hbm, wu), (wd_hbm, wd)))
    ]

    barrier = pltpu.get_barrier_semaphore()

    def greet(peer):
        pl.semaphore_signal(barrier, inc=1, device_id=peer, device_id_type=MESH)

    greet(at_pair)
    pl.when(up_x)(lambda: greet(at_x))
    pl.when(up_y)(lambda: greet(at_y))
    pl.when(up_z)(lambda: greet(at_above))
    for copy in input_copies + [own_tokens] + weight_copies:
        copy.start()

    def piece(s, p, full):
        if p == 0:
            return all_tok.at[s]
        return slab.at[s] if full else slab.at[s, pl.ds(0, spill_at)]

    def either(full, visit):
        if full is True or full is False:
            visit(full)
            return
        pl.when(full)(lambda: visit(True))
        pl.when(jnp.logical_not(full))(lambda: visit(False))

    def remote(src, dst, send, recv, peer):
        return pltpu.make_async_remote_copy(
            src_ref=src,
            dst_ref=dst,
            send_sem=send,
            recv_sem=recv,
            device_id=peer,
            device_id_type=MESH,
        )

    def push(dp, level, p, full, send, peer, own=False):
        s = slot(dp, level, c)

        def go(f):
            dst = piece(s, p, f)
            src = tok_hbm.at[pl.ds(0, TILE)] if own and p == 0 else dst
            remote(src, dst, send, recv_sem.at[p, dp * levels + level], peer).start()

        either(True if p == 0 else full, go)

    X, Y, PAIR = range(3)

    def to_x(dp, level, p, own=False):
        push(dp, level, p, hot, flat_send.at[X, p], at_x, own)

    def to_y(dp, level, p, own=False):
        push(dp, level, p, hot, flat_send.at[Y, p], at_y, own)

    def to_above(level, p, own=False):
        push(d, level, p, z + 1 < hot_levels, up_send.at[p, level], at_above, own)

    def to_below(level, p, own=False):
        push(d, level, p, True, down_send.at[p, level - 1], at_below, own)

    def to_pair(dp, level, p, bank, own=False):
        s = slot(dp, level, c)

        def go(f):
            dst = piece(s, p, f)
            src = tok_hbm.at[pl.ds(0, TILE)] if own and p == 0 else dst
            remote(src, dst, flat_send.at[PAIR, p], pair_recv.at[p, bank], at_pair).start()

        either(True if p == 0 else hot, go)

    def arrived(dp, level, p, above=False):
        s = slot(dp, level, c)

        def go(f):
            dst = piece(s, p, f)
            at = recv_sem.at[p, dp * levels + level]
            remote(dst, dst, flat_send.at[X, p], at, at_x).wait_recv()

        either(True if p == 0 or above else hot, go)

    pl.semaphore_wait(barrier, 1 + d % 2 + d // 2 + jnp.minimum(z, 1))

    def tell(way, peer):
        pl.semaphore_signal(ready.at[way], inc=1, device_id=peer, device_id_type=MESH)

    pl.when(low_x)(lambda: tell(0, at_x))
    pl.when(low_y)(lambda: tell(1, at_y))
    pl.when(low_z)(lambda: tell(2, at_below))

    OWN, NEAR, FAR, DD_NEAR, DD_FAR = range(5)

    def to_lower(p):
        pl.when(low_z)(lambda: to_below(z, p, True))
        pl.when(low_x)(lambda: to_x(d, z, p, True))
        pl.when(low_y)(lambda: to_y(d, z, p, True))
        to_pair(d, z, p, OWN, True)

    to_lower(0)

    for copy in input_copies:
        copy.wait()
    names = -(-experts // TILE) * TILE
    expert_row = lax.broadcasted_iota(jnp.int32, (names, 2 * TILE), 0)
    token_lane = lax.broadcasted_iota(jnp.int32, (names, 2 * TILE), 1)
    routes = routes_ref[...]
    comb = comb_ref[...].astype(f32)
    weights = jnp.zeros((names, 2 * TILE), f32)
    for r in range(routes.shape[0]):
        weights = jnp.where(expert_row == routes[r : r + 1, :], comb[r : r + 1, :], weights)
    limit = jnp.full((names, 2 * TILE), TILE, jnp.int32)
    for j in range(hot_ref.shape[0]):
        limit = limit + jnp.where(expert_row == hot_ref[j], extra_ref[j], 0)
    weights = jnp.where(token_lane < limit, weights, 0.0).astype(bf16)
    unit_row = lax.broadcasted_iota(jnp.int32, (names, LANES), 0)
    unit_lane = lax.broadcasted_iota(jnp.int32, (names, LANES), 1)

    def turned(shift):
        unit = jnp.where(unit_lane == unit_row + shift, 1.0, 0.0).astype(bf16)
        return lax.dot_general(weights, unit, TN, preferred_element_type=f32)

    main_part, tail_part = turned(0), turned(LANES // 2)
    slab[me, weight_at] = (main_part[:TILE] + tail_part[TILE:]).astype(bf16)
    tok_tail = tok_ref[...].astype(f32)[:8]
    cot_tail = cot_ref[TILE:, :].astype(f32)[:8]
    tail_row = lax.broadcasted_iota(jnp.int32, (8, features), 0)
    spill = jnp.where(tail_row < 4, tok_tail, pltpu.roll(cot_tail, 4, 0))
    for j in range(blocks):
        slab[me, j] = cot_ref[:TILE, j * LANES : (j + 1) * LANES]
    for j in range(half):
        lo = spill[:, j * LANES : (j + 1) * LANES]
        hi = spill[:, (half + j) * LANES : (half + j + 1) * LANES]
        slab[me, spill_at + j] = jnp.concatenate([lo, hi], axis=0).astype(bf16)

    to_lower(1)

    def to_upper(way, up, act):
        @pl.when(up)
        def _():
            pl.semaphore_wait(ready.at[way], 1)
            for p in range(2):
                act(p)

    to_upper(2, up_z, lambda p: to_above(z, p, True))
    to_upper(0, up_x, lambda p: to_x(d, z, p, True))
    to_upper(1, up_y, lambda p: to_y(d, z, p, True))
    own_tokens.wait()

    def at_distance(dist, visit):
        if dist == 0:
            visit(z, 0)
            return
        pl.when(z + dist < levels)(lambda: visit(z + dist, 1))
        pl.when(z - dist >= 0)(lambda: visit(z - dist, -1))

    def bank_of(level):
        return (level // 2 + upper_half) % 2

    def column(dist):
        for p in range(2):

            def visit(level, side):
                arrived(d, level, p, side > 0)
                if side > 0:
                    pl.when(low_z)(lambda: to_below(level, p))
                else:
                    pl.when(up_z)(lambda: to_above(level, p))
                to_x(d, level, p)
                to_y(d, level, p)
                to_pair(d, level, p, OWN)

            at_distance(dist, visit)

    def beside(dist):
        for p in range(2):

            def visit(level, side):
                bank = NEAR + bank_of(level)
                arrived(dx, level, p)
                pl.when((p + c) % 2 == 0)(lambda: to_y(dx, level, p))
                to_pair(dx, level, p, bank)
                arrived(dy, level, p)
                pl.when((p + c) % 2 == 1)(lambda: to_x(dy, level, p))
                to_pair(dy, level, p, bank)

            at_distance(dist, visit)

    def across(dist):
        for p in range(2):

            def visit(level, side):
                arrived(dd, level, p)
                to_pair(dd, level, p, DD_NEAR + bank_of(level))

            at_distance(dist, visit)

    def from_pair(bank, at, count):
        region = pl.ds(at, count)
        remote(
            all_tok.at[region],
            all_tok.at[region],
            flat_send.at[PAIR, 0],
            pair_recv.at[0, bank],
            at_pair,
        ).wait_recv()

        def go(f):
            part = slab.at[region] if f else slab.at[region, pl.ds(0, spill_at)]
            remote(
                part, part, flat_send.at[PAIR, 1], pair_recv.at[1, bank], at_pair
            ).wait_recv()

        either(hot, go)

    def group(parts, store):
        each = sum(n for _, _, n in parts)
        main_rows, spill_rows = 2 * each * TILE, each * 8

        def slots_of_core(core):
            return [pl.ds(slot(dp, level, core), n) for dp, level, n in parts]

        lanes_a, lanes_b = slots_of_core(0), slots_of_core(1)

        def rows_of(at, lanes):
            return [slab[r, at] for r in lanes]

        def low8(lanes, at, cut):
            return jnp.concatenate(
                [v.astype(f32)[:, cut : cut + 8].reshape(-1, LANES) for v in rows_of(at, lanes)],
                axis=0,
            )

        def tail_of(lanes):
            return jnp.concatenate(
                [low8(lanes, spill_at + j, 0) for j in range(half)]
                + [low8(lanes, spill_at + j, 8) for j in range(half)],
                axis=1,
            )

        tail_a, tail_b = tail_of(lanes_a), tail_of(lanes_b)
        first = lax.broadcasted_iota(jnp.int32, (spill_rows, features), 0) % 8 < 4
        first_w = lax.broadcasted_iota(jnp.int32, (spill_rows, LANES), 0) % 8 < 4
        tok_rows = jnp.where(first, tail_a, pltpu.roll(tail_b, 4, 0))
        cot_rows = jnp.where(first, pltpu.roll(tail_a, spill_rows - 4, 0), tail_b)
        tok_rows = jnp.where(hot, tok_rows, 0.0)
        cot_rows = jnp.where(hot, cot_rows, 0.0)

        def main_of(at):
            return jnp.concatenate(
                [v.reshape(-1, LANES) for v in rows_of(at, lanes_a + lanes_b)], axis=0
            )

        w_main = main_of(weight_at).astype(f32)
        w_tail = jnp.where(
            first_w, low8(lanes_a, weight_at, 0), pltpu.roll(low8(lanes_b, weight_at, 0), 4, 0)
        )
        main_lane = lax.broadcasted_iota(jnp.int32, (main_rows, LANES), 1)
        tail_lane = lax.broadcasted_iota(jnp.int32, (spill_rows, LANES), 1)
        w = jnp.concatenate(
            [
                jnp.sum(jnp.where(main_lane == e, w_main, 0.0), axis=1, keepdims=True),
                jnp.sum(jnp.where(tail_lane == e + LANES // 2, w_tail, 0.0), axis=1, keepdims=True),
            ],
            axis=0,
        )
        t_ref, og_ref, h_ref, gg_ref, ug_ref, at = store
        rows = pl.ds(at, main_rows + spill_rows)
        t_ref[rows, :] = jnp.concatenate(
            [all_tok[r].reshape(-1, features) for r in lanes_a + lanes_b]
            + [tok_rows.astype(bf16)],
            axis=0,
        )
        cot = jnp.concatenate(
            [
                jnp.concatenate([main_of(j) for j in range(blocks)], axis=1).astype(f32),
                cot_rows,
            ],
            axis=0,
        )
        og_ref[rows, :] = (w * cot).astype(bf16)
        t = t_ref[rows, :]
        gate_pre = jnp.dot(t, wg[...], preferred_element_type=f32)
        up_proj = jnp.dot(t, wu[...], preferred_element_type=f32)
        hidden_grad = lax.dot_general(og_ref[rows, :], wd[...], NT, preferred_element_type=f32)
        sig = jax.nn.sigmoid(gate_pre)
        act = gate_pre * sig
        h_ref[rows, :] = (act * up_proj).astype(bf16)
        gg_ref[rows, :] = (hidden_grad * up_proj * sig * (1.0 + gate_pre * (1.0 - sig))).astype(
            bf16
        )
        ug_ref[rows, :] = (hidden_grad * act).astype(bf16)

    main_rows = experts * TILE
    group_rows = main_rows + levels * 8
    early = (all_t, all_og, all_h, all_gg, all_ug)
    late = (late_t, late_og, late_h, late_gg, late_ug)

    column(1)
    beside(0)
    column(2)
    beside(1)
    column(3)
    from_pair(OWN, slot(d, 0, pc), levels)
    for copy in weight_copies:
        copy.wait()
    group([(d, 0, levels)], early + (0,))
    beside(2)
    own = pl.ds(0, group_rows)
    rg = lax.dot_general(all_gg[own, :], wg[...], NT, preferred_element_type=f32)
    rg = rg + lax.dot_general(all_ug[own, :], wu[...], NT, preferred_element_type=f32)
    lane_rows = main_rows // 2
    for j in range(blocks):
        cols = slice(j * LANES, (j + 1) * LANES)
        for core in range(2):
            row_out[core, :, j] = (
                rg[core * lane_rows : (core + 1) * lane_rows, cols]
                .reshape(levels, TILE, LANES)
                .astype(bf16)
            )
    for j in range(half):
        lo = rg[main_rows:, j * LANES : (j + 1) * LANES].reshape(levels, 8, LANES)
        hi = rg[main_rows:, (half + j) * LANES : (half + j + 1) * LANES].reshape(levels, 8, LANES)
        both = jnp.concatenate([lo, hi], axis=1).astype(bf16)
        for core in range(2):
            row_out[core, :, blocks + j] = both

    def row_copy(f):
        src, dst = row_out.at[pc], pair_in
        if not f:
            src, dst = row_out.at[pc, :, pl.ds(0, blocks)], pair_in.at[:, pl.ds(0, blocks)]
        return remote(src, dst, row_sem.at[0], row_sem.at[1], at_pair)

    either(hot, lambda f: row_copy(f).start())
    across(0)
    from_pair(NEAR, 0, levels)
    group([(dx, near, 2), (dy, near, 2)], early + (group_rows,))

    either(hot, lambda f: row_copy(f).wait_recv())
    for level in range(levels):
        row_sum[level, :blocks] = (
            row_out[c, level, :blocks].astype(f32) + pair_in[level, :blocks].astype(f32)
        ).astype(bf16)

    @pl.when(hot)
    def _():
        for level in range(levels):
            row_sum[level, blocks:] = (
                row_out[c, level, blocks:].astype(f32) + pair_in[level, blocks:].astype(f32)
            ).astype(bf16)

    def z_copy(level, sender, send, peer, f):
        src, dst = row_sum.at[level], z_in.at[sender]
        if not f:
            part = pl.ds(0, blocks)
            src, dst = row_sum.at[level, part], z_in.at[sender, part]
        return remote(src, dst, z_send.at[send], z_recv.at[sender], peer)

    for level in range(levels):

        @pl.when(z != level)
        def _():
            either(hot, lambda f: z_copy(level, z, level, (d, level * 2 + c), f).start())

    across(1)
    beside(3)
    from_pair(DD_NEAR, 0, 2)
    group([(dd, near, 2)], early + (2 * group_rows,))
    from_pair(FAR, 0, levels)
    group([(dx, far, 2), (dy, far, 2)], late + (0,))
    across(2)
    across(3)

    share = features // 4
    cols = pl.ds(pl.multiple_of(d * share, LANES), share)
    t_cols = all_t[:, cols]
    acc_gate[...] = lax.dot_general(t_cols, all_gg[...], TN, preferred_element_type=f32)
    acc_up[...] = lax.dot_general(t_cols, all_ug[...], TN, preferred_element_type=f32)
    acc_down[...] = lax.dot_general(all_h[...], all_og[...], TN, preferred_element_type=f32)
    z_in[z] = row_sum[z]

    from_pair(DD_FAR, 0, 2)
    group([(dd, far, 2)], late + (group_rows,))
    late_cols[...] = late_t[:, cols]

    for level in range(levels):

        @pl.when(z != level)
        def _():
            z_copy(level, level, level, at_pair, level < hot_levels).wait_recv()

    total = z_in[0, :blocks].astype(f32)
    spilled = z_in[0, blocks:].astype(f32)
    for level in range(1, levels):
        total = total + z_in[level, :blocks].astype(f32)
        if level < hot_levels:
            spilled = spilled + z_in[level, blocks:].astype(f32)
    kept_row = lax.broadcasted_iota(jnp.int32, (8, LANES), 0) < 4
    blank = jnp.zeros((8, LANES), f32)
    for j in range(blocks):
        tg_ref[:TILE, j * LANES : (j + 1) * LANES] = total[j].astype(bf16)
    for j in range(half):
        for at, rows in ((j, spilled[j][:8]), (half + j, spilled[j][8:])):
            rows = jnp.where(c == 0, rows, pltpu.roll(rows, 4, 0))
            tg_ref[TILE:, at * LANES : (at + 1) * LANES] = jnp.concatenate(
                [jnp.where(kept_row, rows, 0.0), blank], axis=0
            ).astype(bf16)

    def sent(send, p, count, f):
        region = pl.ds(0, count)
        part = all_tok.at[region]
        if p == 1:
            part = slab.at[region] if f else slab.at[region, pl.ds(0, spill_at)]
        remote(part, part, send, recv_sem.at[0, 0], at_x).wait_send()

    for p in range(2):
        for way in (X, Y):
            send = flat_send.at[way, p]
            more = (p + c) % 2 == (1 if way == X else 0)
            less = (p + c) % 2 == (0 if way == X else 1)
            wide = True if p == 0 else hot
            pl.when(less)(lambda: either(wide, lambda f: sent(send, p, levels, f)))
            pl.when(more)(lambda: either(wide, lambda f: sent(send, p, 2 * levels, f)))
        either(wide, lambda f: sent(flat_send.at[PAIR, p], p, 4 * levels, f))
        for level in range(1, levels):
            pl.when(jnp.logical_and(level >= z, low_z))(
                lambda: sent(down_send.at[p, level - 1], p, 1, True)
            )
        for level in range(levels - 1):
            pl.when(jnp.logical_and(level <= z, up_z))(
                lambda: either(
                    True if p == 0 else z + 1 < hot_levels,
                    lambda f: sent(up_send.at[p, level], p, 1, f),
                )
            )
    either(hot, lambda f: row_copy(f).wait_send())
    for level in range(levels):

        @pl.when(z != level)
        def _():
            either(hot, lambda f: z_copy(level, z, level, at_pair, f).wait_send())


def finish_kernel(
    tg_ref,
    acc_gate,
    acc_up,
    acc_down,
    late_cols,
    late_og,
    late_h,
    late_gg,
    late_ug,
    tg_out,
    gg_out,
    gu_out,
    gd_out,
    gg_ref,
    gu_ref,
    gd_ref,
    sem,
):
    bf16, f32 = jnp.bfloat16, jnp.float32
    copies = [pltpu.make_async_copy(tg_ref, tg_out, sem.at[0])]
    copies[0].start()
    hidden_size = acc_gate.shape[1]

    def write(src, dst):
        copies.append(pltpu.make_async_copy(src, dst, sem.at[len(copies)]))
        copies[-1].start()

    for j in range(hidden_size // LANES):
        rows = pl.ds(j * LANES, LANES)
        term = lax.dot_general(late_h[:, rows], late_og[...], TN, preferred_element_type=f32)
        gd_ref[rows, :] = (acc_down[rows, :] + term).astype(bf16)
        write(gd_ref.at[rows], gd_out.at[0, rows])
    term = lax.dot_general(late_cols[...], late_gg[...], TN, preferred_element_type=f32)
    gg_ref[...] = (acc_gate[...] + term).astype(bf16)
    write(gg_ref, gg_out.at[0])
    term = lax.dot_general(late_cols[...], late_ug[...], TN, preferred_element_type=f32)
    gu_ref[...] = (acc_up[...] + term).astype(bf16)
    write(gu_ref, gu_out.at[0])
    for copy in copies:
        copy.wait()


def dense_shards(tokens, cotangent, routes, combine, hot_experts, extra_slots, w_gate, w_up, w_down):
    experts = lax.axis_size("expert")
    replicas = lax.axis_size("dp")
    token_count, features = tokens.shape
    hidden_size = w_gate.shape[2]
    blocks = features // LANES
    half = blocks // 2
    levels = experts // 2
    slots = replicas * experts
    share = features // replicas
    group_rows = experts * TILE + levels * 8
    early_rows, late_rows = 2 * group_rows + group_rows // 2, group_rows + group_rows // 2
    bf16, f32 = jnp.bfloat16, jnp.float32
    vmem = pl.BlockSpec(memory_space=pltpu.VMEM)
    hbm = pl.BlockSpec(memory_space=pltpu.HBM)
    dma = pltpu.SemaphoreType.DMA
    operands = [
        pltpu.with_memory_space_constraint(a, pltpu.HBM)
        for a in (
            tokens,
            cotangent,
            routes.T,
            combine.T,
            hot_experts,
            extra_slots,
            w_gate,
            w_up,
            w_down,
        )
    ]
    parts = pl.pallas_call(
        functools.partial(dense_kernel, experts),
        out_shape=(
            jax.ShapeDtypeStruct((token_count, features), bf16),
            jax.ShapeDtypeStruct((share, hidden_size), f32),
            jax.ShapeDtypeStruct((share, hidden_size), f32),
            jax.ShapeDtypeStruct((hidden_size, features), f32),
            jax.ShapeDtypeStruct((late_rows, share), bf16),
            jax.ShapeDtypeStruct((late_rows, features), bf16),
            jax.ShapeDtypeStruct((late_rows, hidden_size), bf16),
            jax.ShapeDtypeStruct((late_rows, hidden_size), bf16),
            jax.ShapeDtypeStruct((late_rows, hidden_size), bf16),
        ),
        in_specs=[hbm] * 9,
        out_specs=(vmem,) * 9,
        scratch_shapes=[
            pltpu.VMEM((TILE, features), bf16),
            pltpu.VMEM(cotangent.shape, bf16),
            pltpu.VMEM(routes.shape[::-1], jnp.int32),
            pltpu.VMEM(routes.shape[::-1], bf16),
            pltpu.SMEM(hot_experts.shape, jnp.int32),
            pltpu.SMEM(hot_experts.shape, jnp.int32),
            pltpu.VMEM((slots, TILE, features), bf16),
            pltpu.VMEM((slots, blocks + 1 + half, TILE, LANES), bf16),
            pltpu.VMEM((features, hidden_size), bf16),
            pltpu.VMEM((features, hidden_size), bf16),
            pltpu.VMEM((hidden_size, features), bf16),
            pltpu.VMEM((early_rows, features), bf16),
            pltpu.VMEM((early_rows, features), bf16),
            pltpu.VMEM((early_rows, hidden_size), bf16),
            pltpu.VMEM((early_rows, hidden_size), bf16),
            pltpu.VMEM((early_rows, hidden_size), bf16),
            pltpu.VMEM((late_rows, features), bf16),
            pltpu.VMEM((2, levels, blocks + half, TILE, LANES), bf16),
            pltpu.VMEM((levels, blocks + half, TILE, LANES), bf16),
            pltpu.VMEM((levels, blocks + half, TILE, LANES), bf16),
            pltpu.VMEM((levels, blocks + half, TILE, LANES), bf16),
            dma((7,)),
            dma((3,)),
            dma((3, 2)),
            dma((2, levels - 1)),
            dma((2, levels - 1)),
            dma((2, slots // 2)),
            dma((2, 5)),
            dma((2,)),
            dma((levels,)),
            dma((levels,)),
            pltpu.SemaphoreType.REGULAR((3,)),
        ],
        compiler_params=pltpu.CompilerParams(
            collective_id=0, has_side_effects=True, vmem_limit_bytes=32 * 1024 * 1024
        ),
    )(*operands)
    return pl.pallas_call(
        finish_kernel,
        out_shape=(
            jax.ShapeDtypeStruct((token_count, features), bf16),
            jax.ShapeDtypeStruct((1, share, hidden_size), bf16),
            jax.ShapeDtypeStruct((1, share, hidden_size), bf16),
            jax.ShapeDtypeStruct((1, hidden_size, features), bf16),
        ),
        in_specs=[vmem] * len(parts),
        out_specs=(hbm,) * 4,
        scratch_shapes=[
            pltpu.VMEM((share, hidden_size), bf16),
            pltpu.VMEM((share, hidden_size), bf16),
            pltpu.VMEM((hidden_size, features), bf16),
            dma((3 + hidden_size // LANES,)),
        ],
        compiler_params=pltpu.CompilerParams(vmem_limit_bytes=16 * 1024 * 1024),
    )(*parts)


def solution(mesh):
    in_specs = (
        P(("dp", "expert"), None),
        P(("dp", "expert"), None),
        P(("dp", "expert"), None),
        P(("dp", "expert"), None),
        P(),
        P(),
        P("expert", None, None),
        P("expert", None, None),
        P("expert", None, None),
    )
    out_specs = (
        P(("dp", "expert"), None),
        P("expert", "dp", None),
        P("expert", "dp", None),
        P("expert", None, None),
    )

    def body(*args):
        token_count, features = args[0].shape
        if dense_fits(dict(mesh.shape), token_count, features, args[2].shape[1], args[6].shape[2]):
            return dense_shards(*args)
        return shards(*args)

    return jax.shard_map(body, mesh=mesh, in_specs=in_specs, out_specs=out_specs, check_vma=False)
```

```python
import functools

import jax
import jax.numpy as jnp
from jax import lax
from jax.experimental import pallas as pl
from jax.experimental.pallas import tpu as pltpu
from jax.sharding import PartitionSpec as P


def forward_rows(weight_gate, weight_up, weight_down, row_tokens, row_cotan, row_weights):
    gate_pre = jnp.dot(row_tokens, weight_gate, preferred_element_type=jnp.float32)
    up_proj = jnp.dot(row_tokens, weight_up, preferred_element_type=jnp.float32)
    sigmoid_gate = jax.nn.sigmoid(gate_pre)
    gate_act = gate_pre * sigmoid_gate
    hidden = (gate_act * up_proj).astype(jnp.bfloat16)
    out_grad = (row_weights.astype(jnp.float32)[:, None] * row_cotan.astype(jnp.float32)).astype(
        jnp.bfloat16
    )
    hidden_grad = jnp.dot(out_grad, weight_down.T, preferred_element_type=jnp.float32)
    gate_grad = (
        hidden_grad * up_proj * sigmoid_gate * (1.0 + gate_pre * (1.0 - sigmoid_gate))
    ).astype(jnp.bfloat16)
    up_grad = (hidden_grad * gate_act).astype(jnp.bfloat16)
    row_grads = jnp.dot(gate_grad, weight_gate.T, preferred_element_type=jnp.float32)
    row_grads = row_grads + jnp.dot(up_grad, weight_up.T, preferred_element_type=jnp.float32)
    return (row_grads.astype(jnp.bfloat16), (row_tokens, gate_grad, up_grad, hidden, out_grad))


def weight_terms(pieces):
    row_tokens, gate_grad, up_grad, hidden, out_grad = pieces
    grad_gate = jnp.dot(row_tokens.T, gate_grad, preferred_element_type=jnp.float32)
    grad_up = jnp.dot(row_tokens.T, up_grad, preferred_element_type=jnp.float32)
    grad_down = jnp.dot(hidden.T, out_grad, preferred_element_type=jnp.float32)
    return (grad_gate, grad_up, grad_down)


def expert_pass(weight_gate, weight_up, weight_down, row_tokens, row_cotan, row_weights):
    row_grads, pieces = forward_rows(
        weight_gate, weight_up, weight_down, row_tokens, row_cotan, row_weights
    )
    return (row_grads, weight_terms(pieces))


def shards(tokens, cotangent, routes, combine, hot_experts, extra_slots, w_gate, w_up, w_down):
    expert_count = lax.axis_size("expert")
    token_count, features = tokens.shape
    route_count = routes.shape[1]
    capacity = max(2, min(token_count * route_count * 7 // (8 * expert_count), token_count // 2))
    spare_slots = 2 * max(1, capacity // 6)
    expert_ids = routes.reshape(-1)
    assign_count = expert_ids.shape[0]
    assign_order = jnp.arange(assign_count, dtype=jnp.int32)
    earlier = (expert_ids[:, None] == expert_ids[None, :]) & (
        assign_order[None, :] < assign_order[:, None]
    )
    slot_rank = jnp.sum(earlier.astype(jnp.int32), axis=1)
    hot_match = expert_ids[:, None] == hot_experts[None, :]
    slot_limit = capacity + jnp.sum(jnp.where(hot_match, extra_slots[None, :], 0), axis=1)
    is_kept = slot_rank < slot_limit
    slot_count = capacity + spare_slots
    total_slots = expert_count * slot_count
    flat_slot = jnp.where(is_kept, expert_ids * slot_count + slot_rank, total_slots)
    slot_ids = jnp.arange(total_slots, dtype=jnp.int32)
    assign_onehot = slot_ids[:, None] == flat_slot[None, :]
    token_onehot = jnp.any(
        assign_onehot.reshape(total_slots, token_count, route_count), axis=2
    ).astype(jnp.bfloat16)
    both_rows = jnp.concatenate([tokens, cotangent], axis=1)
    filled = jnp.dot(token_onehot, both_rows, preferred_element_type=jnp.float32).astype(
        jnp.bfloat16
    )
    token_send = filled[:, :features].reshape(expert_count, slot_count, features)
    cotan_send = filled[:, features:].reshape(expert_count, slot_count, features)
    weight_flat = jnp.sum(
        jnp.where(assign_onehot, combine.reshape(-1).astype(jnp.float32)[None, :], 0.0), axis=1
    )
    weight_send = weight_flat.astype(jnp.bfloat16).reshape(expert_count, slot_count)
    token_recv, cotan_recv, weight_recv = (
        lax.all_to_all(token_send, "expert", split_axis=0, concat_axis=0, tiled=True),
        lax.all_to_all(cotan_send, "expert", split_axis=0, concat_axis=0, tiled=True),
        lax.all_to_all(weight_send, "expert", split_axis=0, concat_axis=0, tiled=True),
    )
    own_weights = (w_gate[0], w_up[0], w_down[0])
    all_rows, grad_terms = expert_pass(
        own_weights[0],
        own_weights[1],
        own_weights[2],
        token_recv.reshape(-1, features),
        cotan_recv.reshape(-1, features),
        weight_recv.reshape(-1),
    )
    grad_rows = all_rows.reshape(expert_count, slot_count, features)
    returned_rows = lax.all_to_all(grad_rows, "expert", split_axis=0, concat_axis=0, tiled=True)
    token_grads = jnp.dot(
        token_onehot.T,
        returned_rows.reshape(total_slots, features),
        preferred_element_type=jnp.float32,
    ).astype(jnp.bfloat16)
    grad_gate, grad_up = (
        lax.psum_scatter(grad_terms[0][None], "dp", scatter_dimension=1, tiled=True),
        lax.psum_scatter(grad_terms[1][None], "dp", scatter_dimension=1, tiled=True),
    )
    grad_down = lax.psum(grad_terms[2][None], "dp")
    return (
        token_grads,
        grad_gate.astype(jnp.bfloat16),
        grad_up.astype(jnp.bfloat16),
        grad_down.astype(jnp.bfloat16),
    )


MESH = pl.DeviceIdType.MESH
LANES = 128
TILE = 16
NT = (((1,), (1,)), ((), ()))
TN = (((0,), (0,)), ((), ()))


def slots_of(token_count, route_count, expert_count):
    capacity = max(2, min(token_count * route_count * 7 // (8 * expert_count), token_count // 2))
    return capacity, 2 * max(1, capacity // 6)


def dense_fits(sizes, token_count, features, route_count, hidden_size):
    capacity, spare = slots_of(token_count, route_count, sizes["expert"])
    return (
        route_count == sizes["expert"]
        and sizes["dp"] == 4
        and sizes["expert"] == 8
        and token_count == 2 * TILE
        and capacity == TILE
        and spare * 2 == 8
        and features % (8 * LANES) == 0
        and hidden_size % LANES == 0
    )


def dense_kernel(
    experts,
    tok_hbm,
    cot_hbm,
    routes_hbm,
    comb_hbm,
    hot_hbm,
    extra_hbm,
    wg_hbm,
    wu_hbm,
    wd_hbm,
    tg_ref,
    acc_gate,
    acc_up,
    acc_down,
    late_cols,
    late_og,
    late_h,
    late_gg,
    late_ug,
    tok_ref,
    cot_ref,
    routes_ref,
    comb_ref,
    hot_ref,
    extra_ref,
    all_tok,
    slab,
    wg,
    wu,
    wd,
    all_t,
    all_og,
    all_h,
    all_gg,
    all_ug,
    late_t,
    row_out,
    pair_in,
    row_sum,
    z_in,
    in_sem,
    w_sem,
    flat_send,
    own_send,
    z_own,
    diag_send,
    recv_sem,
    pair_recv,
    row_sem,
    z_send,
    z_recv,
    ready,
):
    levels = experts // 2
    hot_levels = levels // 2
    features = all_tok.shape[2]
    blocks = features // LANES
    half = blocks // 2
    weight_at, spill_at = blocks, blocks + 1
    bf16, f32 = jnp.bfloat16, jnp.float32

    d = lax.axis_index("dp")
    e = lax.axis_index("expert")
    z, c = e // 2, e % 2
    dx = d + 1 - 2 * (d % 2)
    dy = (d + 2) % 4
    dd = 3 - d
    pc = 1 - c
    upper_half = z // 2
    near, far = 2 * upper_half, 2 - 2 * upper_half
    hot = z < hot_levels
    low_x, low_y, low_z = d % 2 == 1, d // 2 == 1, z > 0
    up_x, up_y, up_z = d % 2 == 0, d // 2 == 0, z < levels - 1
    first_z, last_z = z == 0, z == levels - 1
    at_below, at_above = (d, jnp.maximum(e - 2, 0)), (d, jnp.minimum(e + 2, experts - 1))
    at_top, at_bottom = (d, (levels - 1) * 2 + c), (d, c)
    at_x, at_y, at_pair = (dx, e), (dy, e), (d, z * 2 + pc)
    at_diag = (dd, e)
    upper = z >= hot_levels
    low_d, up_d = jnp.logical_and(upper, d > dd), jnp.logical_and(upper, d < dd)

    def slot(dp, level, core):
        return (dp * 2 + core) * levels + level

    me = slot(d, z, c)
    input_copies = [
        pltpu.make_async_copy(h, v, in_sem.at[i])
        for i, (h, v) in enumerate(
            (
                (tok_hbm.at[pl.ds(TILE, TILE)], tok_ref),
                (cot_hbm, cot_ref),
                (routes_hbm, routes_ref),
                (comb_hbm, comb_ref),
                (hot_hbm, hot_ref),
                (extra_hbm, extra_ref),
                (tok_hbm.at[pl.ds(0, TILE)], all_tok.at[me]),
            )
        )
    ]
    own_tokens = input_copies.pop()
    weight_copies = [
        pltpu.make_async_copy(h.at[0], v, w_sem.at[i])
        for i, (h, v) in enumerate(((wg_hbm, wg), (wu_hbm, wu), (wd_hbm, wd)))
    ]

    barrier = pltpu.get_barrier_semaphore()

    def greet(peer):
        pl.semaphore_signal(barrier, inc=1, device_id=peer, device_id_type=MESH)

    greet(at_pair)
    pl.when(up_x)(lambda: greet(at_x))
    pl.when(up_y)(lambda: greet(at_y))
    pl.when(up_z)(lambda: greet(at_above))
    pl.when(first_z)(lambda: greet(at_top))
    pl.when(up_d)(lambda: greet(at_diag))
    for copy in input_copies + [own_tokens] + weight_copies:
        copy.start()

    def piece(s, p, full):
        if p == 0:
            return all_tok.at[s]
        return slab.at[s] if full else slab.at[s, pl.ds(0, spill_at)]

    def either(full, visit):
        if full is True or full is False:
            visit(full)
            return
        pl.when(full)(lambda: visit(True))
        pl.when(jnp.logical_not(full))(lambda: visit(False))

    def remote(src, dst, send, recv, peer):
        return pltpu.make_async_remote_copy(
            src_ref=src,
            dst_ref=dst,
            send_sem=send,
            recv_sem=recv,
            device_id=peer,
            device_id_type=MESH,
        )

    def push(dp, level, p, full, send, peer, own=False):
        s = slot(dp, level, c)

        def go(f):
            dst = piece(s, p, f)
            src = tok_hbm.at[pl.ds(0, TILE)] if own and p == 0 else dst
            remote(src, dst, send, recv_sem.at[p, dp * levels + level], peer).start()

        either(True if p == 0 else full, go)

    X, Y, PAIR = range(3)

    def to_side(way, dp, level, p, full, own):
        peer = at_x if way == X else at_y
        send = flat_send.at[way, p]
        if p == 0 or not own:
            push(dp, level, p, full, send, peer, own)
            return
        pl.when(hot)(lambda: push(dp, level, p, True, send, peer, own))
        pl.when(upper)(lambda: push(dp, level, p, True, own_send.at[way], peer, own))

    def to_x(dp, level, p, own=False):
        to_side(X, dp, level, p, True if own else hot, own)

    def to_y(dp, level, p, own=False):
        to_side(Y, dp, level, p, True if own else hot, own)

    def to_below(p):
        push(d, z, p, True, z_own.at[p, 0], at_below, True)

    def to_above(p):
        push(d, z, p, z + 1 < hot_levels, z_own.at[p, 1], at_above, True)

    def to_top(p):
        push(d, z, p, False, z_own.at[p, 0], at_top, True)

    def to_bottom(p):
        push(d, z, p, True, z_own.at[p, 2], at_bottom, True)

    def pass_down(level, p, at):
        push(d, level, p, True, z_own.at[p, at], at_below)

    def pass_up(level, p):
        push(d, level, p, False, z_own.at[p, 3], at_above)

    def to_diag(p):
        push(d, z, p, True, diag_send.at[p, 0], at_diag, True)

    def pass_across(p, at, peer):
        push(dd, z, p, True, diag_send.at[p, at], peer)

    def to_pair(dp, level, p, bank, own=False):
        s = slot(dp, level, c)

        def go(f):
            dst = piece(s, p, f)
            src = tok_hbm.at[pl.ds(0, TILE)] if own and p == 0 else dst
            remote(src, dst, flat_send.at[PAIR, p], pair_recv.at[p, bank], at_pair).start()

        either(True if p == 0 else hot, go)

    def arrived(dp, level, p, full):
        s = slot(dp, level, c)

        def go(f):
            dst = piece(s, p, f)
            at = recv_sem.at[p, dp * levels + level]
            remote(dst, dst, flat_send.at[X, p], at, at_x).wait_recv()

        either(True if p == 0 else full, go)

    pl.semaphore_wait(
        barrier, 1 + d % 2 + d // 2 + jnp.minimum(z, 1) + z // (levels - 1) + upper_half * (d // 2)
    )

    def tell(way, peer):
        pl.semaphore_signal(ready.at[way], inc=1, device_id=peer, device_id_type=MESH)

    pl.when(low_x)(lambda: tell(0, at_x))
    pl.when(low_y)(lambda: tell(1, at_y))
    pl.when(low_z)(lambda: tell(3, at_below))
    pl.when(last_z)(lambda: tell(4, at_bottom))
    pl.when(low_d)(lambda: tell(2, at_diag))

    OWN, NEAR, FAR, DD = range(4)

    def to_lower(p):
        pl.when(low_z)(lambda: to_below(p))
        pl.when(last_z)(lambda: to_bottom(p))
        pl.when(low_x)(lambda: to_x(d, z, p, True))
        pl.when(low_y)(lambda: to_y(d, z, p, True))
        pl.when(low_d)(lambda: to_diag(p))
        to_pair(d, z, p, OWN, True)

    to_lower(0)

    for copy in input_copies:
        copy.wait()
    names = -(-experts // TILE) * TILE
    expert_row = lax.broadcasted_iota(jnp.int32, (names, 2 * TILE), 0)
    token_lane = lax.broadcasted_iota(jnp.int32, (names, 2 * TILE), 1)
    routes = routes_ref[...]
    comb = comb_ref[...].astype(f32)
    weights = jnp.zeros((names, 2 * TILE), f32)
    for r in range(routes.shape[0]):
        weights = jnp.where(expert_row == routes[r : r + 1, :], comb[r : r + 1, :], weights)
    limit = jnp.full((names, 2 * TILE), TILE, jnp.int32)
    for j in range(hot_ref.shape[0]):
        limit = limit + jnp.where(expert_row == hot_ref[j], extra_ref[j], 0)
    weights = jnp.where(token_lane < limit, weights, 0.0).astype(bf16)
    unit_row = lax.broadcasted_iota(jnp.int32, (names, LANES), 0)
    unit_lane = lax.broadcasted_iota(jnp.int32, (names, LANES), 1)

    def turned(shift):
        unit = jnp.where(unit_lane == unit_row + shift, 1.0, 0.0).astype(bf16)
        return lax.dot_general(weights, unit, TN, preferred_element_type=f32)

    main_part, tail_part = turned(0), turned(LANES // 2)
    slab[me, weight_at] = (main_part[:TILE] + tail_part[TILE:]).astype(bf16)
    tok_tail = tok_ref[...].astype(f32)[:8]
    cot_tail = cot_ref[TILE:, :].astype(f32)[:8]
    tail_row = lax.broadcasted_iota(jnp.int32, (8, features), 0)
    spill = jnp.where(tail_row < 4, tok_tail, pltpu.roll(cot_tail, 4, 0))
    for j in range(blocks):
        slab[me, j] = cot_ref[:TILE, j * LANES : (j + 1) * LANES]
    for j in range(half):
        lo = spill[:, j * LANES : (j + 1) * LANES]
        hi = spill[:, (half + j) * LANES : (half + j + 1) * LANES]
        slab[me, spill_at + j] = jnp.concatenate([lo, hi], axis=0).astype(bf16)

    to_lower(1)

    def to_upper(way, up, act):
        @pl.when(up)
        def _():
            pl.semaphore_wait(ready.at[way], 1)
            for p in range(2):
                act(p)

    to_upper(3, up_z, to_above)
    to_upper(0, up_x, lambda p: to_x(d, z, p, True))
    to_upper(1, up_y, lambda p: to_y(d, z, p, True))
    to_upper(2, up_d, to_diag)
    own_tokens.wait()

    def at_distance(dist, visit):
        if dist == 0:
            visit(z, 0)
            return
        pl.when(z - dist >= 0)(lambda: visit(z - dist, -1))
        pl.when(z + dist < levels)(lambda: visit(z + dist, 1))

    def bank_of(level):
        return (level // 2 + upper_half) % 2

    def column(dist, p):
        def visit(level, side):
            arrived(d, level, p, True if side > 0 else hot)
            if dist == 1 and side > 0:
                pl.when(low_z)(lambda: pass_down(level, p, 2))
            elif dist == 1:
                pl.when(up_z)(lambda: pass_up(level, p))
            to_x(d, level, p)
            to_y(d, level, p)
            to_pair(d, level, p, OWN)

        at_distance(dist, visit)

    def beside(dist, p):
        full = True if dist == 0 else hot
        keep = (hot, True, low_z, low_z)[dist]

        def visit(level, side, keep=keep):
            bank = NEAR + bank_of(level)
            if dist == 1 and side < 0:
                keep = z != 1
            arrived(dx, level, p, full)
            turn = jnp.logical_and((p + c) % 2 == 0, keep)
            pl.when(turn)(lambda: to_y(dx, level, p))
            to_pair(dx, level, p, bank)
            arrived(dy, level, p, full)
            turn = jnp.logical_and((p + c) % 2 == 1, keep)
            pl.when(turn)(lambda: to_x(dy, level, p))
            to_pair(dy, level, p, bank)

        at_distance(dist, visit)

    def across(dist, p):
        full = True if dist == 0 else hot

        def visit(level, side):
            arrived(dd, level, p, full)
            if dist == 0:
                pl.when(last_z)(lambda: pass_across(p, 1, at_bottom))
                pl.when(z == 2)(lambda: pass_across(p, 1, at_bottom))
                pl.when(first_z)(lambda: pass_across(p, 1, at_above))
            to_pair(dd, level, p, DD)

        at_distance(dist, visit)

    def from_pair(bank, at, count):
        region = pl.ds(at, count)
        remote(
            all_tok.at[region],
            all_tok.at[region],
            flat_send.at[PAIR, 0],
            pair_recv.at[0, bank],
            at_pair,
        ).wait_recv()

        def go(f):
            part = slab.at[region] if f else slab.at[region, pl.ds(0, spill_at)]
            remote(
                part, part, flat_send.at[PAIR, 1], pair_recv.at[1, bank], at_pair
            ).wait_recv()

        either(hot, go)

    def group(parts, store):
        each = sum(n for _, _, n in parts)
        main_rows, spill_rows = 2 * each * TILE, each * 8

        def slots_of_core(core):
            return [pl.ds(slot(dp, level, core), n) for dp, level, n in parts]

        lanes_a, lanes_b = slots_of_core(0), slots_of_core(1)

        def rows_of(at, lanes):
            return [slab[r, at] for r in lanes]

        def low8(lanes, at, cut):
            return jnp.concatenate(
                [v.astype(f32)[:, cut : cut + 8].reshape(-1, LANES) for v in rows_of(at, lanes)],
                axis=0,
            )

        def tail_of(lanes):
            return jnp.concatenate(
                [low8(lanes, spill_at + j, 0) for j in range(half)]
                + [low8(lanes, spill_at + j, 8) for j in range(half)],
                axis=1,
            )

        tail_a, tail_b = tail_of(lanes_a), tail_of(lanes_b)
        first = lax.broadcasted_iota(jnp.int32, (spill_rows, features), 0) % 8 < 4
        first_w = lax.broadcasted_iota(jnp.int32, (spill_rows, LANES), 0) % 8 < 4
        tok_rows = jnp.where(first, tail_a, pltpu.roll(tail_b, 4, 0))
        cot_rows = jnp.where(first, pltpu.roll(tail_a, spill_rows - 4, 0), tail_b)
        tok_rows = jnp.where(hot, tok_rows, 0.0)
        cot_rows = jnp.where(hot, cot_rows, 0.0)

        def main_of(at):
            return jnp.concatenate(
                [v.reshape(-1, LANES) for v in rows_of(at, lanes_a + lanes_b)], axis=0
            )

        w_main = main_of(weight_at).astype(f32)
        w_tail = jnp.where(
            first_w, low8(lanes_a, weight_at, 0), pltpu.roll(low8(lanes_b, weight_at, 0), 4, 0)
        )
        main_lane = lax.broadcasted_iota(jnp.int32, (main_rows, LANES), 1)
        tail_lane = lax.broadcasted_iota(jnp.int32, (spill_rows, LANES), 1)
        w = jnp.concatenate(
            [
                jnp.sum(jnp.where(main_lane == e, w_main, 0.0), axis=1, keepdims=True),
                jnp.sum(jnp.where(tail_lane == e + LANES // 2, w_tail, 0.0), axis=1, keepdims=True),
            ],
            axis=0,
        )
        t_ref, og_ref, h_ref, gg_ref, ug_ref, at = store
        rows = pl.ds(at, main_rows + spill_rows)
        t_ref[rows, :] = jnp.concatenate(
            [all_tok[r].reshape(-1, features) for r in lanes_a + lanes_b]
            + [tok_rows.astype(bf16)],
            axis=0,
        )
        cot = jnp.concatenate(
            [
                jnp.concatenate([main_of(j) for j in range(blocks)], axis=1).astype(f32),
                cot_rows,
            ],
            axis=0,
        )
        og_ref[rows, :] = (w * cot).astype(bf16)
        t = t_ref[rows, :]
        gate_pre = jnp.dot(t, wg[...], preferred_element_type=f32)
        up_proj = jnp.dot(t, wu[...], preferred_element_type=f32)
        hidden_grad = lax.dot_general(og_ref[rows, :], wd[...], NT, preferred_element_type=f32)
        sig = jax.nn.sigmoid(gate_pre)
        act = gate_pre * sig
        h_ref[rows, :] = (act * up_proj).astype(bf16)
        gg_ref[rows, :] = (hidden_grad * up_proj * sig * (1.0 + gate_pre * (1.0 - sig))).astype(
            bf16
        )
        ug_ref[rows, :] = (hidden_grad * act).astype(bf16)

    main_rows = experts * TILE
    group_rows = main_rows + levels * 8
    early = (all_t, all_og, all_h, all_gg, all_ug)
    late = (late_t, late_og, late_h, late_gg, late_ug)

    for p in range(2):
        beside(0, p)
        column(1, p)
    to_upper(4, first_z, to_top)

    for p in range(2):
        for dist in (2, 3):
            column(dist, p)

    @pl.when(upper)
    def _():
        for p in range(2):
            across(0, p)

    from_pair(OWN, slot(d, 0, pc), levels)
    for copy in weight_copies:
        copy.wait()
    group([(d, 0, levels)], early + (0,))
    @pl.when(hot)
    def _():
        for p in range(2):
            across(0, p)

    own = pl.ds(0, group_rows)
    rg = lax.dot_general(all_gg[own, :], wg[...], NT, preferred_element_type=f32)
    rg = rg + lax.dot_general(all_ug[own, :], wu[...], NT, preferred_element_type=f32)
    lane_rows = main_rows // 2
    for j in range(blocks):
        cols = slice(j * LANES, (j + 1) * LANES)
        for core in range(2):
            row_out[core, :, j] = (
                rg[core * lane_rows : (core + 1) * lane_rows, cols]
                .reshape(levels, TILE, LANES)
                .astype(bf16)
            )
    for j in range(half):
        lo = rg[main_rows:, j * LANES : (j + 1) * LANES].reshape(levels, 8, LANES)
        hi = rg[main_rows:, (half + j) * LANES : (half + j + 1) * LANES].reshape(levels, 8, LANES)
        both = jnp.concatenate([lo, hi], axis=1).astype(bf16)
        for core in range(2):
            row_out[core, :, blocks + j] = both

    def row_copy(f):
        src, dst = row_out.at[pc], pair_in
        if not f:
            src, dst = row_out.at[pc, :, pl.ds(0, blocks)], pair_in.at[:, pl.ds(0, blocks)]
        return remote(src, dst, row_sem.at[0], row_sem.at[1], at_pair)

    either(hot, lambda f: row_copy(f).start())
    for p in range(2):
        beside(1, p)

    either(hot, lambda f: row_copy(f).wait_recv())
    for level in range(levels):
        row_sum[level, :blocks] = (
            row_out[c, level, :blocks].astype(f32) + pair_in[level, :blocks].astype(f32)
        ).astype(bf16)

    @pl.when(hot)
    def _():
        for level in range(levels):
            row_sum[level, blocks:] = (
                row_out[c, level, blocks:].astype(f32) + pair_in[level, blocks:].astype(f32)
            ).astype(bf16)

    def z_copy(level, sender, send, peer, f):
        src, dst = row_sum.at[level], z_in.at[sender]
        if not f:
            part = pl.ds(0, blocks)
            src, dst = row_sum.at[level, part], z_in.at[sender, part]
        return remote(src, dst, z_send.at[send], z_recv.at[sender], peer)

    for level in range(levels):

        @pl.when(z != level)
        def _():
            either(hot, lambda f: z_copy(level, z, level, (d, level * 2 + c), f).start())

    @pl.when(low_z)
    def _():
        for dist in (2, 3):
            for p in range(2):
                beside(dist, p)

    from_pair(NEAR, 0, levels)
    group([(dx, near, 2), (dy, near, 2)], early + (group_rows,))

    @pl.when(first_z)
    def _():
        for dist in (2, 3):
            for p in range(2):
                beside(dist, p)

    def across_when(cond, *dists):
        @pl.when(cond)
        def _():
            for dist in dists:
                for p in range(2):
                    across(dist, p)

    across_when(first_z, 3, 2)
    across_when(low_z, 1)
    across_when(last_z, 2, 3)
    share = features // 4
    cols = pl.ds(pl.multiple_of(d * share, LANES), share)
    t_cols = all_t[:, cols]
    acc_gate[...] = lax.dot_general(t_cols, all_gg[...], TN, preferred_element_type=f32)
    acc_up[...] = lax.dot_general(t_cols, all_ug[...], TN, preferred_element_type=f32)
    acc_down[...] = lax.dot_general(all_h[...], all_og[...], TN, preferred_element_type=f32)
    from_pair(FAR, 0, levels)
    group([(dx, far, 2), (dy, far, 2)], late + (0,))
    across_when(first_z, 1)
    across_when(jnp.logical_and(low_z, up_z), 2)
    from_pair(DD, 0, levels)
    group([(dd, 0, levels)], late + (group_rows,))
    late_cols[...] = late_t[:, cols]
    z_in[z] = row_sum[z]

    for level in range(levels):

        @pl.when(z != level)
        def _():
            z_copy(level, level, level, at_pair, level < hot_levels).wait_recv()

    total = z_in[0, :blocks].astype(f32)
    spilled = z_in[0, blocks:].astype(f32)
    for level in range(1, levels):
        total = total + z_in[level, :blocks].astype(f32)
        if level < hot_levels:
            spilled = spilled + z_in[level, blocks:].astype(f32)
    kept_row = lax.broadcasted_iota(jnp.int32, (8, LANES), 0) < 4
    blank = jnp.zeros((8, LANES), f32)
    for j in range(blocks):
        tg_ref[:TILE, j * LANES : (j + 1) * LANES] = total[j].astype(bf16)
    for j in range(half):
        for at, rows in ((j, spilled[j][:8]), (half + j, spilled[j][8:])):
            rows = jnp.where(c == 0, rows, pltpu.roll(rows, 4, 0))
            tg_ref[TILE:, at * LANES : (at + 1) * LANES] = jnp.concatenate(
                [jnp.where(kept_row, rows, 0.0), blank], axis=0
            ).astype(bf16)

    def sent(send, p, count, f, first=0):
        region = pl.ds(first, count)
        part = all_tok.at[region]
        if p == 1:
            part = slab.at[region] if f else slab.at[region, pl.ds(0, spill_at)]
        remote(part, part, send, recv_sem.at[0, 0], at_x).wait_send()

    for p in range(2):
        wide = True if p == 0 else hot
        for way in (X, Y):
            send = flat_send.at[way, p]
            more = (p + c) % 2 == (1 if way == X else 0)
            less = (p + c) % 2 == (0 if way == X else 1)
            for at, extra in ((0, 2), (1, levels - 1), (2, levels - 1)):
                here = (z == 0, z == 1, upper)[at]
                own = 1 if at == 2 and p == 1 else 0
                f = not (at == 2 and p == 1)
                pl.when(jnp.logical_and(here, less))(
                    functools.partial(sent, send, p, levels - own, f)
                )
                pl.when(jnp.logical_and(here, more))(
                    functools.partial(sent, send, p, levels - own + extra, f)
                )
            if p == 1:
                pl.when(upper)(functools.partial(sent, own_send.at[way], 1, 1, True))
        either(wide, lambda f: sent(flat_send.at[PAIR, p], p, 4 * levels, f))

        pl.when(upper)(functools.partial(sent, diag_send.at[p, 0], p, 1, True))
        pl.when(z != 1)(functools.partial(sent, diag_send.at[p, 1], p, 1, True))

        pl.when(first_z)(functools.partial(sent, z_own.at[p, 0], p, 1, False))
        pl.when(first_z)(functools.partial(sent, z_own.at[p, 1], p, 1, True))
        pl.when(low_z)(functools.partial(sent, z_own.at[p, 0], p, 1, True))
        pl.when(low_z)(functools.partial(sent, z_own.at[p, 2], p, 1, True))

        @pl.when(jnp.logical_and(low_z, up_z))
        def _():
            sent(z_own.at[p, 1], p, 1, False)
            sent(z_own.at[p, 3], p, 1, False)

    either(hot, lambda f: row_copy(f).wait_send())
    for level in range(levels):

        @pl.when(z != level)
        def _():
            either(hot, lambda f: z_copy(level, z, level, at_pair, f).wait_send())


def finish_kernel(
    tg_ref,
    acc_gate,
    acc_up,
    acc_down,
    late_cols,
    late_og,
    late_h,
    late_gg,
    late_ug,
    tg_out,
    gg_out,
    gu_out,
    gd_out,
    gg_ref,
    gu_ref,
    gd_ref,
    sem,
):
    bf16, f32 = jnp.bfloat16, jnp.float32
    copies = [pltpu.make_async_copy(tg_ref, tg_out, sem.at[0])]
    copies[0].start()
    hidden_size = acc_gate.shape[1]

    def write(src, dst):
        copies.append(pltpu.make_async_copy(src, dst, sem.at[len(copies)]))
        copies[-1].start()

    for j in range(hidden_size // LANES):
        rows = pl.ds(j * LANES, LANES)
        term = lax.dot_general(late_h[:, rows], late_og[...], TN, preferred_element_type=f32)
        gd_ref[rows, :] = (acc_down[rows, :] + term).astype(bf16)
        write(gd_ref.at[rows], gd_out.at[0, rows])
    term = lax.dot_general(late_cols[...], late_gg[...], TN, preferred_element_type=f32)
    gg_ref[...] = (acc_gate[...] + term).astype(bf16)
    write(gg_ref, gg_out.at[0])
    term = lax.dot_general(late_cols[...], late_ug[...], TN, preferred_element_type=f32)
    gu_ref[...] = (acc_up[...] + term).astype(bf16)
    write(gu_ref, gu_out.at[0])
    for copy in copies:
        copy.wait()


def dense_shards(tokens, cotangent, routes, combine, hot_experts, extra_slots, w_gate, w_up, w_down):
    experts = lax.axis_size("expert")
    replicas = lax.axis_size("dp")
    token_count, features = tokens.shape
    hidden_size = w_gate.shape[2]
    blocks = features // LANES
    half = blocks // 2
    levels = experts // 2
    slots = replicas * experts
    share = features // replicas
    group_rows = experts * TILE + levels * 8
    early_rows, late_rows = 2 * group_rows, 2 * group_rows
    bf16, f32 = jnp.bfloat16, jnp.float32
    vmem = pl.BlockSpec(memory_space=pltpu.VMEM)
    hbm = pl.BlockSpec(memory_space=pltpu.HBM)
    dma = pltpu.SemaphoreType.DMA
    operands = [
        pltpu.with_memory_space_constraint(a, pltpu.HBM)
        for a in (
            tokens,
            cotangent,
            routes.T,
            combine.T,
            hot_experts,
            extra_slots,
            w_gate,
            w_up,
            w_down,
        )
    ]
    parts = pl.pallas_call(
        functools.partial(dense_kernel, experts),
        out_shape=(
            jax.ShapeDtypeStruct((token_count, features), bf16),
            jax.ShapeDtypeStruct((share, hidden_size), f32),
            jax.ShapeDtypeStruct((share, hidden_size), f32),
            jax.ShapeDtypeStruct((hidden_size, features), f32),
            jax.ShapeDtypeStruct((late_rows, share), bf16),
            jax.ShapeDtypeStruct((late_rows, features), bf16),
            jax.ShapeDtypeStruct((late_rows, hidden_size), bf16),
            jax.ShapeDtypeStruct((late_rows, hidden_size), bf16),
            jax.ShapeDtypeStruct((late_rows, hidden_size), bf16),
        ),
        in_specs=[hbm] * 9,
        out_specs=(vmem,) * 9,
        scratch_shapes=[
            pltpu.VMEM((TILE, features), bf16),
            pltpu.VMEM(cotangent.shape, bf16),
            pltpu.VMEM(routes.shape[::-1], jnp.int32),
            pltpu.VMEM(routes.shape[::-1], bf16),
            pltpu.SMEM(hot_experts.shape, jnp.int32),
            pltpu.SMEM(hot_experts.shape, jnp.int32),
            pltpu.VMEM((slots, TILE, features), bf16),
            pltpu.VMEM((slots, blocks + 1 + half, TILE, LANES), bf16),
            pltpu.VMEM((features, hidden_size), bf16),
            pltpu.VMEM((features, hidden_size), bf16),
            pltpu.VMEM((hidden_size, features), bf16),
            pltpu.VMEM((early_rows, features), bf16),
            pltpu.VMEM((early_rows, features), bf16),
            pltpu.VMEM((early_rows, hidden_size), bf16),
            pltpu.VMEM((early_rows, hidden_size), bf16),
            pltpu.VMEM((early_rows, hidden_size), bf16),
            pltpu.VMEM((late_rows, features), bf16),
            pltpu.VMEM((2, levels, blocks + half, TILE, LANES), bf16),
            pltpu.VMEM((levels, blocks + half, TILE, LANES), bf16),
            pltpu.VMEM((levels, blocks + half, TILE, LANES), bf16),
            pltpu.VMEM((levels, blocks + half, TILE, LANES), bf16),
            dma((7,)),
            dma((3,)),
            dma((3, 2)),
            dma((2,)),
            dma((2, levels)),
            dma((2, 2)),
            dma((2, slots // 2)),
            dma((2, 4)),
            dma((2,)),
            dma((levels,)),
            dma((levels,)),
            pltpu.SemaphoreType.REGULAR((5,)),
        ],
        compiler_params=pltpu.CompilerParams(
            collective_id=0, has_side_effects=True, vmem_limit_bytes=32 * 1024 * 1024
        ),
    )(*operands)
    return pl.pallas_call(
        finish_kernel,
        out_shape=(
            jax.ShapeDtypeStruct((token_count, features), bf16),
            jax.ShapeDtypeStruct((1, share, hidden_size), bf16),
            jax.ShapeDtypeStruct((1, share, hidden_size), bf16),
            jax.ShapeDtypeStruct((1, hidden_size, features), bf16),
        ),
        in_specs=[vmem] * len(parts),
        out_specs=(hbm,) * 4,
        scratch_shapes=[
            pltpu.VMEM((share, hidden_size), bf16),
            pltpu.VMEM((share, hidden_size), bf16),
            pltpu.VMEM((hidden_size, features), bf16),
            dma((3 + hidden_size // LANES,)),
        ],
        compiler_params=pltpu.CompilerParams(vmem_limit_bytes=16 * 1024 * 1024),
    )(*parts)


def solution(mesh):
    in_specs = (
        P(("dp", "expert"), None),
        P(("dp", "expert"), None),
        P(("dp", "expert"), None),
        P(("dp", "expert"), None),
        P(),
        P(),
        P("expert", None, None),
        P("expert", None, None),
        P("expert", None, None),
    )
    out_specs = (
        P(("dp", "expert"), None),
        P("expert", "dp", None),
        P("expert", "dp", None),
        P("expert", None, None),
    )

    def body(*args):
        token_count, features = args[0].shape
        if dense_fits(dict(mesh.shape), token_count, features, args[2].shape[1], args[6].shape[2]):
            return dense_shards(*args)
        return shards(*args)

    return jax.shard_map(body, mesh=mesh, in_specs=in_specs, out_specs=out_specs, check_vma=False)
```

```python
import functools

import jax
import jax.numpy as jnp
from jax import lax
from jax.experimental import pallas as pl
from jax.experimental.pallas import tpu as pltpu
from jax.sharding import PartitionSpec as P


def forward_rows(weight_gate, weight_up, weight_down, row_tokens, row_cotan, row_weights):
    gate_pre = jnp.dot(row_tokens, weight_gate, preferred_element_type=jnp.float32)
    up_proj = jnp.dot(row_tokens, weight_up, preferred_element_type=jnp.float32)
    sigmoid_gate = jax.nn.sigmoid(gate_pre)
    gate_act = gate_pre * sigmoid_gate
    hidden = (gate_act * up_proj).astype(jnp.bfloat16)
    out_grad = (row_weights.astype(jnp.float32)[:, None] * row_cotan.astype(jnp.float32)).astype(
        jnp.bfloat16
    )
    hidden_grad = jnp.dot(out_grad, weight_down.T, preferred_element_type=jnp.float32)
    gate_grad = (
        hidden_grad * up_proj * sigmoid_gate * (1.0 + gate_pre * (1.0 - sigmoid_gate))
    ).astype(jnp.bfloat16)
    up_grad = (hidden_grad * gate_act).astype(jnp.bfloat16)
    row_grads = jnp.dot(gate_grad, weight_gate.T, preferred_element_type=jnp.float32)
    row_grads = row_grads + jnp.dot(up_grad, weight_up.T, preferred_element_type=jnp.float32)
    return (row_grads.astype(jnp.bfloat16), (row_tokens, gate_grad, up_grad, hidden, out_grad))


def weight_terms(pieces):
    row_tokens, gate_grad, up_grad, hidden, out_grad = pieces
    grad_gate = jnp.dot(row_tokens.T, gate_grad, preferred_element_type=jnp.float32)
    grad_up = jnp.dot(row_tokens.T, up_grad, preferred_element_type=jnp.float32)
    grad_down = jnp.dot(hidden.T, out_grad, preferred_element_type=jnp.float32)
    return (grad_gate, grad_up, grad_down)


def expert_pass(weight_gate, weight_up, weight_down, row_tokens, row_cotan, row_weights):
    row_grads, pieces = forward_rows(
        weight_gate, weight_up, weight_down, row_tokens, row_cotan, row_weights
    )
    return (row_grads, weight_terms(pieces))


def shards(tokens, cotangent, routes, combine, hot_experts, extra_slots, w_gate, w_up, w_down):
    expert_count = lax.axis_size("expert")
    token_count, features = tokens.shape
    route_count = routes.shape[1]
    capacity = max(2, min(token_count * route_count * 7 // (8 * expert_count), token_count // 2))
    spare_slots = 2 * max(1, capacity // 6)
    expert_ids = routes.reshape(-1)
    assign_count = expert_ids.shape[0]
    assign_order = jnp.arange(assign_count, dtype=jnp.int32)
    earlier = (expert_ids[:, None] == expert_ids[None, :]) & (
        assign_order[None, :] < assign_order[:, None]
    )
    slot_rank = jnp.sum(earlier.astype(jnp.int32), axis=1)
    hot_match = expert_ids[:, None] == hot_experts[None, :]
    slot_limit = capacity + jnp.sum(jnp.where(hot_match, extra_slots[None, :], 0), axis=1)
    is_kept = slot_rank < slot_limit
    slot_count = capacity + spare_slots
    total_slots = expert_count * slot_count
    flat_slot = jnp.where(is_kept, expert_ids * slot_count + slot_rank, total_slots)
    slot_ids = jnp.arange(total_slots, dtype=jnp.int32)
    assign_onehot = slot_ids[:, None] == flat_slot[None, :]
    token_onehot = jnp.any(
        assign_onehot.reshape(total_slots, token_count, route_count), axis=2
    ).astype(jnp.bfloat16)
    both_rows = jnp.concatenate([tokens, cotangent], axis=1)
    filled = jnp.dot(token_onehot, both_rows, preferred_element_type=jnp.float32).astype(
        jnp.bfloat16
    )
    token_send = filled[:, :features].reshape(expert_count, slot_count, features)
    cotan_send = filled[:, features:].reshape(expert_count, slot_count, features)
    weight_flat = jnp.sum(
        jnp.where(assign_onehot, combine.reshape(-1).astype(jnp.float32)[None, :], 0.0), axis=1
    )
    weight_send = weight_flat.astype(jnp.bfloat16).reshape(expert_count, slot_count)
    token_recv, cotan_recv, weight_recv = (
        lax.all_to_all(token_send, "expert", split_axis=0, concat_axis=0, tiled=True),
        lax.all_to_all(cotan_send, "expert", split_axis=0, concat_axis=0, tiled=True),
        lax.all_to_all(weight_send, "expert", split_axis=0, concat_axis=0, tiled=True),
    )
    own_weights = (w_gate[0], w_up[0], w_down[0])
    all_rows, grad_terms = expert_pass(
        own_weights[0],
        own_weights[1],
        own_weights[2],
        token_recv.reshape(-1, features),
        cotan_recv.reshape(-1, features),
        weight_recv.reshape(-1),
    )
    grad_rows = all_rows.reshape(expert_count, slot_count, features)
    returned_rows = lax.all_to_all(grad_rows, "expert", split_axis=0, concat_axis=0, tiled=True)
    token_grads = jnp.dot(
        token_onehot.T,
        returned_rows.reshape(total_slots, features),
        preferred_element_type=jnp.float32,
    ).astype(jnp.bfloat16)
    grad_gate, grad_up = (
        lax.psum_scatter(grad_terms[0][None], "dp", scatter_dimension=1, tiled=True),
        lax.psum_scatter(grad_terms[1][None], "dp", scatter_dimension=1, tiled=True),
    )
    grad_down = lax.psum(grad_terms[2][None], "dp")
    return (
        token_grads,
        grad_gate.astype(jnp.bfloat16),
        grad_up.astype(jnp.bfloat16),
        grad_down.astype(jnp.bfloat16),
    )


MESH = pl.DeviceIdType.MESH
LANES = 128
TILE = 16
NT = (((1,), (1,)), ((), ()))
TN = (((0,), (0,)), ((), ()))


def slots_of(token_count, route_count, expert_count):
    capacity = max(2, min(token_count * route_count * 7 // (8 * expert_count), token_count // 2))
    return capacity, 2 * max(1, capacity // 6)


def dense_fits(sizes, token_count, features, route_count, hidden_size):
    capacity, spare = slots_of(token_count, route_count, sizes["expert"])
    return (
        route_count == sizes["expert"]
        and sizes["dp"] == 4
        and sizes["expert"] == 8
        and token_count == 2 * TILE
        and capacity == TILE
        and spare * 2 == 8
        and features % (8 * LANES) == 0
        and hidden_size % LANES == 0
    )


def dense_kernel(
    experts,
    tok_hbm,
    cot_hbm,
    routes_hbm,
    comb_hbm,
    hot_hbm,
    extra_hbm,
    wg_hbm,
    wu_hbm,
    wd_hbm,
    tg_ref,
    acc_gate,
    acc_up,
    acc_down,
    late_cols,
    late_og,
    late_h,
    late_gg,
    late_ug,
    tok_ref,
    cot_ref,
    routes_ref,
    comb_ref,
    hot_ref,
    extra_ref,
    all_tok,
    slab,
    wg,
    wu,
    wd,
    all_t,
    all_og,
    all_h,
    all_gg,
    all_ug,
    late_t,
    mid_t,
    mid_og,
    mid_h,
    mid_gg,
    mid_ug,
    row_out,
    pair_in,
    row_sum,
    z_in,
    in_sem,
    w_sem,
    send_sem,
    recv_sem,
    pair_recv,
    row_sem,
    z_recv,
    ready,
):
    levels = experts // 2
    hot_levels = levels // 2
    features = all_tok.shape[2]
    blocks = features // LANES
    half = blocks // 2
    weight_at, spill_at = blocks, blocks + 1
    bf16, f32 = jnp.bfloat16, jnp.float32

    d = lax.axis_index("dp")
    e = lax.axis_index("expert")
    z, c = e // 2, e % 2
    dx = d + 1 - 2 * (d % 2)
    dy = (d + 2) % 4
    dd = 3 - d
    pc = 1 - c
    upper_half = z // 2
    near, far = 2 * upper_half, 2 - 2 * upper_half
    hot = z < hot_levels
    low_x, low_y, low_z = d % 2 == 1, d // 2 == 1, z > 0
    up_x, up_y, up_z = d % 2 == 0, d // 2 == 0, z < levels - 1
    first_z, last_z = z == 0, z == levels - 1
    at_below, at_above = (d, jnp.maximum(e - 2, 0)), (d, jnp.minimum(e + 2, experts - 1))
    at_top, at_bottom = (d, (levels - 1) * 2 + c), (d, c)
    at_x, at_y, at_pair = (dx, e), (dy, e), (d, z * 2 + pc)
    at_diag = (dd, e)
    upper = z >= hot_levels
    low_d, up_d = jnp.logical_and(upper, d > dd), jnp.logical_and(upper, d < dd)

    def slot(dp, level, core):
        return (dp * 2 + core) * levels + level

    me = slot(d, z, c)
    input_copies = [
        pltpu.make_async_copy(h, v, in_sem.at[i])
        for i, (h, v) in enumerate(
            (
                (tok_hbm.at[pl.ds(TILE, TILE)], tok_ref),
                (cot_hbm, cot_ref),
                (routes_hbm, routes_ref),
                (comb_hbm, comb_ref),
                (hot_hbm, hot_ref),
                (extra_hbm, extra_ref),
                (tok_hbm.at[pl.ds(0, TILE)], all_tok.at[me]),
            )
        )
    ]
    own_tokens = input_copies.pop()
    weight_copies = [
        pltpu.make_async_copy(h.at[0], v, w_sem.at[i])
        for i, (h, v) in enumerate(((wg_hbm, wg), (wu_hbm, wu), (wd_hbm, wd)))
    ]

    barrier = pltpu.get_barrier_semaphore()

    def greet(peer):
        pl.semaphore_signal(barrier, inc=1, device_id=peer, device_id_type=MESH)

    pl.when(c == 0)(lambda: greet(at_pair))
    pl.when(up_x)(lambda: greet(at_x))
    pl.when(up_y)(lambda: greet(at_y))
    pl.when(up_z)(lambda: greet(at_above))
    pl.when(first_z)(lambda: greet(at_top))
    pl.when(up_d)(lambda: greet(at_diag))
    for copy in input_copies + [own_tokens] + weight_copies:
        copy.start()

    def piece(s, p, full):
        if p == 0:
            return all_tok.at[s]
        return slab.at[s] if full else slab.at[s, pl.ds(0, spill_at)]

    def either(full, visit):
        if full is True or full is False:
            visit(full)
            return
        pl.when(full)(lambda: visit(True))
        pl.when(jnp.logical_not(full))(lambda: visit(False))

    def remote(src, dst, send, recv, peer):
        return pltpu.make_async_remote_copy(
            src_ref=src,
            dst_ref=dst,
            send_sem=send,
            recv_sem=recv,
            device_id=peer,
            device_id_type=MESH,
        )

    def kind(p, f):
        return send_sem.at[0 if p == 0 else 1 if f else 2]

    def push(dp, level, p, full, peer, own=False):
        s = slot(dp, level, c)

        def go(f):
            dst = piece(s, p, f)
            src = tok_hbm.at[pl.ds(0, TILE)] if own and p == 0 else dst
            remote(src, dst, kind(p, f), recv_sem.at[p, dp * levels + level], peer).start()

        either(True if p == 0 else full, go)

    def to_x(dp, level, p, own=False):
        push(dp, level, p, True if own else hot, at_x, own)

    def to_y(dp, level, p, own=False):
        push(dp, level, p, True if own else hot, at_y, own)

    def to_below(p):
        push(d, z, p, True, at_below, True)

    def to_above(p):
        push(d, z, p, z + 1 < hot_levels, at_above, True)

    def to_top(p):
        push(d, z, p, False, at_top, True)

    def to_bottom(p):
        push(d, z, p, True, at_bottom, True)

    def pass_down(level, p):
        push(d, level, p, True, at_below)

    def pass_up(level, p):
        push(d, level, p, False, at_above)

    def to_diag(p):
        push(d, z, p, True, at_diag, True)

    def pass_across(p, peer):
        push(dd, z, p, True, peer)

    def to_pair(dp, level, p, bank, own=False):
        s = slot(dp, level, c)

        def go(f):
            dst = piece(s, p, f)
            src = tok_hbm.at[pl.ds(0, TILE)] if own and p == 0 else dst
            remote(src, dst, kind(p, f), pair_recv.at[p, bank], at_pair).start()

        either(True if p == 0 else hot, go)

    def to_other(dp, level, p, peer):
        part = piece(slot(dp, level, c), p, True)
        remote(part, part, kind(p, True), pair_recv.at[p, DD], peer).start()

    def arrived(dp, level, p, full):
        s = slot(dp, level, c)

        def go(f):
            dst = piece(s, p, f)
            at = recv_sem.at[p, dp * levels + level]
            remote(dst, dst, send_sem.at[0], at, at_x).wait_recv()

        either(True if p == 0 else full, go)

    lower_peers = (
        c + d % 2 + d // 2 + jnp.minimum(z, 1) + z // (levels - 1) + upper_half * (d // 2)
    )
    pl.when(lower_peers > 0)(lambda: pl.semaphore_wait(barrier, lower_peers))

    def tell(way, peer):
        pl.semaphore_signal(ready.at[way], inc=1, device_id=peer, device_id_type=MESH)

    pl.when(c == 1)(lambda: tell(5, at_pair))
    pl.when(low_x)(lambda: tell(0, at_x))
    pl.when(low_y)(lambda: tell(1, at_y))
    pl.when(low_z)(lambda: tell(3, at_below))
    pl.when(last_z)(lambda: tell(4, at_bottom))
    pl.when(low_d)(lambda: tell(2, at_diag))

    OWN, NEAR, FAR, DD = range(4)

    def to_lower(p):
        pl.when(low_z)(lambda: to_below(p))
        pl.when(last_z)(lambda: to_bottom(p))
        pl.when(low_x)(lambda: to_x(d, z, p, True))
        pl.when(low_y)(lambda: to_y(d, z, p, True))
        pl.when(low_d)(lambda: to_diag(p))

    to_lower(0)

    for copy in input_copies:
        copy.wait()
    names = -(-experts // TILE) * TILE
    expert_row = lax.broadcasted_iota(jnp.int32, (names, 2 * TILE), 0)
    token_lane = lax.broadcasted_iota(jnp.int32, (names, 2 * TILE), 1)
    routes = routes_ref[...]
    comb = comb_ref[...].astype(f32)
    weights = jnp.zeros((names, 2 * TILE), f32)
    for r in range(routes.shape[0]):
        weights = jnp.where(expert_row == routes[r : r + 1, :], comb[r : r + 1, :], weights)
    limit = jnp.full((names, 2 * TILE), TILE, jnp.int32)
    for j in range(hot_ref.shape[0]):
        limit = limit + jnp.where(expert_row == hot_ref[j], extra_ref[j], 0)
    weights = jnp.where(token_lane < limit, weights, 0.0).astype(bf16)
    unit_row = lax.broadcasted_iota(jnp.int32, (names, LANES), 0)
    unit_lane = lax.broadcasted_iota(jnp.int32, (names, LANES), 1)

    def turned(shift):
        unit = jnp.where(unit_lane == unit_row + shift, 1.0, 0.0).astype(bf16)
        return lax.dot_general(weights, unit, TN, preferred_element_type=f32)

    main_part, tail_part = turned(0), turned(LANES // 2)
    slab[me, weight_at] = (main_part[:TILE] + tail_part[TILE:]).astype(bf16)
    tok_tail = tok_ref[...].astype(f32)[:8]
    cot_tail = cot_ref[TILE:, :].astype(f32)[:8]
    tail_row = lax.broadcasted_iota(jnp.int32, (8, features), 0)
    spill = jnp.where(tail_row < 4, tok_tail, pltpu.roll(cot_tail, 4, 0))
    for j in range(blocks):
        slab[me, j] = cot_ref[:TILE, j * LANES : (j + 1) * LANES]
    for j in range(half):
        lo = spill[:, j * LANES : (j + 1) * LANES]
        hi = spill[:, (half + j) * LANES : (half + j + 1) * LANES]
        slab[me, spill_at + j] = jnp.concatenate([lo, hi], axis=0).astype(bf16)

    to_lower(1)
    pl.when(c == 0)(lambda: pl.semaphore_wait(ready.at[5], 1))
    for p in range(2):
        to_pair(d, z, p, OWN, True)

    def to_upper(way, up, act):
        @pl.when(up)
        def _():
            pl.semaphore_wait(ready.at[way], 1)
            for p in range(2):
                act(p)

    to_upper(3, up_z, to_above)
    to_upper(0, up_x, lambda p: to_x(d, z, p, True))
    to_upper(1, up_y, lambda p: to_y(d, z, p, True))
    to_upper(2, up_d, to_diag)
    own_tokens.wait()

    def at_distance(dist, visit):
        if dist == 0:
            visit(z, 0)
            return
        pl.when(z - dist >= 0)(lambda: visit(z - dist, -1))
        pl.when(z + dist < levels)(lambda: visit(z + dist, 1))

    def bank_of(level):
        return (level // 2 + upper_half) % 2

    def column(dist, p):
        def visit(level, side):
            arrived(d, level, p, True if side > 0 else hot)
            if dist == 1 and side > 0:
                pl.when(low_z)(lambda: pass_down(level, p))
            elif dist == 1:
                pl.when(up_z)(lambda: pass_up(level, p))
            to_x(d, level, p)
            to_y(d, level, p)
            to_pair(d, level, p, OWN)

        at_distance(dist, visit)

    def beside(dist, p):
        full = True if dist == 0 else hot
        keep = (hot, True, low_z, low_z)[dist]

        def visit(level, side, keep=keep):
            bank = NEAR + bank_of(level)
            if dist == 1 and side < 0:
                keep = z != 1
            arrived(dx, level, p, full)
            turn = jnp.logical_and((p + c) % 2 == 0, keep)
            pl.when(turn)(lambda: to_y(dx, level, p))
            if dist in (1, 2) and side > 0:
                both = jnp.logical_and(turn, z == dist - 1)
                pl.when(both)(lambda: to_other(dx, level, p, (dy, z * 2 + pc)))
            to_pair(dx, level, p, bank)
            arrived(dy, level, p, full)
            turn = jnp.logical_and((p + c) % 2 == 1, keep)
            pl.when(turn)(lambda: to_x(dy, level, p))
            if dist in (1, 2) and side > 0:
                both = jnp.logical_and(turn, z == dist - 1)
                pl.when(both)(lambda: to_other(dy, level, p, (dx, z * 2 + pc)))
            to_pair(dy, level, p, bank)

        at_distance(dist, visit)

    def across(dist, p):
        full = True if dist == 0 else hot

        def visit(level, side):
            arrived(dd, level, p, full)
            if dist == 0:
                pl.when(last_z)(lambda: pass_across(p, at_bottom))
                pl.when(z == 2)(lambda: pass_across(p, at_bottom))
                pl.when(first_z)(lambda: pass_across(p, at_above))
            if dist in (1, 2) and side > 0:
                pl.when(z != dist - 1)(lambda: to_pair(dd, level, p, DD))
            else:
                to_pair(dd, level, p, DD)

        at_distance(dist, visit)

    def from_pair(bank, at, count):
        region = pl.ds(at, count)
        remote(
            all_tok.at[region],
            all_tok.at[region],
            send_sem.at[0],
            pair_recv.at[0, bank],
            at_pair,
        ).wait_recv()

        def go(f):
            part = slab.at[region] if f else slab.at[region, pl.ds(0, spill_at)]
            remote(
                part, part, send_sem.at[1], pair_recv.at[1, bank], at_pair
            ).wait_recv()

        either(hot, go)

    def group(parts, store):
        each = sum(n for _, _, n in parts)
        main_rows, spill_rows = 2 * each * TILE, each * 8

        def slots_of_core(core):
            return [pl.ds(slot(dp, level, core), n) for dp, level, n in parts]

        lanes_a, lanes_b = slots_of_core(0), slots_of_core(1)

        def rows_of(at, lanes):
            return [slab[r, at] for r in lanes]

        def low8(lanes, at, cut):
            return jnp.concatenate(
                [v.astype(f32)[:, cut : cut + 8].reshape(-1, LANES) for v in rows_of(at, lanes)],
                axis=0,
            )

        def tail_of(lanes):
            return jnp.concatenate(
                [low8(lanes, spill_at + j, 0) for j in range(half)]
                + [low8(lanes, spill_at + j, 8) for j in range(half)],
                axis=1,
            )

        tail_a, tail_b = tail_of(lanes_a), tail_of(lanes_b)
        first = lax.broadcasted_iota(jnp.int32, (spill_rows, features), 0) % 8 < 4
        first_w = lax.broadcasted_iota(jnp.int32, (spill_rows, LANES), 0) % 8 < 4
        tok_rows = jnp.where(first, tail_a, pltpu.roll(tail_b, 4, 0))
        cot_rows = jnp.where(first, pltpu.roll(tail_a, spill_rows - 4, 0), tail_b)
        tok_rows = jnp.where(hot, tok_rows, 0.0)
        cot_rows = jnp.where(hot, cot_rows, 0.0)

        def main_of(at):
            return jnp.concatenate(
                [v.reshape(-1, LANES) for v in rows_of(at, lanes_a + lanes_b)], axis=0
            )

        w_main = main_of(weight_at).astype(f32)
        w_tail = jnp.where(
            first_w, low8(lanes_a, weight_at, 0), pltpu.roll(low8(lanes_b, weight_at, 0), 4, 0)
        )
        main_lane = lax.broadcasted_iota(jnp.int32, (main_rows, LANES), 1)
        tail_lane = lax.broadcasted_iota(jnp.int32, (spill_rows, LANES), 1)
        w = jnp.concatenate(
            [
                jnp.sum(jnp.where(main_lane == e, w_main, 0.0), axis=1, keepdims=True),
                jnp.sum(jnp.where(tail_lane == e + LANES // 2, w_tail, 0.0), axis=1, keepdims=True),
            ],
            axis=0,
        )
        t_ref, og_ref, h_ref, gg_ref, ug_ref, at = store
        rows = pl.ds(at, main_rows + spill_rows)
        t_ref[rows, :] = jnp.concatenate(
            [all_tok[r].reshape(-1, features) for r in lanes_a + lanes_b]
            + [tok_rows.astype(bf16)],
            axis=0,
        )
        cot = jnp.concatenate(
            [
                jnp.concatenate([main_of(j) for j in range(blocks)], axis=1).astype(f32),
                cot_rows,
            ],
            axis=0,
        )
        og_ref[rows, :] = (w * cot).astype(bf16)
        t = t_ref[rows, :]
        gate_pre = jnp.dot(t, wg[...], preferred_element_type=f32)
        up_proj = jnp.dot(t, wu[...], preferred_element_type=f32)
        hidden_grad = lax.dot_general(og_ref[rows, :], wd[...], NT, preferred_element_type=f32)
        sig = jax.nn.sigmoid(gate_pre)
        act = gate_pre * sig
        h_ref[rows, :] = (act * up_proj).astype(bf16)
        gg_ref[rows, :] = (hidden_grad * up_proj * sig * (1.0 + gate_pre * (1.0 - sig))).astype(
            bf16
        )
        ug_ref[rows, :] = (hidden_grad * act).astype(bf16)

    main_rows = experts * TILE
    group_rows = main_rows + levels * 8
    early = (all_t, all_og, all_h, all_gg, all_ug)
    mid = (mid_t, mid_og, mid_h, mid_gg, mid_ug)
    late = (late_t, late_og, late_h, late_gg, late_ug)

    for p in range(2):
        beside(0, p)
        column(1, p)
    to_upper(4, first_z, to_top)

    for p in range(2):
        for dist in (2, 3):
            column(dist, p)

    @pl.when(upper)
    def _():
        for p in range(2):
            across(0, p)

    from_pair(OWN, slot(d, 0, pc), levels)
    for copy in weight_copies:
        copy.wait()
    group([(d, 0, levels)], early + (0,))
    @pl.when(hot)
    def _():
        for p in range(2):
            across(0, p)

    own = pl.ds(0, group_rows)
    rg = lax.dot_general(all_gg[own, :], wg[...], NT, preferred_element_type=f32)
    rg = rg + lax.dot_general(all_ug[own, :], wu[...], NT, preferred_element_type=f32)
    lane_rows = main_rows // 2
    for j in range(blocks):
        cols = slice(j * LANES, (j + 1) * LANES)
        for core in range(2):
            row_out[core, :, j] = (
                rg[core * lane_rows : (core + 1) * lane_rows, cols]
                .reshape(levels, TILE, LANES)
                .astype(bf16)
            )
    for j in range(half):
        lo = rg[main_rows:, j * LANES : (j + 1) * LANES].reshape(levels, 8, LANES)
        hi = rg[main_rows:, (half + j) * LANES : (half + j + 1) * LANES].reshape(levels, 8, LANES)
        both = jnp.concatenate([lo, hi], axis=1).astype(bf16)
        for core in range(2):
            row_out[core, :, blocks + j] = both

    def row_copy(f):
        src, dst = row_out.at[pc], pair_in
        if not f:
            src, dst = row_out.at[pc, :, pl.ds(0, blocks)], pair_in.at[:, pl.ds(0, blocks)]
        return remote(src, dst, row_sem.at[0], row_sem.at[1], at_pair)

    either(hot, lambda f: row_copy(f).start())
    for p in range(2):
        beside(1, p)

    either(hot, lambda f: row_copy(f).wait_recv())
    for level in range(levels):
        row_sum[level, :blocks] = (
            row_out[c, level, :blocks].astype(f32) + pair_in[level, :blocks].astype(f32)
        ).astype(bf16)

    @pl.when(hot)
    def _():
        for level in range(levels):
            row_sum[level, blocks:] = (
                row_out[c, level, blocks:].astype(f32) + pair_in[level, blocks:].astype(f32)
            ).astype(bf16)

    def z_copy(level, sender, peer, f):
        src, dst = row_sum.at[level], z_in.at[sender]
        if not f:
            part = pl.ds(0, blocks)
            src, dst = row_sum.at[level, part], z_in.at[sender, part]
        return remote(src, dst, row_sem.at[0], z_recv.at[sender], peer)

    for level in range(levels):

        @pl.when(z != level)
        def _():
            either(hot, lambda f: z_copy(level, z, (d, level * 2 + c), f).start())

    @pl.when(low_z)
    def _():
        for dist in (2, 3):
            for p in range(2):
                beside(dist, p)

    from_pair(NEAR, 0, levels)
    group([(dx, near, 2), (dy, near, 2)], early + (group_rows,))

    @pl.when(first_z)
    def _():
        for dist in (2, 3):
            for p in range(2):
                beside(dist, p)

    def across_when(cond, *dists):
        @pl.when(cond)
        def _():
            for dist in dists:
                for p in range(2):
                    across(dist, p)

    share = features // 4
    cols = pl.ds(pl.multiple_of(d * share, LANES), share)
    t_cols = all_t[:, cols]
    acc_gate[...] = lax.dot_general(t_cols, all_gg[...], TN, preferred_element_type=f32)
    acc_up[...] = lax.dot_general(t_cols, all_ug[...], TN, preferred_element_type=f32)
    acc_down[...] = lax.dot_general(all_h[...], all_og[...], TN, preferred_element_type=f32)
    across_when(first_z, 3, 2)
    across_when(low_z, 1)
    across_when(last_z, 2, 3)
    from_pair(FAR, 0, levels)
    group([(dx, far, 2), (dy, far, 2)], mid + (0,))
    m_cols = mid_t[:, cols]
    acc_gate[...] += lax.dot_general(m_cols, mid_gg[...], TN, preferred_element_type=f32)
    acc_up[...] += lax.dot_general(m_cols, mid_ug[...], TN, preferred_element_type=f32)
    acc_down[...] += lax.dot_general(mid_h[...], mid_og[...], TN, preferred_element_type=f32)
    across_when(first_z, 1)
    across_when(jnp.logical_and(low_z, up_z), 2)
    from_pair(DD, 0, levels)
    group([(dd, 0, levels)], late + (0,))
    late_cols[...] = late_t[:, cols]
    z_in[z] = row_sum[z]

    for level in range(levels):

        @pl.when(z != level)
        def _():
            z_copy(level, level, at_pair, level < hot_levels).wait_recv()

    total = z_in[0, :blocks].astype(f32)
    spilled = z_in[0, blocks:].astype(f32)
    for level in range(1, levels):
        total = total + z_in[level, :blocks].astype(f32)
        if level < hot_levels:
            spilled = spilled + z_in[level, blocks:].astype(f32)
    kept_row = lax.broadcasted_iota(jnp.int32, (8, LANES), 0) < 4
    blank = jnp.zeros((8, LANES), f32)
    for j in range(blocks):
        tg_ref[:TILE, j * LANES : (j + 1) * LANES] = total[j].astype(bf16)
    for j in range(half):
        for at, rows in ((j, spilled[j][:8]), (half + j, spilled[j][8:])):
            rows = jnp.where(c == 0, rows, pltpu.roll(rows, 4, 0))
            tg_ref[TILE:, at * LANES : (at + 1) * LANES] = jnp.concatenate(
                [jnp.where(kept_row, rows, 0.0), blank], axis=0
            ).astype(bf16)

    def sent(sem, slots, width):
        part = slab.at[pl.ds(0, slots), pl.ds(0, width)]
        remote(part, part, sem, recv_sem.at[0, 0], at_x).wait_send()

    wide = slab.shape[1]
    relays = 4 * levels
    sides = 2 * levels
    for level, tokens_out, full_out, cold_out in (
        (0, relays + sides + 5, relays + sides + 4, 1),
        (1, relays + sides + 7, relays + sides + 5, 2),
        (2, relays + sides + 9, 6, relays + sides + 3),
        (3, relays + sides + 7, 6, relays + sides + 1),
    ):

        @pl.when(z == level)
        def _():
            if tokens_out <= slab.shape[0]:
                sent(send_sem.at[0], tokens_out, blocks)
            else:
                sent(send_sem.at[0], blocks * 3, tokens_out // 3)
            sent(send_sem.at[1], full_out, wide)
            sent(send_sem.at[2], cold_out, spill_at)

    either(hot, lambda f: sent(row_sem.at[0], 2 * levels - 1, blocks + half if f else blocks))


def finish_kernel(
    tg_ref,
    acc_gate,
    acc_up,
    acc_down,
    late_cols,
    late_og,
    late_h,
    late_gg,
    late_ug,
    tg_out,
    gg_out,
    gu_out,
    gd_out,
    gg_ref,
    gu_ref,
    gd_ref,
    sem,
):
    bf16, f32 = jnp.bfloat16, jnp.float32
    copies = [pltpu.make_async_copy(tg_ref, tg_out, sem.at[0])]
    copies[0].start()
    hidden_size = acc_gate.shape[1]

    def write(src, dst):
        copies.append(pltpu.make_async_copy(src, dst, sem.at[len(copies)]))
        copies[-1].start()

    for j in range(hidden_size // LANES):
        rows = pl.ds(j * LANES, LANES)
        term = lax.dot_general(late_h[:, rows], late_og[...], TN, preferred_element_type=f32)
        gd_ref[rows, :] = (acc_down[rows, :] + term).astype(bf16)
        write(gd_ref.at[rows], gd_out.at[0, rows])
    term = lax.dot_general(late_cols[...], late_gg[...], TN, preferred_element_type=f32)
    gg_ref[...] = (acc_gate[...] + term).astype(bf16)
    write(gg_ref, gg_out.at[0])
    term = lax.dot_general(late_cols[...], late_ug[...], TN, preferred_element_type=f32)
    gu_ref[...] = (acc_up[...] + term).astype(bf16)
    write(gu_ref, gu_out.at[0])
    for copy in copies:
        copy.wait()


def dense_shards(tokens, cotangent, routes, combine, hot_experts, extra_slots, w_gate, w_up, w_down):
    experts = lax.axis_size("expert")
    replicas = lax.axis_size("dp")
    token_count, features = tokens.shape
    hidden_size = w_gate.shape[2]
    blocks = features // LANES
    half = blocks // 2
    levels = experts // 2
    slots = replicas * experts
    share = features // replicas
    group_rows = experts * TILE + levels * 8
    early_rows, late_rows = 2 * group_rows, group_rows
    bf16, f32 = jnp.bfloat16, jnp.float32
    vmem = pl.BlockSpec(memory_space=pltpu.VMEM)
    hbm = pl.BlockSpec(memory_space=pltpu.HBM)
    dma = pltpu.SemaphoreType.DMA
    operands = [
        pltpu.with_memory_space_constraint(a, pltpu.HBM)
        for a in (
            tokens,
            cotangent,
            routes.T,
            combine.T,
            hot_experts,
            extra_slots,
            w_gate,
            w_up,
            w_down,
        )
    ]
    parts = pl.pallas_call(
        functools.partial(dense_kernel, experts),
        out_shape=(
            jax.ShapeDtypeStruct((token_count, features), bf16),
            jax.ShapeDtypeStruct((share, hidden_size), f32),
            jax.ShapeDtypeStruct((share, hidden_size), f32),
            jax.ShapeDtypeStruct((hidden_size, features), f32),
            jax.ShapeDtypeStruct((late_rows, share), bf16),
            jax.ShapeDtypeStruct((late_rows, features), bf16),
            jax.ShapeDtypeStruct((late_rows, hidden_size), bf16),
            jax.ShapeDtypeStruct((late_rows, hidden_size), bf16),
            jax.ShapeDtypeStruct((late_rows, hidden_size), bf16),
        ),
        in_specs=[hbm] * 9,
        out_specs=(vmem,) * 9,
        scratch_shapes=[
            pltpu.VMEM((TILE, features), bf16),
            pltpu.VMEM(cotangent.shape, bf16),
            pltpu.VMEM(routes.shape[::-1], jnp.int32),
            pltpu.VMEM(routes.shape[::-1], bf16),
            pltpu.SMEM(hot_experts.shape, jnp.int32),
            pltpu.SMEM(hot_experts.shape, jnp.int32),
            pltpu.VMEM((slots, TILE, features), bf16),
            pltpu.VMEM((slots, blocks + 1 + half, TILE, LANES), bf16),
            pltpu.VMEM((features, hidden_size), bf16),
            pltpu.VMEM((features, hidden_size), bf16),
            pltpu.VMEM((hidden_size, features), bf16),
            pltpu.VMEM((early_rows, features), bf16),
            pltpu.VMEM((early_rows, features), bf16),
            pltpu.VMEM((early_rows, hidden_size), bf16),
            pltpu.VMEM((early_rows, hidden_size), bf16),
            pltpu.VMEM((early_rows, hidden_size), bf16),
            pltpu.VMEM((late_rows, features), bf16),
            pltpu.VMEM((late_rows, features), bf16),
            pltpu.VMEM((late_rows, features), bf16),
            pltpu.VMEM((late_rows, hidden_size), bf16),
            pltpu.VMEM((late_rows, hidden_size), bf16),
            pltpu.VMEM((late_rows, hidden_size), bf16),
            pltpu.VMEM((2, levels, blocks + half, TILE, LANES), bf16),
            pltpu.VMEM((levels, blocks + half, TILE, LANES), bf16),
            pltpu.VMEM((levels, blocks + half, TILE, LANES), bf16),
            pltpu.VMEM((levels, blocks + half, TILE, LANES), bf16),
            dma((7,)),
            dma((3,)),
            dma((3,)),
            dma((2, slots // 2)),
            dma((2, 4)),
            dma((2,)),
            dma((levels,)),
            pltpu.SemaphoreType.REGULAR((6,)),
        ],
        compiler_params=pltpu.CompilerParams(
            collective_id=0, has_side_effects=True, vmem_limit_bytes=32 * 1024 * 1024
        ),
    )(*operands)
    return pl.pallas_call(
        finish_kernel,
        out_shape=(
            jax.ShapeDtypeStruct((token_count, features), bf16),
            jax.ShapeDtypeStruct((1, share, hidden_size), bf16),
            jax.ShapeDtypeStruct((1, share, hidden_size), bf16),
            jax.ShapeDtypeStruct((1, hidden_size, features), bf16),
        ),
        in_specs=[vmem] * len(parts),
        out_specs=(hbm,) * 4,
        scratch_shapes=[
            pltpu.VMEM((share, hidden_size), bf16),
            pltpu.VMEM((share, hidden_size), bf16),
            pltpu.VMEM((hidden_size, features), bf16),
            dma((3 + hidden_size // LANES,)),
        ],
        compiler_params=pltpu.CompilerParams(vmem_limit_bytes=16 * 1024 * 1024),
    )(*parts)


def solution(mesh):
    in_specs = (
        P(("dp", "expert"), None),
        P(("dp", "expert"), None),
        P(("dp", "expert"), None),
        P(("dp", "expert"), None),
        P(),
        P(),
        P("expert", None, None),
        P("expert", None, None),
        P("expert", None, None),
    )
    out_specs = (
        P(("dp", "expert"), None),
        P("expert", "dp", None),
        P("expert", "dp", None),
        P("expert", None, None),
    )

    def body(*args):
        token_count, features = args[0].shape
        if dense_fits(dict(mesh.shape), token_count, features, args[2].shape[1], args[6].shape[2]):
            return dense_shards(*args)
        return shards(*args)

    return jax.shard_map(body, mesh=mesh, in_specs=in_specs, out_specs=out_specs, check_vma=False)
```

```python
import functools

import jax
import jax.numpy as jnp
from jax import lax
from jax.experimental import pallas as pl
from jax.experimental.pallas import tpu as pltpu
from jax.sharding import PartitionSpec as P


def forward_rows(weight_gate, weight_up, weight_down, row_tokens, row_cotan, row_weights):
    gate_pre = jnp.dot(row_tokens, weight_gate, preferred_element_type=jnp.float32)
    up_proj = jnp.dot(row_tokens, weight_up, preferred_element_type=jnp.float32)
    sigmoid_gate = jax.nn.sigmoid(gate_pre)
    gate_act = gate_pre * sigmoid_gate
    hidden = (gate_act * up_proj).astype(jnp.bfloat16)
    out_grad = (row_weights.astype(jnp.float32)[:, None] * row_cotan.astype(jnp.float32)).astype(
        jnp.bfloat16
    )
    hidden_grad = jnp.dot(out_grad, weight_down.T, preferred_element_type=jnp.float32)
    gate_grad = (
        hidden_grad * up_proj * sigmoid_gate * (1.0 + gate_pre * (1.0 - sigmoid_gate))
    ).astype(jnp.bfloat16)
    up_grad = (hidden_grad * gate_act).astype(jnp.bfloat16)
    row_grads = jnp.dot(gate_grad, weight_gate.T, preferred_element_type=jnp.float32)
    row_grads = row_grads + jnp.dot(up_grad, weight_up.T, preferred_element_type=jnp.float32)
    return (row_grads.astype(jnp.bfloat16), (row_tokens, gate_grad, up_grad, hidden, out_grad))


def weight_terms(pieces):
    row_tokens, gate_grad, up_grad, hidden, out_grad = pieces
    grad_gate = jnp.dot(row_tokens.T, gate_grad, preferred_element_type=jnp.float32)
    grad_up = jnp.dot(row_tokens.T, up_grad, preferred_element_type=jnp.float32)
    grad_down = jnp.dot(hidden.T, out_grad, preferred_element_type=jnp.float32)
    return (grad_gate, grad_up, grad_down)


def expert_pass(weight_gate, weight_up, weight_down, row_tokens, row_cotan, row_weights):
    row_grads, pieces = forward_rows(
        weight_gate, weight_up, weight_down, row_tokens, row_cotan, row_weights
    )
    return (row_grads, weight_terms(pieces))


def shards(tokens, cotangent, routes, combine, hot_experts, extra_slots, w_gate, w_up, w_down):
    expert_count = lax.axis_size("expert")
    token_count, features = tokens.shape
    route_count = routes.shape[1]
    capacity = max(2, min(token_count * route_count * 7 // (8 * expert_count), token_count // 2))
    spare_slots = 2 * max(1, capacity // 6)
    expert_ids = routes.reshape(-1)
    assign_count = expert_ids.shape[0]
    assign_order = jnp.arange(assign_count, dtype=jnp.int32)
    earlier = (expert_ids[:, None] == expert_ids[None, :]) & (
        assign_order[None, :] < assign_order[:, None]
    )
    slot_rank = jnp.sum(earlier.astype(jnp.int32), axis=1)
    hot_match = expert_ids[:, None] == hot_experts[None, :]
    slot_limit = capacity + jnp.sum(jnp.where(hot_match, extra_slots[None, :], 0), axis=1)
    is_kept = slot_rank < slot_limit
    slot_count = capacity + spare_slots
    total_slots = expert_count * slot_count
    flat_slot = jnp.where(is_kept, expert_ids * slot_count + slot_rank, total_slots)
    slot_ids = jnp.arange(total_slots, dtype=jnp.int32)
    assign_onehot = slot_ids[:, None] == flat_slot[None, :]
    token_onehot = jnp.any(
        assign_onehot.reshape(total_slots, token_count, route_count), axis=2
    ).astype(jnp.bfloat16)
    both_rows = jnp.concatenate([tokens, cotangent], axis=1)
    filled = jnp.dot(token_onehot, both_rows, preferred_element_type=jnp.float32).astype(
        jnp.bfloat16
    )
    token_send = filled[:, :features].reshape(expert_count, slot_count, features)
    cotan_send = filled[:, features:].reshape(expert_count, slot_count, features)
    weight_flat = jnp.sum(
        jnp.where(assign_onehot, combine.reshape(-1).astype(jnp.float32)[None, :], 0.0), axis=1
    )
    weight_send = weight_flat.astype(jnp.bfloat16).reshape(expert_count, slot_count)
    token_recv, cotan_recv, weight_recv = (
        lax.all_to_all(token_send, "expert", split_axis=0, concat_axis=0, tiled=True),
        lax.all_to_all(cotan_send, "expert", split_axis=0, concat_axis=0, tiled=True),
        lax.all_to_all(weight_send, "expert", split_axis=0, concat_axis=0, tiled=True),
    )
    own_weights = (w_gate[0], w_up[0], w_down[0])
    all_rows, grad_terms = expert_pass(
        own_weights[0],
        own_weights[1],
        own_weights[2],
        token_recv.reshape(-1, features),
        cotan_recv.reshape(-1, features),
        weight_recv.reshape(-1),
    )
    grad_rows = all_rows.reshape(expert_count, slot_count, features)
    returned_rows = lax.all_to_all(grad_rows, "expert", split_axis=0, concat_axis=0, tiled=True)
    token_grads = jnp.dot(
        token_onehot.T,
        returned_rows.reshape(total_slots, features),
        preferred_element_type=jnp.float32,
    ).astype(jnp.bfloat16)
    grad_gate, grad_up = (
        lax.psum_scatter(grad_terms[0][None], "dp", scatter_dimension=1, tiled=True),
        lax.psum_scatter(grad_terms[1][None], "dp", scatter_dimension=1, tiled=True),
    )
    grad_down = lax.psum(grad_terms[2][None], "dp")
    return (
        token_grads,
        grad_gate.astype(jnp.bfloat16),
        grad_up.astype(jnp.bfloat16),
        grad_down.astype(jnp.bfloat16),
    )


MESH = pl.DeviceIdType.MESH
LANES = 128
TILE = 16
NT = (((1,), (1,)), ((), ()))
TN = (((0,), (0,)), ((), ()))


def slots_of(token_count, route_count, expert_count):
    capacity = max(2, min(token_count * route_count * 7 // (8 * expert_count), token_count // 2))
    return capacity, 2 * max(1, capacity // 6)


def dense_fits(sizes, token_count, features, route_count, hidden_size):
    capacity, spare = slots_of(token_count, route_count, sizes["expert"])
    return (
        route_count == sizes["expert"]
        and sizes["dp"] == 4
        and sizes["expert"] == 8
        and token_count == 2 * TILE
        and capacity == TILE
        and spare * 2 == 8
        and features % (8 * LANES) == 0
        and hidden_size % LANES == 0
    )


def dense_kernel(
    experts,
    tok_hbm,
    cot_hbm,
    routes_hbm,
    comb_hbm,
    hot_hbm,
    extra_hbm,
    wg_hbm,
    wu_hbm,
    wd_hbm,
    tg_ref,
    acc_gate,
    acc_up,
    acc_down,
    late_cols,
    late_og,
    late_h,
    late_gg,
    late_ug,
    tok_ref,
    cot_ref,
    routes_ref,
    comb_ref,
    hot_ref,
    extra_ref,
    all_tok,
    slab,
    wg,
    wu,
    wd,
    all_t,
    all_og,
    all_h,
    all_gg,
    all_ug,
    late_t,
    mid_t,
    mid_og,
    mid_h,
    mid_gg,
    mid_ug,
    row_out,
    pair_in,
    row_sum,
    z_in,
    in_sem,
    w_sem,
    send_sem,
    recv_sem,
    pair_recv,
    row_sem,
    z_recv,
    ready,
):
    levels = experts // 2
    hot_levels = levels // 2
    features = all_tok.shape[2]
    blocks = features // LANES
    half = blocks // 2
    weight_at, spill_at = blocks, blocks + 1
    bf16, f32 = jnp.bfloat16, jnp.float32

    d = lax.axis_index("dp")
    e = lax.axis_index("expert")
    z, c = e // 2, e % 2
    dx = d + 1 - 2 * (d % 2)
    dy = (d + 2) % 4
    dd = 3 - d
    pc = 1 - c
    upper_half = z // 2
    near, far = 2 * upper_half, 2 - 2 * upper_half
    hot = z < hot_levels
    low_x, low_y, low_z = d % 2 == 1, d // 2 == 1, z > 0
    up_x, up_y, up_z = d % 2 == 0, d // 2 == 0, z < levels - 1
    first_z, last_z = z == 0, z == levels - 1
    at_below, at_above = (d, jnp.maximum(e - 2, 0)), (d, jnp.minimum(e + 2, experts - 1))
    at_top, at_bottom = (d, (levels - 1) * 2 + c), (d, c)
    at_x, at_y, at_pair = (dx, e), (dy, e), (d, z * 2 + pc)
    at_diag = (dd, e)
    upper = z >= hot_levels
    low_d, up_d = jnp.logical_and(upper, d > dd), jnp.logical_and(upper, d < dd)

    def slot(dp, level, core):
        return (dp * 2 + core) * levels + level

    me = slot(d, z, c)
    input_copies = [
        pltpu.make_async_copy(h, v, in_sem.at[i])
        for i, (h, v) in enumerate(
            (
                (tok_hbm.at[pl.ds(TILE, TILE)], tok_ref),
                (cot_hbm, cot_ref),
                (routes_hbm, routes_ref),
                (comb_hbm, comb_ref),
                (hot_hbm, hot_ref),
                (extra_hbm, extra_ref),
                (tok_hbm.at[pl.ds(0, TILE)], all_tok.at[me]),
            )
        )
    ]
    own_tokens = input_copies.pop()
    weight_copies = [
        pltpu.make_async_copy(h.at[0], v, w_sem.at[i])
        for i, (h, v) in enumerate(((wg_hbm, wg), (wu_hbm, wu), (wd_hbm, wd)))
    ]

    barrier = pltpu.get_barrier_semaphore()

    def greet(peer):
        pl.semaphore_signal(barrier, inc=1, device_id=peer, device_id_type=MESH)

    pl.when(c == 0)(lambda: greet(at_pair))
    pl.when(up_x)(lambda: greet(at_x))
    pl.when(up_y)(lambda: greet(at_y))
    pl.when(up_z)(lambda: greet(at_above))
    pl.when(first_z)(lambda: greet(at_top))
    pl.when(up_d)(lambda: greet(at_diag))
    for copy in input_copies + [own_tokens] + weight_copies:
        copy.start()

    def piece(s, p, full):
        if p == 0:
            return all_tok.at[s]
        return slab.at[s] if full else slab.at[s, pl.ds(0, spill_at)]

    def either(full, visit):
        if full is True or full is False:
            visit(full)
            return
        pl.when(full)(lambda: visit(True))
        pl.when(jnp.logical_not(full))(lambda: visit(False))

    def remote(src, dst, send, recv, peer):
        return pltpu.make_async_remote_copy(
            src_ref=src,
            dst_ref=dst,
            send_sem=send,
            recv_sem=recv,
            device_id=peer,
            device_id_type=MESH,
        )

    def kind(p, f):
        return send_sem.at[0 if p == 0 else 1 if f else 2]

    def push(dp, level, p, full, peer, own=False):
        s = slot(dp, level, c)

        def go(f):
            dst = piece(s, p, f)
            src = tok_hbm.at[pl.ds(0, TILE)] if own and p == 0 else dst
            remote(src, dst, kind(p, f), recv_sem.at[p, dp * levels + level], peer).start()

        either(True if p == 0 else full, go)

    def to_x(dp, level, p, own=False):
        push(dp, level, p, True if own else hot, at_x, own)

    def to_y(dp, level, p, own=False):
        push(dp, level, p, True if own else hot, at_y, own)

    def to_below(p):
        push(d, z, p, True, at_below, True)

    def to_above(p):
        push(d, z, p, z + 1 < hot_levels, at_above, True)

    def to_top(p):
        push(d, z, p, False, at_top, True)

    def to_bottom(p):
        push(d, z, p, True, at_bottom, True)

    def pass_down(level, p):
        push(d, level, p, True, at_below)

    def pass_up(level, p):
        push(d, level, p, False, at_above)

    def to_diag(p):
        push(d, z, p, True, at_diag, True)

    def pass_across(p, peer):
        push(dd, z, p, True, peer)

    def to_pair(dp, level, p, bank, own=False):
        s = slot(dp, level, c)

        def go(f):
            dst = piece(s, p, f)
            src = tok_hbm.at[pl.ds(0, TILE)] if own and p == 0 else dst
            remote(src, dst, kind(p, f), pair_recv.at[bank], at_pair).start()

        either(True if p == 0 else hot, go)

    def to_other(dp, level, p, peer):
        part = piece(slot(dp, level, c), p, True)
        remote(part, part, kind(p, True), pair_recv.at[DD], peer).start()

    def arrived(dp, level, p, full):
        s = slot(dp, level, c)

        def go(f):
            dst = piece(s, p, f)
            at = recv_sem.at[p, dp * levels + level]
            remote(dst, dst, send_sem.at[0], at, at_x).wait_recv()

        either(True if p == 0 else full, go)

    lower_peers = (
        c + d % 2 + d // 2 + jnp.minimum(z, 1) + z // (levels - 1) + upper_half * (d // 2)
    )
    pl.when(lower_peers > 0)(lambda: pl.semaphore_wait(barrier, lower_peers))

    def tell(way, peer):
        pl.semaphore_signal(ready.at[way], inc=1, device_id=peer, device_id_type=MESH)

    pl.when(c == 1)(lambda: tell(5, at_pair))
    pl.when(low_x)(lambda: tell(0, at_x))
    pl.when(low_y)(lambda: tell(1, at_y))
    pl.when(low_z)(lambda: tell(3, at_below))
    pl.when(last_z)(lambda: tell(4, at_bottom))
    pl.when(low_d)(lambda: tell(2, at_diag))

    OWN, NEAR, FAR, DD = range(4)

    def to_lower(p):
        pl.when(low_z)(lambda: to_below(p))
        pl.when(last_z)(lambda: to_bottom(p))
        pl.when(low_x)(lambda: to_x(d, z, p, True))
        pl.when(low_y)(lambda: to_y(d, z, p, True))
        pl.when(low_d)(lambda: to_diag(p))

    to_lower(0)

    for copy in input_copies:
        copy.wait()
    names = -(-experts // TILE) * TILE
    expert_row = lax.broadcasted_iota(jnp.int32, (names, 2 * TILE), 0)
    token_lane = lax.broadcasted_iota(jnp.int32, (names, 2 * TILE), 1)
    routes = routes_ref[...]
    comb = comb_ref[...].astype(f32)
    weights = jnp.zeros((names, 2 * TILE), f32)
    for r in range(routes.shape[0]):
        weights = jnp.where(expert_row == routes[r : r + 1, :], comb[r : r + 1, :], weights)
    limit = jnp.full((names, 2 * TILE), TILE, jnp.int32)
    for j in range(hot_ref.shape[0]):
        limit = limit + jnp.where(expert_row == hot_ref[j], extra_ref[j], 0)
    weights = jnp.where(token_lane < limit, weights, 0.0).astype(bf16)
    unit_row = lax.broadcasted_iota(jnp.int32, (names, LANES), 0)
    unit_lane = lax.broadcasted_iota(jnp.int32, (names, LANES), 1)

    def turned(shift):
        unit = jnp.where(unit_lane == unit_row + shift, 1.0, 0.0).astype(bf16)
        return lax.dot_general(weights, unit, TN, preferred_element_type=f32)

    main_part, tail_part = turned(0), turned(LANES // 2)
    slab[me, weight_at] = (main_part[:TILE] + tail_part[TILE:]).astype(bf16)
    tok_tail = tok_ref[...].astype(f32)[:8]
    cot_tail = cot_ref[TILE:, :].astype(f32)[:8]
    tail_row = lax.broadcasted_iota(jnp.int32, (8, features), 0)
    spill = jnp.where(tail_row < 4, tok_tail, pltpu.roll(cot_tail, 4, 0))
    for j in range(blocks):
        slab[me, j] = cot_ref[:TILE, j * LANES : (j + 1) * LANES]
    for j in range(half):
        lo = spill[:, j * LANES : (j + 1) * LANES]
        hi = spill[:, (half + j) * LANES : (half + j + 1) * LANES]
        slab[me, spill_at + j] = jnp.concatenate([lo, hi], axis=0).astype(bf16)

    to_lower(1)
    pl.when(c == 0)(lambda: pl.semaphore_wait(ready.at[5], 1))
    for p in range(2):
        to_pair(d, z, p, OWN, True)

    def to_upper(way, up, act):
        @pl.when(up)
        def _():
            pl.semaphore_wait(ready.at[way], 1)
            for p in range(2):
                act(p)

    to_upper(3, up_z, to_above)
    to_upper(0, up_x, lambda p: to_x(d, z, p, True))
    to_upper(1, up_y, lambda p: to_y(d, z, p, True))
    to_upper(2, up_d, to_diag)
    own_tokens.wait()

    def at_distance(dist, visit):
        if dist == 0:
            visit(z, 0)
            return
        pl.when(z - dist >= 0)(lambda: visit(z - dist, -1))
        pl.when(z + dist < levels)(lambda: visit(z + dist, 1))

    def bank_of(level):
        return (level // 2 + upper_half) % 2

    def column(dist, p):
        def visit(level, side):
            arrived(d, level, p, True if side > 0 else hot)
            if dist == 1 and side > 0:
                pl.when(low_z)(lambda: pass_down(level, p))
            elif dist == 1:
                pl.when(up_z)(lambda: pass_up(level, p))
            to_x(d, level, p)
            to_y(d, level, p)
            to_pair(d, level, p, OWN)

        at_distance(dist, visit)

    def beside(dist, p):
        full = True if dist == 0 else hot
        keep = (hot, True, low_z, low_z)[dist]

        def visit(level, side, keep=keep):
            bank = NEAR + bank_of(level)
            if dist == 1 and side < 0:
                keep = z != 1
            arrived(dx, level, p, full)
            turn = jnp.logical_and((p + c) % 2 == 0, keep)
            pl.when(turn)(lambda: to_y(dx, level, p))
            if dist in (1, 2) and side > 0:
                both = jnp.logical_and(turn, z == dist - 1)
                pl.when(both)(lambda: to_other(dx, level, p, (dy, z * 2 + pc)))
            to_pair(dx, level, p, bank)
            arrived(dy, level, p, full)
            turn = jnp.logical_and((p + c) % 2 == 1, keep)
            pl.when(turn)(lambda: to_x(dy, level, p))
            if dist in (1, 2) and side > 0:
                both = jnp.logical_and(turn, z == dist - 1)
                pl.when(both)(lambda: to_other(dy, level, p, (dx, z * 2 + pc)))
            to_pair(dy, level, p, bank)

        at_distance(dist, visit)

    def across(dist, p):
        full = True if dist == 0 else hot

        def visit(level, side):
            arrived(dd, level, p, full)
            if dist == 0:
                pl.when(last_z)(lambda: pass_across(p, at_bottom))
                pl.when(z == 2)(lambda: pass_across(p, at_bottom))
                pl.when(first_z)(lambda: pass_across(p, at_above))
            if dist in (1, 2) and side > 0:
                pl.when(z != dist - 1)(lambda: to_pair(dd, level, p, DD))
            else:
                to_pair(dd, level, p, DD)

        at_distance(dist, visit)

    def from_pair(bank, at, count):
        def go(f):
            tiles = blocks + (slab.shape[1] if f else spill_at)
            part = slab.at[pl.ds(0, tiles), pl.ds(0, count)]
            remote(part, part, send_sem.at[0], pair_recv.at[bank], at_pair).wait_recv()

        either(hot, go)

    def group(parts, store):
        each = sum(n for _, _, n in parts)
        main_rows, spill_rows = 2 * each * TILE, each * 8

        def slots_of_core(core):
            return [pl.ds(slot(dp, level, core), n) for dp, level, n in parts]

        lanes_a, lanes_b = slots_of_core(0), slots_of_core(1)

        def rows_of(at, lanes):
            return [slab[r, at] for r in lanes]

        def low8(lanes, at, cut):
            return jnp.concatenate(
                [v.astype(f32)[:, cut : cut + 8].reshape(-1, LANES) for v in rows_of(at, lanes)],
                axis=0,
            )

        def tail_of(lanes):
            return jnp.concatenate(
                [low8(lanes, spill_at + j, 0) for j in range(half)]
                + [low8(lanes, spill_at + j, 8) for j in range(half)],
                axis=1,
            )

        tail_a, tail_b = tail_of(lanes_a), tail_of(lanes_b)
        first = lax.broadcasted_iota(jnp.int32, (spill_rows, features), 0) % 8 < 4
        first_w = lax.broadcasted_iota(jnp.int32, (spill_rows, LANES), 0) % 8 < 4
        tok_rows = jnp.where(first, tail_a, pltpu.roll(tail_b, 4, 0))
        cot_rows = jnp.where(first, pltpu.roll(tail_a, spill_rows - 4, 0), tail_b)
        tok_rows = jnp.where(hot, tok_rows, 0.0)
        cot_rows = jnp.where(hot, cot_rows, 0.0)

        def main_of(at):
            return jnp.concatenate(
                [v.reshape(-1, LANES) for v in rows_of(at, lanes_a + lanes_b)], axis=0
            )

        w_main = main_of(weight_at).astype(f32)
        w_tail = jnp.where(
            first_w, low8(lanes_a, weight_at, 0), pltpu.roll(low8(lanes_b, weight_at, 0), 4, 0)
        )
        main_lane = lax.broadcasted_iota(jnp.int32, (main_rows, LANES), 1)
        tail_lane = lax.broadcasted_iota(jnp.int32, (spill_rows, LANES), 1)
        w = jnp.concatenate(
            [
                jnp.sum(jnp.where(main_lane == e, w_main, 0.0), axis=1, keepdims=True),
                jnp.sum(jnp.where(tail_lane == e + LANES // 2, w_tail, 0.0), axis=1, keepdims=True),
            ],
            axis=0,
        )
        t_ref, og_ref, h_ref, gg_ref, ug_ref, at = store
        rows = pl.ds(at, main_rows + spill_rows)
        t_ref[rows, :] = jnp.concatenate(
            [all_tok[r].reshape(-1, features) for r in lanes_a + lanes_b]
            + [tok_rows.astype(bf16)],
            axis=0,
        )
        cot = jnp.concatenate(
            [
                jnp.concatenate([main_of(j) for j in range(blocks)], axis=1).astype(f32),
                cot_rows,
            ],
            axis=0,
        )
        og_ref[rows, :] = (w * cot).astype(bf16)
        t = t_ref[rows, :]
        gate_pre = jnp.dot(t, wg[...], preferred_element_type=f32)
        up_proj = jnp.dot(t, wu[...], preferred_element_type=f32)
        hidden_grad = lax.dot_general(og_ref[rows, :], wd[...], NT, preferred_element_type=f32)
        sig = jax.nn.sigmoid(gate_pre)
        act = gate_pre * sig
        h_ref[rows, :] = (act * up_proj).astype(bf16)
        gg_ref[rows, :] = (hidden_grad * up_proj * sig * (1.0 + gate_pre * (1.0 - sig))).astype(
            bf16
        )
        ug_ref[rows, :] = (hidden_grad * act).astype(bf16)

    main_rows = experts * TILE
    group_rows = main_rows + levels * 8
    early = (all_t, all_og, all_h, all_gg, all_ug)
    mid = (mid_t, mid_og, mid_h, mid_gg, mid_ug)
    late = (late_t, late_og, late_h, late_gg, late_ug)

    for p in range(2):
        beside(0, p)
        column(1, p)
    to_upper(4, first_z, to_top)

    for p in range(2):
        for dist in (2, 3):
            column(dist, p)

    @pl.when(upper)
    def _():
        for p in range(2):
            across(0, p)

    from_pair(OWN, slot(d, 0, pc), levels)
    for copy in weight_copies:
        copy.wait()
    group([(d, 0, levels)], early + (0,))
    @pl.when(hot)
    def _():
        for p in range(2):
            across(0, p)

    own = pl.ds(0, group_rows)
    rg = lax.dot_general(all_gg[own, :], wg[...], NT, preferred_element_type=f32)
    rg = rg + lax.dot_general(all_ug[own, :], wu[...], NT, preferred_element_type=f32)
    lane_rows = main_rows // 2
    for j in range(blocks):
        cols = slice(j * LANES, (j + 1) * LANES)
        for core in range(2):
            row_out[core, :, j] = (
                rg[core * lane_rows : (core + 1) * lane_rows, cols]
                .reshape(levels, TILE, LANES)
                .astype(bf16)
            )
    for j in range(half):
        lo = rg[main_rows:, j * LANES : (j + 1) * LANES].reshape(levels, 8, LANES)
        hi = rg[main_rows:, (half + j) * LANES : (half + j + 1) * LANES].reshape(levels, 8, LANES)
        both = jnp.concatenate([lo, hi], axis=1).astype(bf16)
        for core in range(2):
            row_out[core, :, blocks + j] = both

    def row_copy(f):
        src, dst = row_out.at[pc], pair_in
        if not f:
            src, dst = row_out.at[pc, :, pl.ds(0, blocks)], pair_in.at[:, pl.ds(0, blocks)]
        return remote(src, dst, row_sem.at[0], row_sem.at[1], at_pair)

    either(hot, lambda f: row_copy(f).start())
    for p in range(2):
        beside(1, p)

    either(hot, lambda f: row_copy(f).wait_recv())
    for level in range(levels):
        row_sum[level, :blocks] = (
            row_out[c, level, :blocks].astype(f32) + pair_in[level, :blocks].astype(f32)
        ).astype(bf16)

    @pl.when(hot)
    def _():
        for level in range(levels):
            row_sum[level, blocks:] = (
                row_out[c, level, blocks:].astype(f32) + pair_in[level, blocks:].astype(f32)
            ).astype(bf16)

    def z_copy(level, sender, peer, f):
        src, dst = row_sum.at[level], z_in.at[sender]
        if not f:
            part = pl.ds(0, blocks)
            src, dst = row_sum.at[level, part], z_in.at[sender, part]
        return remote(src, dst, row_sem.at[0], z_recv.at[0], peer)

    for level in range(levels):

        @pl.when(z != level)
        def _():
            either(hot, lambda f: z_copy(level, z, (d, level * 2 + c), f).start())

    @pl.when(low_z)
    def _():
        for dist in (2, 3):
            for p in range(2):
                beside(dist, p)

    from_pair(NEAR, 0, levels)
    group([(dx, near, 2), (dy, near, 2)], early + (group_rows,))

    @pl.when(first_z)
    def _():
        for dist in (2, 3):
            for p in range(2):
                beside(dist, p)

    def across_when(cond, *dists):
        @pl.when(cond)
        def _():
            for dist in dists:
                for p in range(2):
                    across(dist, p)

    share = features // 4
    cols = pl.ds(pl.multiple_of(d * share, LANES), share)
    t_cols = all_t[:, cols]
    acc_gate[...] = lax.dot_general(t_cols, all_gg[...], TN, preferred_element_type=f32)
    acc_up[...] = lax.dot_general(t_cols, all_ug[...], TN, preferred_element_type=f32)
    acc_down[...] = lax.dot_general(all_h[...], all_og[...], TN, preferred_element_type=f32)
    across_when(first_z, 3, 2)
    across_when(low_z, 1)
    across_when(last_z, 2, 3)
    from_pair(FAR, 0, levels)
    group([(dx, far, 2), (dy, far, 2)], mid + (0,))
    m_cols = mid_t[:, cols]
    acc_gate[...] += lax.dot_general(m_cols, mid_gg[...], TN, preferred_element_type=f32)
    acc_up[...] += lax.dot_general(m_cols, mid_ug[...], TN, preferred_element_type=f32)
    acc_down[...] += lax.dot_general(mid_h[...], mid_og[...], TN, preferred_element_type=f32)
    across_when(first_z, 1)
    across_when(jnp.logical_and(low_z, up_z), 2)
    from_pair(DD, 0, levels)
    group([(dd, 0, levels)], late + (0,))
    late_cols[...] = late_t[:, cols]
    z_in[z] = row_sum[z]

    def returned(low, high):
        count = (low * (blocks + half) + high * blocks) // half
        part = slab.at[pl.ds(0, count), pl.ds(0, half)]
        remote(part, part, send_sem.at[0], z_recv.at[0], at_pair).wait_recv()

    pl.when(hot)(lambda: returned(hot_levels - 1, levels - hot_levels))
    pl.when(upper)(lambda: returned(hot_levels, levels - hot_levels - 1))

    total = z_in[0, :blocks].astype(f32)
    spilled = z_in[0, blocks:].astype(f32)
    for level in range(1, levels):
        total = total + z_in[level, :blocks].astype(f32)
        if level < hot_levels:
            spilled = spilled + z_in[level, blocks:].astype(f32)
    kept_row = lax.broadcasted_iota(jnp.int32, (8, LANES), 0) < 4
    blank = jnp.zeros((8, LANES), f32)
    for j in range(blocks):
        tg_ref[:TILE, j * LANES : (j + 1) * LANES] = total[j].astype(bf16)
    for j in range(half):
        for at, rows in ((j, spilled[j][:8]), (half + j, spilled[j][8:])):
            rows = jnp.where(c == 0, rows, pltpu.roll(rows, 4, 0))
            tg_ref[TILE:, at * LANES : (at + 1) * LANES] = jnp.concatenate(
                [jnp.where(kept_row, rows, 0.0), blank], axis=0
            ).astype(bf16)

    def sent(sem, slots, width):
        part = slab.at[pl.ds(0, slots), pl.ds(0, width)]
        remote(part, part, sem, recv_sem.at[0, 0], at_x).wait_send()

    wide = slab.shape[1]
    relays = 4 * levels
    sides = 2 * levels
    for level, tokens_out, full_out, cold_out in (
        (0, relays + sides + 5, relays + sides + 4, 1),
        (1, relays + sides + 7, relays + sides + 5, 2),
        (2, relays + sides + 9, 6, relays + sides + 3),
        (3, relays + sides + 7, 6, relays + sides + 1),
    ):

        @pl.when(z == level)
        def _():
            if tokens_out <= slab.shape[0]:
                sent(send_sem.at[0], tokens_out, blocks)
            else:
                sent(send_sem.at[0], blocks * 3, tokens_out // 3)
            sent(send_sem.at[1], full_out, wide)
            sent(send_sem.at[2], cold_out, spill_at)

    either(hot, lambda f: sent(row_sem.at[0], 2 * levels - 1, blocks + half if f else blocks))


def finish_kernel(
    tg_ref,
    acc_gate,
    acc_up,
    acc_down,
    late_cols,
    late_og,
    late_h,
    late_gg,
    late_ug,
    tg_out,
    gg_out,
    gu_out,
    gd_out,
    gg_ref,
    gu_ref,
    gd_ref,
    sem,
):
    bf16, f32 = jnp.bfloat16, jnp.float32
    copies = [pltpu.make_async_copy(tg_ref, tg_out, sem.at[0])]
    copies[0].start()
    hidden_size = acc_gate.shape[1]

    def write(src, dst):
        copies.append(pltpu.make_async_copy(src, dst, sem.at[len(copies)]))
        copies[-1].start()

    for j in range(hidden_size // LANES):
        rows = pl.ds(j * LANES, LANES)
        term = lax.dot_general(late_h[:, rows], late_og[...], TN, preferred_element_type=f32)
        gd_ref[rows, :] = (acc_down[rows, :] + term).astype(bf16)
        write(gd_ref.at[rows], gd_out.at[0, rows])
    term = lax.dot_general(late_cols[...], late_gg[...], TN, preferred_element_type=f32)
    gg_ref[...] = (acc_gate[...] + term).astype(bf16)
    write(gg_ref, gg_out.at[0])
    term = lax.dot_general(late_cols[...], late_ug[...], TN, preferred_element_type=f32)
    gu_ref[...] = (acc_up[...] + term).astype(bf16)
    write(gu_ref, gu_out.at[0])
    for copy in copies:
        copy.wait()


def dense_shards(tokens, cotangent, routes, combine, hot_experts, extra_slots, w_gate, w_up, w_down):
    experts = lax.axis_size("expert")
    replicas = lax.axis_size("dp")
    token_count, features = tokens.shape
    hidden_size = w_gate.shape[2]
    blocks = features // LANES
    half = blocks // 2
    levels = experts // 2
    slots = replicas * experts
    share = features // replicas
    group_rows = experts * TILE + levels * 8
    early_rows, late_rows = 2 * group_rows, group_rows
    bf16, f32 = jnp.bfloat16, jnp.float32
    vmem = pl.BlockSpec(memory_space=pltpu.VMEM)
    hbm = pl.BlockSpec(memory_space=pltpu.HBM)
    dma = pltpu.SemaphoreType.DMA
    operands = [
        pltpu.with_memory_space_constraint(a, pltpu.HBM)
        for a in (
            tokens,
            cotangent,
            routes.T,
            combine.T,
            hot_experts,
            extra_slots,
            w_gate,
            w_up,
            w_down,
        )
    ]
    parts = pl.pallas_call(
        functools.partial(dense_kernel, experts),
        out_shape=(
            jax.ShapeDtypeStruct((token_count, features), bf16),
            jax.ShapeDtypeStruct((share, hidden_size), f32),
            jax.ShapeDtypeStruct((share, hidden_size), f32),
            jax.ShapeDtypeStruct((hidden_size, features), f32),
            jax.ShapeDtypeStruct((late_rows, share), bf16),
            jax.ShapeDtypeStruct((late_rows, features), bf16),
            jax.ShapeDtypeStruct((late_rows, hidden_size), bf16),
            jax.ShapeDtypeStruct((late_rows, hidden_size), bf16),
            jax.ShapeDtypeStruct((late_rows, hidden_size), bf16),
        ),
        in_specs=[hbm] * 9,
        out_specs=(vmem,) * 9,
        scratch_shapes=[
            pltpu.VMEM((TILE, features), bf16),
            pltpu.VMEM(cotangent.shape, bf16),
            pltpu.VMEM(routes.shape[::-1], jnp.int32),
            pltpu.VMEM(routes.shape[::-1], bf16),
            pltpu.SMEM(hot_experts.shape, jnp.int32),
            pltpu.SMEM(hot_experts.shape, jnp.int32),
            pltpu.VMEM((slots, TILE, features), bf16),
            pltpu.VMEM((slots, blocks + 1 + half, TILE, LANES), bf16),
            pltpu.VMEM((features, hidden_size), bf16),
            pltpu.VMEM((features, hidden_size), bf16),
            pltpu.VMEM((hidden_size, features), bf16),
            pltpu.VMEM((early_rows, features), bf16),
            pltpu.VMEM((early_rows, features), bf16),
            pltpu.VMEM((early_rows, hidden_size), bf16),
            pltpu.VMEM((early_rows, hidden_size), bf16),
            pltpu.VMEM((early_rows, hidden_size), bf16),
            pltpu.VMEM((late_rows, features), bf16),
            pltpu.VMEM((late_rows, features), bf16),
            pltpu.VMEM((late_rows, features), bf16),
            pltpu.VMEM((late_rows, hidden_size), bf16),
            pltpu.VMEM((late_rows, hidden_size), bf16),
            pltpu.VMEM((late_rows, hidden_size), bf16),
            pltpu.VMEM((2, levels, blocks + half, TILE, LANES), bf16),
            pltpu.VMEM((levels, blocks + half, TILE, LANES), bf16),
            pltpu.VMEM((levels, blocks + half, TILE, LANES), bf16),
            pltpu.VMEM((levels, blocks + half, TILE, LANES), bf16),
            dma((7,)),
            dma((3,)),
            dma((3,)),
            dma((2, slots // 2)),
            dma((4,)),
            dma((2,)),
            dma((1,)),
            pltpu.SemaphoreType.REGULAR((6,)),
        ],
        compiler_params=pltpu.CompilerParams(
            collective_id=0, has_side_effects=True, vmem_limit_bytes=32 * 1024 * 1024
        ),
    )(*operands)
    return pl.pallas_call(
        finish_kernel,
        out_shape=(
            jax.ShapeDtypeStruct((token_count, features), bf16),
            jax.ShapeDtypeStruct((1, share, hidden_size), bf16),
            jax.ShapeDtypeStruct((1, share, hidden_size), bf16),
            jax.ShapeDtypeStruct((1, hidden_size, features), bf16),
        ),
        in_specs=[vmem] * len(parts),
        out_specs=(hbm,) * 4,
        scratch_shapes=[
            pltpu.VMEM((share, hidden_size), bf16),
            pltpu.VMEM((share, hidden_size), bf16),
            pltpu.VMEM((hidden_size, features), bf16),
            dma((3 + hidden_size // LANES,)),
        ],
        compiler_params=pltpu.CompilerParams(vmem_limit_bytes=16 * 1024 * 1024),
    )(*parts)


def solution(mesh):
    in_specs = (
        P(("dp", "expert"), None),
        P(("dp", "expert"), None),
        P(("dp", "expert"), None),
        P(("dp", "expert"), None),
        P(),
        P(),
        P("expert", None, None),
        P("expert", None, None),
        P("expert", None, None),
    )
    out_specs = (
        P(("dp", "expert"), None),
        P("expert", "dp", None),
        P("expert", "dp", None),
        P("expert", None, None),
    )

    def body(*args):
        token_count, features = args[0].shape
        if dense_fits(dict(mesh.shape), token_count, features, args[2].shape[1], args[6].shape[2]):
            return dense_shards(*args)
        return shards(*args)

    return jax.shard_map(body, mesh=mesh, in_specs=in_specs, out_specs=out_specs, check_vma=False)
```

```python
import functools

import jax
import jax.numpy as jnp
from jax import lax
from jax.experimental import pallas as pl
from jax.experimental.pallas import tpu as pltpu
from jax.sharding import PartitionSpec as P


def forward_rows(weight_gate, weight_up, weight_down, row_tokens, row_cotan, row_weights):
    gate_pre = jnp.dot(row_tokens, weight_gate, preferred_element_type=jnp.float32)
    up_proj = jnp.dot(row_tokens, weight_up, preferred_element_type=jnp.float32)
    sigmoid_gate = jax.nn.sigmoid(gate_pre)
    gate_act = gate_pre * sigmoid_gate
    hidden = (gate_act * up_proj).astype(jnp.bfloat16)
    out_grad = (row_weights.astype(jnp.float32)[:, None] * row_cotan.astype(jnp.float32)).astype(
        jnp.bfloat16
    )
    hidden_grad = jnp.dot(out_grad, weight_down.T, preferred_element_type=jnp.float32)
    gate_grad = (
        hidden_grad * up_proj * sigmoid_gate * (1.0 + gate_pre * (1.0 - sigmoid_gate))
    ).astype(jnp.bfloat16)
    up_grad = (hidden_grad * gate_act).astype(jnp.bfloat16)
    row_grads = jnp.dot(gate_grad, weight_gate.T, preferred_element_type=jnp.float32)
    row_grads = row_grads + jnp.dot(up_grad, weight_up.T, preferred_element_type=jnp.float32)
    return (row_grads.astype(jnp.bfloat16), (row_tokens, gate_grad, up_grad, hidden, out_grad))


def weight_terms(pieces):
    row_tokens, gate_grad, up_grad, hidden, out_grad = pieces
    grad_gate = jnp.dot(row_tokens.T, gate_grad, preferred_element_type=jnp.float32)
    grad_up = jnp.dot(row_tokens.T, up_grad, preferred_element_type=jnp.float32)
    grad_down = jnp.dot(hidden.T, out_grad, preferred_element_type=jnp.float32)
    return (grad_gate, grad_up, grad_down)


def expert_pass(weight_gate, weight_up, weight_down, row_tokens, row_cotan, row_weights):
    row_grads, pieces = forward_rows(
        weight_gate, weight_up, weight_down, row_tokens, row_cotan, row_weights
    )
    return (row_grads, weight_terms(pieces))


def shards(tokens, cotangent, routes, combine, hot_experts, extra_slots, w_gate, w_up, w_down):
    expert_count = lax.axis_size("expert")
    token_count, features = tokens.shape
    route_count = routes.shape[1]
    capacity = max(2, min(token_count * route_count * 7 // (8 * expert_count), token_count // 2))
    spare_slots = 2 * max(1, capacity // 6)
    expert_ids = routes.reshape(-1)
    assign_count = expert_ids.shape[0]
    assign_order = jnp.arange(assign_count, dtype=jnp.int32)
    earlier = (expert_ids[:, None] == expert_ids[None, :]) & (
        assign_order[None, :] < assign_order[:, None]
    )
    slot_rank = jnp.sum(earlier.astype(jnp.int32), axis=1)
    hot_match = expert_ids[:, None] == hot_experts[None, :]
    slot_limit = capacity + jnp.sum(jnp.where(hot_match, extra_slots[None, :], 0), axis=1)
    is_kept = slot_rank < slot_limit
    slot_count = capacity + spare_slots
    total_slots = expert_count * slot_count
    flat_slot = jnp.where(is_kept, expert_ids * slot_count + slot_rank, total_slots)
    slot_ids = jnp.arange(total_slots, dtype=jnp.int32)
    assign_onehot = slot_ids[:, None] == flat_slot[None, :]
    token_onehot = jnp.any(
        assign_onehot.reshape(total_slots, token_count, route_count), axis=2
    ).astype(jnp.bfloat16)
    both_rows = jnp.concatenate([tokens, cotangent], axis=1)
    filled = jnp.dot(token_onehot, both_rows, preferred_element_type=jnp.float32).astype(
        jnp.bfloat16
    )
    token_send = filled[:, :features].reshape(expert_count, slot_count, features)
    cotan_send = filled[:, features:].reshape(expert_count, slot_count, features)
    weight_flat = jnp.sum(
        jnp.where(assign_onehot, combine.reshape(-1).astype(jnp.float32)[None, :], 0.0), axis=1
    )
    weight_send = weight_flat.astype(jnp.bfloat16).reshape(expert_count, slot_count)
    token_recv, cotan_recv, weight_recv = (
        lax.all_to_all(token_send, "expert", split_axis=0, concat_axis=0, tiled=True),
        lax.all_to_all(cotan_send, "expert", split_axis=0, concat_axis=0, tiled=True),
        lax.all_to_all(weight_send, "expert", split_axis=0, concat_axis=0, tiled=True),
    )
    own_weights = (w_gate[0], w_up[0], w_down[0])
    all_rows, grad_terms = expert_pass(
        own_weights[0],
        own_weights[1],
        own_weights[2],
        token_recv.reshape(-1, features),
        cotan_recv.reshape(-1, features),
        weight_recv.reshape(-1),
    )
    grad_rows = all_rows.reshape(expert_count, slot_count, features)
    returned_rows = lax.all_to_all(grad_rows, "expert", split_axis=0, concat_axis=0, tiled=True)
    token_grads = jnp.dot(
        token_onehot.T,
        returned_rows.reshape(total_slots, features),
        preferred_element_type=jnp.float32,
    ).astype(jnp.bfloat16)
    grad_gate, grad_up = (
        lax.psum_scatter(grad_terms[0][None], "dp", scatter_dimension=1, tiled=True),
        lax.psum_scatter(grad_terms[1][None], "dp", scatter_dimension=1, tiled=True),
    )
    grad_down = lax.psum(grad_terms[2][None], "dp")
    return (
        token_grads,
        grad_gate.astype(jnp.bfloat16),
        grad_up.astype(jnp.bfloat16),
        grad_down.astype(jnp.bfloat16),
    )


MESH = pl.DeviceIdType.MESH
LANES = 128
TILE = 16
NT = (((1,), (1,)), ((), ()))
TN = (((0,), (0,)), ((), ()))


def slots_of(token_count, route_count, expert_count):
    capacity = max(2, min(token_count * route_count * 7 // (8 * expert_count), token_count // 2))
    return capacity, 2 * max(1, capacity // 6)


def dense_fits(sizes, token_count, features, route_count, hidden_size):
    capacity, spare = slots_of(token_count, route_count, sizes["expert"])
    return (
        route_count == sizes["expert"]
        and sizes["dp"] == 4
        and sizes["expert"] == 8
        and token_count == 2 * TILE
        and capacity == TILE
        and spare * 2 == 8
        and features % (8 * LANES) == 0
        and hidden_size % LANES == 0
    )


def dense_kernel(
    experts,
    tok_hbm,
    cot_hbm,
    routes_hbm,
    comb_hbm,
    hot_hbm,
    extra_hbm,
    wg_hbm,
    wu_hbm,
    wd_hbm,
    tg_ref,
    acc_gate,
    acc_up,
    acc_down,
    late_cols,
    late_og,
    late_h,
    late_gg,
    late_ug,
    tok_ref,
    cot_ref,
    routes_ref,
    comb_ref,
    hot_ref,
    extra_ref,
    all_tok,
    slab,
    wg,
    wu,
    wd,
    all_t,
    all_og,
    all_h,
    all_gg,
    all_ug,
    late_t,
    mid_t,
    mid_og,
    mid_h,
    mid_gg,
    mid_ug,
    row_out,
    pair_in,
    row_sum,
    z_in,
    in_sem,
    w_sem,
    send_sem,
    recv_sem,
    pair_recv,
    row_sem,
    z_recv,
    ready,
):
    levels = experts // 2
    hot_levels = levels // 2
    features = all_tok.shape[2]
    blocks = features // LANES
    half = blocks // 2
    weight_at, spill_at = blocks, blocks + 1
    bf16, f32 = jnp.bfloat16, jnp.float32

    d = lax.axis_index("dp")
    e = lax.axis_index("expert")
    z, c = e // 2, e % 2
    dx = d + 1 - 2 * (d % 2)
    dy = (d + 2) % 4
    dd = 3 - d
    pc = 1 - c
    upper_half = z // 2
    near, far = 2 * upper_half, 2 - 2 * upper_half
    hot = z < hot_levels
    low_x, low_y, low_z = d % 2 == 1, d // 2 == 1, z > 0
    up_x, up_y, up_z = d % 2 == 0, d // 2 == 0, z < levels - 1
    first_z, last_z = z == 0, z == levels - 1
    at_below, at_above = (d, jnp.maximum(e - 2, 0)), (d, jnp.minimum(e + 2, experts - 1))
    at_top, at_bottom = (d, (levels - 1) * 2 + c), (d, c)
    at_x, at_y, at_pair = (dx, e), (dy, e), (d, z * 2 + pc)
    at_diag = (dd, e)
    upper = z >= hot_levels
    low_d, up_d = jnp.logical_and(upper, d > dd), jnp.logical_and(upper, d < dd)

    def slot(dp, level, core):
        return (dp * 2 + core) * levels + level

    me = slot(d, z, c)
    input_copies = [
        pltpu.make_async_copy(h, v, in_sem.at[i])
        for i, (h, v) in enumerate(
            (
                (tok_hbm.at[pl.ds(TILE, TILE)], tok_ref),
                (cot_hbm, cot_ref),
                (routes_hbm, routes_ref),
                (comb_hbm, comb_ref),
                (hot_hbm, hot_ref),
                (extra_hbm, extra_ref),
                (tok_hbm.at[pl.ds(0, TILE)], all_tok.at[me]),
            )
        )
    ]
    own_tokens = input_copies.pop()
    weight_copies = [
        pltpu.make_async_copy(h.at[0], v, w_sem.at[i])
        for i, (h, v) in enumerate(((wg_hbm, wg), (wu_hbm, wu), (wd_hbm, wd)))
    ]

    barrier = pltpu.get_barrier_semaphore()

    def greet(peer):
        pl.semaphore_signal(barrier, inc=1, device_id=peer, device_id_type=MESH)

    pl.when(c == 0)(lambda: greet(at_pair))
    pl.when(up_x)(lambda: greet(at_x))
    pl.when(up_y)(lambda: greet(at_y))
    pl.when(up_z)(lambda: greet(at_above))
    pl.when(first_z)(lambda: greet(at_top))
    pl.when(up_d)(lambda: greet(at_diag))
    for copy in input_copies + [own_tokens] + weight_copies:
        copy.start()

    def piece(s, p, full):
        if p == 0:
            return all_tok.at[s]
        return slab.at[s] if full else slab.at[s, pl.ds(0, spill_at)]

    def either(full, visit):
        if full is True or full is False:
            visit(full)
            return
        pl.when(full)(lambda: visit(True))
        pl.when(jnp.logical_not(full))(lambda: visit(False))

    def remote(src, dst, send, recv, peer):
        return pltpu.make_async_remote_copy(
            src_ref=src,
            dst_ref=dst,
            send_sem=send,
            recv_sem=recv,
            device_id=peer,
            device_id_type=MESH,
        )

    def kind(p, f):
        return send_sem.at[0 if p == 0 else 1 if f else 2]

    def push(dp, level, p, full, peer, own=False):
        s = slot(dp, level, c)

        def go(f):
            dst = piece(s, p, f)
            src = tok_hbm.at[pl.ds(0, TILE)] if own and p == 0 else dst
            remote(src, dst, kind(p, f), recv_sem.at[p, dp * levels + level], peer).start()

        either(True if p == 0 else full, go)

    def to_x(dp, level, p, own=False):
        push(dp, level, p, True if own else hot, at_x, own)

    def to_y(dp, level, p, own=False):
        push(dp, level, p, True if own else hot, at_y, own)

    def to_below(p):
        push(d, z, p, True, at_below, True)

    def to_above(p):
        push(d, z, p, z + 1 < hot_levels, at_above, True)

    def to_top(p):
        push(d, z, p, False, at_top, True)

    def to_bottom(p):
        push(d, z, p, True, at_bottom, True)

    def pass_down(level, p):
        push(d, level, p, True, at_below)

    def pass_up(level, p):
        push(d, level, p, False, at_above)

    def to_diag(p):
        push(d, z, p, True, at_diag, True)

    def pass_across(p, peer):
        push(dd, z, p, True, peer)

    def to_pair(dp, level, p, bank, own=False):
        s = slot(dp, level, c)

        def go(f):
            dst = piece(s, p, f)
            src = tok_hbm.at[pl.ds(0, TILE)] if own and p == 0 else dst
            remote(src, dst, kind(p, f), pair_recv.at[bank], at_pair).start()

        either(True if p == 0 else hot, go)

    def to_other(dp, level, p, peer):
        part = piece(slot(dp, level, c), p, True)
        remote(part, part, kind(p, True), pair_recv.at[DD], peer).start()

    def arrived(dp, level, p, full):
        s = slot(dp, level, c)

        def go(f):
            dst = piece(s, p, f)
            at = recv_sem.at[p, dp * levels + level]
            remote(dst, dst, send_sem.at[0], at, at_x).wait_recv()

        either(True if p == 0 else full, go)

    lower_peers = (
        c + d % 2 + d // 2 + jnp.minimum(z, 1) + z // (levels - 1) + upper_half * (d // 2)
    )
    pl.when(lower_peers > 0)(lambda: pl.semaphore_wait(barrier, lower_peers))

    def tell(way, peer):
        pl.semaphore_signal(ready.at[way], inc=1, device_id=peer, device_id_type=MESH)

    pl.when(c == 1)(lambda: tell(5, at_pair))
    pl.when(low_x)(lambda: tell(0, at_x))
    pl.when(low_y)(lambda: tell(1, at_y))
    pl.when(low_z)(lambda: tell(3, at_below))
    pl.when(last_z)(lambda: tell(4, at_bottom))
    pl.when(low_d)(lambda: tell(2, at_diag))

    OWN, NEAR, FAR, DD = range(4)

    def to_lower(p):
        pl.when(low_z)(lambda: to_below(p))
        if p == 1:

            @pl.when(last_z)
            def _():
                to_bottom(0)
                to_bottom(1)

        pl.when(low_x)(lambda: to_x(d, z, p, True))
        pl.when(low_y)(lambda: to_y(d, z, p, True))
        pl.when(low_d)(lambda: to_diag(p))

    to_lower(0)

    for copy in input_copies:
        copy.wait()
    names = -(-experts // TILE) * TILE
    expert_row = lax.broadcasted_iota(jnp.int32, (names, 2 * TILE), 0)
    token_lane = lax.broadcasted_iota(jnp.int32, (names, 2 * TILE), 1)
    routes = routes_ref[...]
    comb = comb_ref[...].astype(f32)
    weights = jnp.zeros((names, 2 * TILE), f32)
    for r in range(routes.shape[0]):
        weights = jnp.where(expert_row == routes[r : r + 1, :], comb[r : r + 1, :], weights)
    limit = jnp.full((names, 2 * TILE), TILE, jnp.int32)
    for j in range(hot_ref.shape[0]):
        limit = limit + jnp.where(expert_row == hot_ref[j], extra_ref[j], 0)
    weights = jnp.where(token_lane < limit, weights, 0.0).astype(bf16)
    unit_row = lax.broadcasted_iota(jnp.int32, (names, LANES), 0)
    unit_lane = lax.broadcasted_iota(jnp.int32, (names, LANES), 1)

    def turned(shift):
        unit = jnp.where(unit_lane == unit_row + shift, 1.0, 0.0).astype(bf16)
        return lax.dot_general(weights, unit, TN, preferred_element_type=f32)

    main_part, tail_part = turned(0), turned(LANES // 2)
    slab[me, weight_at] = (main_part[:TILE] + tail_part[TILE:]).astype(bf16)
    tok_tail = tok_ref[...].astype(f32)[:8]
    cot_tail = cot_ref[TILE:, :].astype(f32)[:8]
    tail_row = lax.broadcasted_iota(jnp.int32, (8, features), 0)
    spill = jnp.where(tail_row < 4, tok_tail, pltpu.roll(cot_tail, 4, 0))
    for j in range(blocks):
        slab[me, j] = cot_ref[:TILE, j * LANES : (j + 1) * LANES]
    for j in range(half):
        lo = spill[:, j * LANES : (j + 1) * LANES]
        hi = spill[:, (half + j) * LANES : (half + j + 1) * LANES]
        slab[me, spill_at + j] = jnp.concatenate([lo, hi], axis=0).astype(bf16)

    to_lower(1)
    pl.when(c == 0)(lambda: pl.semaphore_wait(ready.at[5], 1))
    for p in range(2):
        to_pair(d, z, p, OWN, True)

    def to_upper(way, up, act):
        @pl.when(up)
        def _():
            pl.semaphore_wait(ready.at[way], 1)
            for p in range(2):
                act(p)

    to_upper(3, up_z, to_above)
    to_upper(0, up_x, lambda p: to_x(d, z, p, True))
    to_upper(1, up_y, lambda p: to_y(d, z, p, True))
    to_upper(2, up_d, to_diag)
    own_tokens.wait()

    def at_distance(dist, visit):
        if dist == 0:
            visit(z, 0)
            return
        pl.when(z - dist >= 0)(lambda: visit(z - dist, -1))
        pl.when(z + dist < levels)(lambda: visit(z + dist, 1))

    def bank_of(level):
        return (level // 2 + upper_half) % 2

    def column(dist, p):
        def visit(level, side):
            arrived(d, level, p, True if side > 0 else hot)
            if dist == 1 and side > 0:
                pl.when(low_z)(lambda: pass_down(level, p))
            elif dist == 1:
                pl.when(up_z)(lambda: pass_up(level, p))
            to_x(d, level, p)
            to_y(d, level, p)
            to_pair(d, level, p, OWN)

        at_distance(dist, visit)

    def beside(dist, p):
        full = True if dist == 0 else hot
        keep = (hot, True, low_z, low_z)[dist]

        def visit(level, side, keep=keep):
            bank = NEAR + bank_of(level)
            if dist == 1 and side < 0:
                keep = z != 1
            arrived(dx, level, p, full)
            turn = jnp.logical_and((p + c) % 2 == 0, keep)
            pl.when(turn)(lambda: to_y(dx, level, p))
            if dist in (1, 2) and side > 0:
                both = jnp.logical_and(turn, z == dist - 1)
                pl.when(both)(lambda: to_other(dx, level, p, (dy, z * 2 + pc)))
            to_pair(dx, level, p, bank)
            arrived(dy, level, p, full)
            turn = jnp.logical_and((p + c) % 2 == 1, keep)
            pl.when(turn)(lambda: to_x(dy, level, p))
            if dist in (1, 2) and side > 0:
                both = jnp.logical_and(turn, z == dist - 1)
                pl.when(both)(lambda: to_other(dy, level, p, (dx, z * 2 + pc)))
            to_pair(dy, level, p, bank)

        at_distance(dist, visit)

    def across(dist, p):
        full = True if dist == 0 else hot

        def visit(level, side):
            arrived(dd, level, p, full)
            if dist == 0:
                pl.when(last_z)(lambda: pass_across(p, at_bottom))
                pl.when(z == 2)(lambda: pass_across(p, at_bottom))
                pl.when(first_z)(lambda: pass_across(p, at_above))
            if dist in (1, 2) and side > 0:
                pl.when(z != dist - 1)(lambda: to_pair(dd, level, p, DD))
            else:
                to_pair(dd, level, p, DD)

        at_distance(dist, visit)

    def from_pair(bank, at, count):
        def go(f):
            tiles = blocks + (slab.shape[1] if f else spill_at)
            part = slab.at[pl.ds(0, tiles), pl.ds(0, count)]
            remote(part, part, send_sem.at[0], pair_recv.at[bank], at_pair).wait_recv()

        either(hot, go)

    def group(parts, store):
        each = sum(n for _, _, n in parts)
        main_rows, spill_rows = 2 * each * TILE, each * 8

        def slots_of_core(core):
            return [pl.ds(slot(dp, level, core), n) for dp, level, n in parts]

        lanes_a, lanes_b = slots_of_core(0), slots_of_core(1)

        def rows_of(at, lanes):
            return [slab[r, at] for r in lanes]

        def low8(lanes, at, cut):
            return jnp.concatenate(
                [v.astype(f32)[:, cut : cut + 8].reshape(-1, LANES) for v in rows_of(at, lanes)],
                axis=0,
            )

        def tail_of(lanes):
            return jnp.concatenate(
                [low8(lanes, spill_at + j, 0) for j in range(half)]
                + [low8(lanes, spill_at + j, 8) for j in range(half)],
                axis=1,
            )

        tail_a, tail_b = tail_of(lanes_a), tail_of(lanes_b)
        first = lax.broadcasted_iota(jnp.int32, (spill_rows, features), 0) % 8 < 4
        first_w = lax.broadcasted_iota(jnp.int32, (spill_rows, LANES), 0) % 8 < 4
        tok_rows = jnp.where(first, tail_a, pltpu.roll(tail_b, 4, 0))
        cot_rows = jnp.where(first, pltpu.roll(tail_a, spill_rows - 4, 0), tail_b)
        tok_rows = jnp.where(hot, tok_rows, 0.0)
        cot_rows = jnp.where(hot, cot_rows, 0.0)

        def main_of(at):
            return jnp.concatenate(
                [v.reshape(-1, LANES) for v in rows_of(at, lanes_a + lanes_b)], axis=0
            )

        w_main = main_of(weight_at).astype(f32)
        w_tail = jnp.where(
            first_w, low8(lanes_a, weight_at, 0), pltpu.roll(low8(lanes_b, weight_at, 0), 4, 0)
        )
        main_lane = lax.broadcasted_iota(jnp.int32, (main_rows, LANES), 1)
        tail_lane = lax.broadcasted_iota(jnp.int32, (spill_rows, LANES), 1)
        w = jnp.concatenate(
            [
                jnp.sum(jnp.where(main_lane == e, w_main, 0.0), axis=1, keepdims=True),
                jnp.sum(jnp.where(tail_lane == e + LANES // 2, w_tail, 0.0), axis=1, keepdims=True),
            ],
            axis=0,
        )
        t_ref, og_ref, h_ref, gg_ref, ug_ref, at = store
        rows = pl.ds(at, main_rows + spill_rows)
        t_ref[rows, :] = jnp.concatenate(
            [all_tok[r].reshape(-1, features) for r in lanes_a + lanes_b]
            + [tok_rows.astype(bf16)],
            axis=0,
        )
        cot = jnp.concatenate(
            [
                jnp.concatenate([main_of(j) for j in range(blocks)], axis=1).astype(f32),
                cot_rows,
            ],
            axis=0,
        )
        og_ref[rows, :] = (w * cot).astype(bf16)
        t = t_ref[rows, :]
        gate_pre = jnp.dot(t, wg[...], preferred_element_type=f32)
        up_proj = jnp.dot(t, wu[...], preferred_element_type=f32)
        hidden_grad = lax.dot_general(og_ref[rows, :], wd[...], NT, preferred_element_type=f32)
        sig = jax.nn.sigmoid(gate_pre)
        act = gate_pre * sig
        h_ref[rows, :] = (act * up_proj).astype(bf16)
        gg_ref[rows, :] = (hidden_grad * up_proj * sig * (1.0 + gate_pre * (1.0 - sig))).astype(
            bf16
        )
        ug_ref[rows, :] = (hidden_grad * act).astype(bf16)

    main_rows = experts * TILE
    group_rows = main_rows + levels * 8
    early = (all_t, all_og, all_h, all_gg, all_ug)
    mid = (mid_t, mid_og, mid_h, mid_gg, mid_ug)
    late = (late_t, late_og, late_h, late_gg, late_ug)

    for p in range(2):
        beside(0, p)
        column(1, p)
    to_upper(4, first_z, to_top)

    for p in range(2):
        for dist in (2, 3):
            column(dist, p)

    @pl.when(upper)
    def _():
        for p in range(2):
            across(0, p)

    from_pair(OWN, slot(d, 0, pc), levels)
    for copy in weight_copies:
        copy.wait()
    group([(d, 0, levels)], early + (0,))
    @pl.when(hot)
    def _():
        for p in range(2):
            across(0, p)

    own = pl.ds(0, group_rows)
    rg = lax.dot_general(all_gg[own, :], wg[...], NT, preferred_element_type=f32)
    rg = rg + lax.dot_general(all_ug[own, :], wu[...], NT, preferred_element_type=f32)
    lane_rows = main_rows // 2
    for j in range(blocks):
        cols = slice(j * LANES, (j + 1) * LANES)
        for core in range(2):
            row_out[core, :, j] = (
                rg[core * lane_rows : (core + 1) * lane_rows, cols]
                .reshape(levels, TILE, LANES)
                .astype(bf16)
            )
    for j in range(half):
        lo = rg[main_rows:, j * LANES : (j + 1) * LANES].reshape(levels, 8, LANES)
        hi = rg[main_rows:, (half + j) * LANES : (half + j + 1) * LANES].reshape(levels, 8, LANES)
        both = jnp.concatenate([lo, hi], axis=1).astype(bf16)
        for core in range(2):
            row_out[core, :, blocks + j] = both

    def row_copy(f):
        src, dst = row_out.at[pc], pair_in
        if not f:
            src, dst = row_out.at[pc, :, pl.ds(0, blocks)], pair_in.at[:, pl.ds(0, blocks)]
        return remote(src, dst, row_sem.at[0], row_sem.at[1], at_pair)

    either(hot, lambda f: row_copy(f).start())
    for p in range(2):
        beside(1, p)

    either(hot, lambda f: row_copy(f).wait_recv())
    for level in range(levels):
        row_sum[level, :blocks] = (
            row_out[c, level, :blocks].astype(f32) + pair_in[level, :blocks].astype(f32)
        ).astype(bf16)

    @pl.when(hot)
    def _():
        for level in range(levels):
            row_sum[level, blocks:] = (
                row_out[c, level, blocks:].astype(f32) + pair_in[level, blocks:].astype(f32)
            ).astype(bf16)

    def z_copy(level, sender, peer, f):
        src, dst = row_sum.at[level], z_in.at[sender]
        if not f:
            part = pl.ds(0, blocks)
            src, dst = row_sum.at[level, part], z_in.at[sender, part]
        return remote(src, dst, row_sem.at[0], z_recv.at[0], peer)

    for level in range(levels):

        @pl.when(z != level)
        def _():
            either(hot, lambda f: z_copy(level, z, (d, level * 2 + c), f).start())

    @pl.when(low_z)
    def _():
        for dist in (2, 3):
            for p in range(2):
                beside(dist, p)

    from_pair(NEAR, 0, levels)
    group([(dx, near, 2), (dy, near, 2)], early + (group_rows,))

    @pl.when(first_z)
    def _():
        for dist in (2, 3):
            for p in range(2):
                beside(dist, p)

    def across_when(cond, *dists):
        @pl.when(cond)
        def _():
            for dist in dists:
                for p in range(2):
                    across(dist, p)

    share = features // 4
    cols = pl.ds(pl.multiple_of(d * share, LANES), share)
    t_cols = all_t[:, cols]
    acc_gate[...] = lax.dot_general(t_cols, all_gg[...], TN, preferred_element_type=f32)
    acc_up[...] = lax.dot_general(t_cols, all_ug[...], TN, preferred_element_type=f32)
    acc_down[...] = lax.dot_general(all_h[...], all_og[...], TN, preferred_element_type=f32)
    across_when(first_z, 3, 2)
    across_when(low_z, 1)
    across_when(last_z, 2, 3)
    from_pair(FAR, 0, levels)
    group([(dx, far, 2), (dy, far, 2)], mid + (0,))
    m_cols = mid_t[:, cols]
    acc_gate[...] += lax.dot_general(m_cols, mid_gg[...], TN, preferred_element_type=f32)
    acc_up[...] += lax.dot_general(m_cols, mid_ug[...], TN, preferred_element_type=f32)
    acc_down[...] += lax.dot_general(mid_h[...], mid_og[...], TN, preferred_element_type=f32)
    across_when(first_z, 1)
    across_when(jnp.logical_and(low_z, up_z), 2)
    from_pair(DD, 0, levels)
    group([(dd, 0, levels)], late + (0,))
    late_cols[...] = late_t[:, cols]
    z_in[z] = row_sum[z]

    def returned(low, high):
        count = (low * (blocks + half) + high * blocks) // half
        part = slab.at[pl.ds(0, count), pl.ds(0, half)]
        remote(part, part, send_sem.at[0], z_recv.at[0], at_pair).wait_recv()

    pl.when(hot)(lambda: returned(hot_levels - 1, levels - hot_levels))
    pl.when(upper)(lambda: returned(hot_levels, levels - hot_levels - 1))

    total = z_in[0, :blocks].astype(f32)
    spilled = z_in[0, blocks:].astype(f32)
    for level in range(1, levels):
        total = total + z_in[level, :blocks].astype(f32)
        if level < hot_levels:
            spilled = spilled + z_in[level, blocks:].astype(f32)
    kept_row = lax.broadcasted_iota(jnp.int32, (8, LANES), 0) < 4
    blank = jnp.zeros((8, LANES), f32)
    for j in range(blocks):
        tg_ref[:TILE, j * LANES : (j + 1) * LANES] = total[j].astype(bf16)
    for j in range(half):
        for at, rows in ((j, spilled[j][:8]), (half + j, spilled[j][8:])):
            rows = jnp.where(c == 0, rows, pltpu.roll(rows, 4, 0))
            tg_ref[TILE:, at * LANES : (at + 1) * LANES] = jnp.concatenate(
                [jnp.where(kept_row, rows, 0.0), blank], axis=0
            ).astype(bf16)

    def sent(sem, slots, width):
        part = slab.at[pl.ds(0, slots), pl.ds(0, width)]
        remote(part, part, sem, recv_sem.at[0, 0], at_x).wait_send()

    wide = slab.shape[1]
    relays = 4 * levels
    sides = 2 * levels
    for level, tokens_out, full_out, cold_out in (
        (0, relays + sides + 5, relays + sides + 4, 1),
        (1, relays + sides + 7, relays + sides + 5, 2),
        (2, relays + sides + 9, 6, relays + sides + 3),
        (3, relays + sides + 7, 6, relays + sides + 1),
    ):

        @pl.when(z == level)
        def _():
            if tokens_out <= slab.shape[0]:
                sent(send_sem.at[0], tokens_out, blocks)
            else:
                sent(send_sem.at[0], blocks * 3, tokens_out // 3)
            sent(send_sem.at[1], full_out, wide)
            sent(send_sem.at[2], cold_out, spill_at)

    either(hot, lambda f: sent(row_sem.at[0], 2 * levels - 1, blocks + half if f else blocks))


def finish_kernel(
    tg_ref,
    acc_gate,
    acc_up,
    acc_down,
    late_cols,
    late_og,
    late_h,
    late_gg,
    late_ug,
    tg_out,
    gg_out,
    gu_out,
    gd_out,
    gg_ref,
    gu_ref,
    gd_ref,
    sem,
):
    bf16, f32 = jnp.bfloat16, jnp.float32
    copies = [pltpu.make_async_copy(tg_ref, tg_out, sem.at[0])]
    copies[0].start()
    hidden_size = acc_gate.shape[1]

    def write(src, dst):
        copies.append(pltpu.make_async_copy(src, dst, sem.at[len(copies)]))
        copies[-1].start()

    for j in range(hidden_size // LANES):
        rows = pl.ds(j * LANES, LANES)
        term = lax.dot_general(late_h[:, rows], late_og[...], TN, preferred_element_type=f32)
        gd_ref[rows, :] = (acc_down[rows, :] + term).astype(bf16)
        write(gd_ref.at[rows], gd_out.at[0, rows])
    term = lax.dot_general(late_cols[...], late_gg[...], TN, preferred_element_type=f32)
    gg_ref[...] = (acc_gate[...] + term).astype(bf16)
    write(gg_ref, gg_out.at[0])
    term = lax.dot_general(late_cols[...], late_ug[...], TN, preferred_element_type=f32)
    gu_ref[...] = (acc_up[...] + term).astype(bf16)
    write(gu_ref, gu_out.at[0])
    for copy in copies:
        copy.wait()


def dense_shards(tokens, cotangent, routes, combine, hot_experts, extra_slots, w_gate, w_up, w_down):
    experts = lax.axis_size("expert")
    replicas = lax.axis_size("dp")
    token_count, features = tokens.shape
    hidden_size = w_gate.shape[2]
    blocks = features // LANES
    half = blocks // 2
    levels = experts // 2
    slots = replicas * experts
    share = features // replicas
    group_rows = experts * TILE + levels * 8
    early_rows, late_rows = 2 * group_rows, group_rows
    bf16, f32 = jnp.bfloat16, jnp.float32
    vmem = pl.BlockSpec(memory_space=pltpu.VMEM)
    hbm = pl.BlockSpec(memory_space=pltpu.HBM)
    dma = pltpu.SemaphoreType.DMA
    operands = [
        pltpu.with_memory_space_constraint(a, pltpu.HBM)
        for a in (
            tokens,
            cotangent,
            routes.T,
            combine.T,
            hot_experts,
            extra_slots,
            w_gate,
            w_up,
            w_down,
        )
    ]
    parts = pl.pallas_call(
        functools.partial(dense_kernel, experts),
        out_shape=(
            jax.ShapeDtypeStruct((token_count, features), bf16),
            jax.ShapeDtypeStruct((share, hidden_size), f32),
            jax.ShapeDtypeStruct((share, hidden_size), f32),
            jax.ShapeDtypeStruct((hidden_size, features), f32),
            jax.ShapeDtypeStruct((late_rows, share), bf16),
            jax.ShapeDtypeStruct((late_rows, features), bf16),
            jax.ShapeDtypeStruct((late_rows, hidden_size), bf16),
            jax.ShapeDtypeStruct((late_rows, hidden_size), bf16),
            jax.ShapeDtypeStruct((late_rows, hidden_size), bf16),
        ),
        in_specs=[hbm] * 9,
        out_specs=(vmem,) * 9,
        scratch_shapes=[
            pltpu.VMEM((TILE, features), bf16),
            pltpu.VMEM(cotangent.shape, bf16),
            pltpu.VMEM(routes.shape[::-1], jnp.int32),
            pltpu.VMEM(routes.shape[::-1], bf16),
            pltpu.SMEM(hot_experts.shape, jnp.int32),
            pltpu.SMEM(hot_experts.shape, jnp.int32),
            pltpu.VMEM((slots, TILE, features), bf16),
            pltpu.VMEM((slots, blocks + 1 + half, TILE, LANES), bf16),
            pltpu.VMEM((features, hidden_size), bf16),
            pltpu.VMEM((features, hidden_size), bf16),
            pltpu.VMEM((hidden_size, features), bf16),
            pltpu.VMEM((early_rows, features), bf16),
            pltpu.VMEM((early_rows, features), bf16),
            pltpu.VMEM((early_rows, hidden_size), bf16),
            pltpu.VMEM((early_rows, hidden_size), bf16),
            pltpu.VMEM((early_rows, hidden_size), bf16),
            pltpu.VMEM((late_rows, features), bf16),
            pltpu.VMEM((late_rows, features), bf16),
            pltpu.VMEM((late_rows, features), bf16),
            pltpu.VMEM((late_rows, hidden_size), bf16),
            pltpu.VMEM((late_rows, hidden_size), bf16),
            pltpu.VMEM((late_rows, hidden_size), bf16),
            pltpu.VMEM((2, levels, blocks + half, TILE, LANES), bf16),
            pltpu.VMEM((levels, blocks + half, TILE, LANES), bf16),
            pltpu.VMEM((levels, blocks + half, TILE, LANES), bf16),
            pltpu.VMEM((levels, blocks + half, TILE, LANES), bf16),
            dma((7,)),
            dma((3,)),
            dma((3,)),
            dma((2, slots // 2)),
            dma((4,)),
            dma((2,)),
            dma((1,)),
            pltpu.SemaphoreType.REGULAR((6,)),
        ],
        compiler_params=pltpu.CompilerParams(
            collective_id=0, has_side_effects=True, vmem_limit_bytes=32 * 1024 * 1024
        ),
    )(*operands)
    return pl.pallas_call(
        finish_kernel,
        out_shape=(
            jax.ShapeDtypeStruct((token_count, features), bf16),
            jax.ShapeDtypeStruct((1, share, hidden_size), bf16),
            jax.ShapeDtypeStruct((1, share, hidden_size), bf16),
            jax.ShapeDtypeStruct((1, hidden_size, features), bf16),
        ),
        in_specs=[vmem] * len(parts),
        out_specs=(hbm,) * 4,
        scratch_shapes=[
            pltpu.VMEM((share, hidden_size), bf16),
            pltpu.VMEM((share, hidden_size), bf16),
            pltpu.VMEM((hidden_size, features), bf16),
            dma((3 + hidden_size // LANES,)),
        ],
        compiler_params=pltpu.CompilerParams(vmem_limit_bytes=16 * 1024 * 1024),
    )(*parts)


def solution(mesh):
    in_specs = (
        P(("dp", "expert"), None),
        P(("dp", "expert"), None),
        P(("dp", "expert"), None),
        P(("dp", "expert"), None),
        P(),
        P(),
        P("expert", None, None),
        P("expert", None, None),
        P("expert", None, None),
    )
    out_specs = (
        P(("dp", "expert"), None),
        P("expert", "dp", None),
        P("expert", "dp", None),
        P("expert", None, None),
    )

    def body(*args):
        token_count, features = args[0].shape
        if dense_fits(dict(mesh.shape), token_count, features, args[2].shape[1], args[6].shape[2]):
            return dense_shards(*args)
        return shards(*args)

    return jax.shard_map(body, mesh=mesh, in_specs=in_specs, out_specs=out_specs, check_vma=False)
```
